1024 devices in a mesh: gx: 128 (over x, y, core), gy: 8 (over z).
Axes of the slice: x: 8, y: 8, z: 8, core: 2. Of those that a mesh axis runs over, the one named last changes fastest.
Arguments:
- concentration: float32 [512, 512, 128], P('gx', 'gy'), may hold values from -4 to 4
- potential: float32 [512, 512, 128], P('gx', 'gy'), may hold values from -4 to 4
- mass_source: float32 [512, 512, 128], P('gx', 'gy'), may hold values from -7 to 7
- potential_source: float32 [512, 512, 128], P('gx', 'gy'), may hold values from -7 to 7
- pore_mask: int32 [512, 512, 128], P('gx', 'gy'), may hold values 0 or 1
- mobility_class: int32 [512, 512, 128], P('gx', 'gy'), may hold values from 0 to 7
- mobility_table: float32 [8], replicated, may hold values from 0.05 to 1
- owner_map: int32 [128, 512], P(None, 'gy'), may hold values from 0 to 127, as said below
Outputs:
- conc_out: float32 [512, 512, 128], P('gx', 'gy')
- pot_out: float32 [512, 512, 128], P('gx', 'gy')
The draws below stay inside these ranges and needn't reach their ends.
Inputs may be any that keep to these rules, and one draw needn't show every extreme that they name: `owner_map`: no owner is named by more than 2 entries of one device; in every draw, for each gy index, one owner is named by exactly 2 entries of every device of that gy index.
All inputs are finite; a program needn't handle non-finite values. No bound on the sum of `pore_mask` on one device may be relied on, other than what follows from the above.
Results may differ from the reference program's by a relative error of at most 0.000058.
Values sent between devices are 32-bit elements; how exact they have to be, the bound alone decides.
A program may use at most 32 MiB of HBM per device.

```python
import math
import jax
import jax.numpy as jnp

X_DEV = 4
NB = 64
Y_DEV = 64
P_SIZE = 128
CAP = 2
NCLASS = 8
PRE = 1
POST = 1
CSWEEP = 3
NX = 512
NY = 512
N_GX = 128
N_GY = 8


def source_field(key):
    keys = jax.random.split(key, 5)
    freq_x = jax.random.randint(keys[0], (), 1, 4).astype(jnp.float32)
    freq_y = jax.random.randint(keys[1], (), 1, 4).astype(jnp.float32)
    freq_p = jax.random.randint(keys[2], (), 1, 3).astype(jnp.float32)
    phase = jax.random.uniform(keys[3], (), jnp.float32, 0.0, 2.0 * math.pi)
    coord_x = jnp.arange(NX, dtype=jnp.float32) / NX
    coord_y = jnp.arange(NY, dtype=jnp.float32) / NY
    coord_p = jnp.arange(P_SIZE, dtype=jnp.float32) / P_SIZE
    wave = jnp.sin(2.0 * math.pi * (freq_x * coord_x[:, None, None] + freq_y * coord_y[None, :, None] + freq_p * coord_p[None, None, :]) + phase)
    rough = jnp.clip(jax.random.normal(keys[4], (NX, NY, P_SIZE), jnp.float32), -4.0, 4.0)
    smooth = 1.5 * wave
    return (rough + smooth).astype(jnp.float32)


def draw_mass_source(key, part):
    return source_field(jax.random.fold_in(key, 101))


def draw_potential_source(key, part):
    return source_field(jax.random.fold_in(key, 202))


def draw_owner_map(key, part):
    device_count = N_GX * N_GY
    slot_count = N_GX * CAP
    device_keys = jax.random.split(jax.random.fold_in(key, 11), device_count)
    reward_extra = jax.random.randint(jax.random.fold_in(key, 23), (N_GY, N_GX), 0, 3 * (1 << 20))
    forced = jax.random.randint(jax.random.fold_in(key, 37), (N_GY,), 0, N_GX)
    slot_holder = jnp.arange(slot_count, dtype=jnp.int32) // CAP
    slot_index = jnp.arange(slot_count, dtype=jnp.int32)

    def one_device(device_key, cluster_index):
        noise_key, order_key = jax.random.split(device_key)
        random_jitter = jax.random.randint(noise_key, (slot_count,), 0, 1 << 20)
        ranking_value = random_jitter + reward_extra[cluster_index][slot_holder]
        ranking_value = jnp.where(slot_holder == forced[cluster_index], 1 << 22, ranking_value)
        ranking_value = ranking_value * 256 + slot_index
        order = jnp.argsort(-ranking_value, stable=True)
        chosen = slot_holder[order[:NB]]
        shuffle = jax.random.permutation(order_key, NB)
        return chosen[shuffle]
    group_ids = (jnp.arange(device_count, dtype=jnp.int32) % N_GY).astype(jnp.int32)
    rows_all = jax.vmap(one_device)(device_keys, group_ids)
    return rows_all.reshape(N_GX, N_GY * NB).astype(jnp.int32)


def with_ends(array, rng, low, largest):
    longest = array.shape.index(max(array.shape))
    spots = []
    for shift in (0, 1):
        where = [jax.random.randint(jax.random.fold_in(rng, axis), (), 0, length) for axis, length in enumerate(array.shape)]
        where[longest] = (where[longest] + shift) % array.shape[longest]
        spots.append(tuple(where))
    return array.at[spots[0]].set(low).at[spots[1]].set(largest)


def steps_of(rng, extent, cuts, least, largest):
    level, own = 1.0, jax.random.fold_in(rng, 6)
    for axis_at, shards_of in cuts:
        draws = jnp.exp(jax.random.uniform(jax.random.fold_in(own, axis_at), (shards_of,), jnp.float32, least / len(cuts), largest / len(cuts)))
        level = level * jnp.repeat(draws, extent[axis_at] // shards_of).reshape([-1 if axis == axis_at else 1 for axis in range(len(extent))])
    return level


def gaussian(key, dims, scale, bound, shards=(), kind=jnp.bfloat16):
    loudness = steps_of(key, dims, shards, -0.22, 0.18) if shards else 1.0
    drawn = jax.random.normal(key, dims, jnp.float32) * scale * loudness
    return jnp.minimum(jnp.maximum(drawn, -bound), bound).astype(kind)


def setup_inputs(seed: int = 0) -> dict:
    arg_keys = jax.random.split(jax.random.key(seed), 9)
    return {
        "concentration": gaussian(arg_keys[0], (NX, NY, P_SIZE), 0.5, 4.0, ((0, 128), (1, 8)), jnp.float32),
        "potential": gaussian(arg_keys[1], (NX, NY, P_SIZE), 0.5, 4.0, ((0, 128), (1, 8)), jnp.float32),
        "mass_source": draw_mass_source(jax.random.fold_in(arg_keys[8], 71), 0),
        "potential_source": draw_potential_source(jax.random.fold_in(arg_keys[8], 71), 0),
        "pore_mask": with_ends((jax.random.randint(arg_keys[4], (NX, NY, P_SIZE), 0, 4) < 3).astype(jnp.int32), jax.random.fold_in(arg_keys[4], 1), 0, 1),
        "mobility_class": with_ends(jax.random.randint(arg_keys[5], (NX, NY, P_SIZE), 0, NCLASS), jax.random.fold_in(arg_keys[5], 1), 0, NCLASS - 1).astype(jnp.int32),
        "mobility_table": jnp.clip(jnp.exp(jax.random.uniform(arg_keys[6], (NCLASS,), jnp.float32, math.log(0.05), math.log(1.0))), 0.05, 1.0),
        "owner_map": draw_owner_map(jax.random.fold_in(arg_keys[8], 71), 0),
    }


time_step = 0.25
split_slope = 1.0
interface = 0.5
relax_fine = 0.6
relax_coarse = 0.6
coarse_flux = 0.0625
coarse_bend = 0.125
coarse_det = 1.0 + 2.0 * coarse_flux * (split_slope + 2.0 * coarse_bend)


def lookup_mobility(pore_mask, mobility_class, mobility_table):
    values = jnp.zeros(mobility_class.shape, jnp.float32)
    for class_marker in range(NCLASS):
        values = jnp.where(mobility_class == class_marker, mobility_table[class_marker], values)
    return pore_mask.astype(jnp.float32) * values


def neighbours(padded):
    center = padded[1:-1, 1:-1, :]
    along_planes = jnp.pad(center, ((0, 0), (0, 0), (1, 1)))
    return (padded[2:, 1:-1, :], padded[:-2, 1:-1, :], padded[1:-1, 2:, :], padded[1:-1, :-2, :], along_planes[:, :, 2:], along_planes[:, :, :-2])


def face_terms(padded_mobility):
    center = padded_mobility[1:-1, 1:-1, :]
    return tuple(0.5 * (center + other) for other in neighbours(padded_mobility))


def residuals(padded_conc, padded_pot, faces, mass_source, potential_source):
    conc_now = padded_conc[1:-1, 1:-1, :]
    pot_now = padded_pot[1:-1, 1:-1, :]
    flux = jnp.zeros_like(pot_now)
    for face, other in zip(faces, neighbours(padded_pot)):
        flux = flux + face * (other - pot_now)
    laplace = -6.0 * conc_now
    for other in neighbours(padded_conc):
        laplace = laplace + other
    excess_mass = mass_source - (conc_now - time_step * flux)
    excess_pot = potential_source - (pot_now - split_slope * conc_now + interface * laplace)
    return excess_mass, excess_pot


def relax_pair(conc_now, pot_now, excess_mass, excess_pot, diagonal):
    other_diagonal = -(split_slope + 6.0 * interface)
    determinant = 1.0 - diagonal * other_diagonal
    new_conc = conc_now + relax_fine * (excess_mass - diagonal * excess_pot) / determinant
    new_pot = pot_now + relax_fine * (excess_pot - other_diagonal * excess_mass) / determinant
    return new_conc, new_pot


def restrict(field):
    size_x, size_y, size_p = field.shape
    return field.reshape(size_x // 2, 2, size_y // 2, 2, size_p // 2, 2).sum(axis=(1, 3, 5)) / 8.0


def prolong(coarse):
    size_x, size_y, size_p = coarse.shape
    wide = jnp.broadcast_to(coarse[:, None, :, None, :, None], (size_x, 2, size_y, 2, size_p, 2))
    return wide.reshape(2 * size_x, 2 * size_y, 2 * size_p)


def neighbour_sum(values):
    padded = jnp.pad(values, [(0, 0)] * (values.ndim - 1) + [(1, 1)])
    return padded[..., 2:] + padded[..., :-2]


def coarse_solve(mean):
    half_planes = mean.shape[-1] // 2
    mass_mean = mean[..., :half_planes]
    pot_mean = mean[..., half_planes:]
    coarse_conc = jnp.zeros_like(mass_mean)
    coarse_pot = jnp.zeros_like(pot_mean)
    for pass_index in range(CSWEEP):
        mass_gap = mass_mean - (coarse_conc + coarse_flux * (2.0 * coarse_pot - neighbour_sum(coarse_pot)))
        pot_gap = pot_mean - (coarse_pot - split_slope * coarse_conc + coarse_bend * (neighbour_sum(coarse_conc) - 2.0 * coarse_conc))
        coarse_conc = coarse_conc + relax_coarse * (mass_gap - 2.0 * coarse_flux * pot_gap) / coarse_det
        coarse_pot = coarse_pot + relax_coarse * (pot_gap + (split_slope + 2.0 * coarse_bend) * mass_gap) / coarse_det
    return jnp.concatenate([coarse_conc, coarse_pot], axis=-1)


def reference(concentration, potential, mass_source, potential_source, pore_mask, mobility_class, mobility_table, owner_map):
    spread = ((1, 1), (1, 1), (0, 0))
    mobility = lookup_mobility(pore_mask, mobility_class, mobility_table)
    faces = face_terms(jnp.pad(mobility, spread))
    diagonal = jnp.zeros_like(mobility)
    for face in faces:
        diagonal = diagonal + face
    diagonal = time_step * diagonal

    def excess_of(conc_now, pot_now):
        return residuals(jnp.pad(conc_now, spread), jnp.pad(pot_now, spread), faces, mass_source, potential_source)

    conc_now, pot_now = concentration, potential
    for pass_index in range(PRE):
        excess_mass, excess_pot = excess_of(conc_now, pot_now)
        conc_now, pot_now = relax_pair(conc_now, pot_now, excess_mass, excess_pot, diagonal)
    excess_mass, excess_pot = excess_of(conc_now, pot_now)
    blocks = jnp.concatenate([restrict(excess_mass), restrict(excess_pot)], axis=-1)
    coarse_x, coarse_y, planes = blocks.shape
    half_x = X_DEV // 2
    half_y = Y_DEV // 2
    owner_grid = owner_map.reshape(N_GX, N_GY, half_x, half_y).transpose(0, 2, 1, 3).reshape(coarse_x, coarse_y)
    group = (jnp.arange(coarse_y) // half_y).astype(jnp.int32)
    segment = (group[None, :] * N_GX + owner_grid).reshape(-1).astype(jnp.int32)
    flat_blocks = blocks.reshape(coarse_x * coarse_y, planes)
    totals = jax.ops.segment_sum(flat_blocks, segment, num_segments=N_GY * N_GX)
    counts = jax.ops.segment_sum(jnp.ones((coarse_x * coarse_y,), jnp.float32), segment, num_segments=N_GY * N_GX)
    means = totals / jnp.maximum(counts, 1.0)[:, None]
    solved = coarse_solve(means)
    correction = solved[segment].reshape(coarse_x, coarse_y, planes)
    half_planes = planes // 2
    conc_now = conc_now + prolong(correction[..., :half_planes])
    pot_now = pot_now + prolong(correction[..., half_planes:])
    for pass_index in range(POST):
        excess_mass, excess_pot = excess_of(conc_now, pot_now)
        conc_now, pot_now = relax_pair(conc_now, pot_now, excess_mass, excess_pot, diagonal)
    return conc_now, pot_now
```

```python
import functools

import jax
import jax.numpy as jnp
from jax import lax
from jax.experimental import pallas as pl
from jax.experimental.pallas import tpu as pltpu
from jax.sharding import PartitionSpec as P

NCLASS = 8
CSWEEP = 3
XROWS = 4
YCELLS = 64
PLANES = 128
PAD = 8
XGROUP = 8

relax_fine = 0.6
relax_coarse = 0.6
coarse_flux = 0.0625
coarse_bend = 0.125
coarse_det = 1.15625

F32 = jnp.float32
B16 = jnp.bfloat16
MESH = pl.DeviceIdType.MESH


def iota(shape, dim):
    return lax.broadcasted_iota(jnp.int32, shape, dim)


def halves(values):
    high = values.astype(B16)
    return high, (values - high.astype(F32)).astype(B16)


def dot(a, b):
    return jnp.dot(a, b, preferred_element_type=F32)


def dot_t(a, b):
    return lax.dot_general(a, b, (((1,), (1,)), ((), ())), preferred_element_type=F32)


def kernel(
    n_gx, n_gy,
    conc_h, pot_h, mass_h, psrc_h, mask_h, class_h, table, owner_h,
    conc_o, pot_o,
    fld, src, mask_v, class_v, owner_v,
    w_x, w_y, w_z, w_d, w_a, new,
    r_hi, r_mid, place, pick, edge_pick, count_v,
    totals, rs_buf, part, ar_buf, sol, y_out, y_in, corr,
    load_sem, ex_send, ex_recv, n_send, n_recv, g_send, g_recv, y_send, y_recv,
):
    ring = n_gx // XGROUP
    gx = lax.axis_index("gx")
    gy = lax.axis_index("gy")
    r = gx % ring
    q = gx // ring
    left, right = (gx + n_gx - 1) % n_gx, (gx + 1) % n_gx
    below, above = (gy + n_gy - 1) % n_gy, (gy + 1) % n_gy
    first, last = PAD, PAD + YCELLS

    def load(source, target, index):
        copy = pltpu.make_async_copy(source, target, load_sem.at[index])
        copy.start()
        return copy

    inner = pl.ds(PAD, YCELLS)
    l_mask = load(mask_h, mask_v, 0)
    l_class = load(class_h, class_v, 1)
    l_conc = load(conc_h, fld.at[0, pl.ds(1, XROWS), inner, :], 2)
    l_pot = load(pot_h, fld.at[1, pl.ds(1, XROWS), inner, :], 3)
    l_mass = load(mass_h, src.at[0, :, inner, :], 4)
    l_psrc = load(psrc_h, src.at[1, :, inner, :], 5)
    l_owner = load(owner_h, owner_v, 6)

    barrier = pltpu.get_barrier_semaphore()

    def greet(a, b):
        pl.semaphore_signal(barrier, inc=1, device_id=(a, b), device_id_type=MESH)

    for a in (left, right):
        greet(a, gy)
        for b in (below, above):
            greet(a, b)
    for b in (below, above):
        greet(gx, b)

    def greet_ring(i, carry):
        greet(q * ring + (r + 1 + i) % ring, gy)
        return carry

    def greet_group(i, carry):
        greet(((q + 1 + i) % XGROUP) * ring + r, gy)
        return carry

    lax.fori_loop(0, ring - 1, greet_ring, 0)
    lax.fori_loop(0, XGROUP - 1, greet_group, 0)

    l_mask.wait()
    l_class.wait()
    for x in range(XROWS):
        classes = class_v[x]
        values = jnp.zeros(classes.shape, F32)
        for marker in range(NCLASS):
            values = jnp.where(classes == marker, table[marker], values)
        fld[2, x + 1, inner, :] = mask_v[x].astype(F32) * values
    for copy in (l_conc, l_pot, l_mass, l_psrc, l_owner):
        copy.wait()
    pl.semaphore_wait(barrier, 8 + ring - 1 + XGROUP - 1)

    def remote(source, target, send, recv, device):
        copy = pltpu.make_async_remote_copy(
            src_ref=source, dst_ref=target, send_sem=send, recv_sem=recv, device_id=device, device_id_type=MESH
        )
        copy.start()
        return copy

    head, tail = pl.ds(first, PAD), pl.ds(last - PAD, PAD)
    over, under = pl.ds(last, PAD), pl.ds(0, PAD)
    rows = pl.ds(1, XROWS)
    plan = [
        (fld.at[:, 1, inner], fld.at[:, XROWS + 1, inner], (left, gy)),
        (fld.at[:, XROWS, inner], fld.at[:, 0, inner], (right, gy)),
        (fld.at[:, rows, head], fld.at[:, rows, over], (gx, below)),
        (fld.at[:, rows, tail], fld.at[:, rows, under], (gx, above)),
        (src.at[:, :, head], src.at[:, :, over], (gx, below)),
        (src.at[:, :, tail], src.at[:, :, under], (gx, above)),
        (fld.at[:, 1, head], fld.at[:, XROWS + 1, over], (left, below)),
        (fld.at[:, 1, tail], fld.at[:, XROWS + 1, under], (left, above)),
        (fld.at[:, XROWS, head], fld.at[:, 0, over], (right, below)),
        (fld.at[:, XROWS, tail], fld.at[:, 0, under], (right, above)),
    ]
    ex = [remote(a, b, ex_send.at[i], ex_recv.at[i], dev) for i, (a, b, dev) in enumerate(plan)]

    half = XROWS // 2
    lanes = half * YCELLS * 2
    half_y = YCELLS // 2
    n_cols = half * half_y

    def spread(rows_n, base):
        k = iota((rows_n, n_cols), 0) + base
        block = k // YCELLS
        column = jnp.where((block == 0) | (block == 2), half_y, 0) + (k % YCELLS) // 2
        return (iota((rows_n, n_cols), 1) == column).astype(F32).astype(B16)

    def owners(g):
        return owner_v[pl.ds(g, 1), :].astype(F32)

    own_p, own_m, own_n = owners(left), owners(gx), owners(right)
    off_l = jnp.where(gx == 0, 1, 0)
    off_r = jnp.where(gx == n_gx - 1, 1, 0)

    def wide(values, rows_n):
        return jnp.broadcast_to(values, (rows_n, n_cols)).astype(B16)

    all_rows = spread(lanes, 0)
    lane_block = iota((8, lanes), 1) // YCELLS
    row_p = dot_t(wide(own_p, 8), all_rows)
    row_m = dot_t(wide(own_m, 8), all_rows)
    row_n = dot_t(wide(own_n, 8), all_rows)
    lane_own = jnp.where(lane_block == 0, row_p - 1000.0 * off_l.astype(F32), row_m)
    lane_own = jnp.where(lane_block == 3, row_n - 1000.0 * off_r.astype(F32), lane_own)
    lane_own = lane_own[0:1, :].astype(jnp.int32)
    place[...] = jnp.where(iota((n_gx, lanes), 0) == lane_own, 0.125, 0.0).astype(B16)

    lane = iota((8, n_gx), 1)
    slot = lane // 8 + r + 1
    slot = jnp.where(slot >= ring, slot - ring, slot)
    lane_agg = (slot * 8 + lane % 8)[0:1, :].astype(F32)

    def picks(rows_n, base, values, off):
        column = dot_t(spread(rows_n, base), wide(values, n_gx)) - 1000.0 * off
        return (column == lane_agg).astype(F32).astype(B16)

    pick[0:YCELLS, :] = picks(YCELLS, 0, own_p, off_l.astype(F32))
    pick[YCELLS : 3 * YCELLS, :] = picks(2 * YCELLS, YCELLS, own_m, 0.0)
    pick[3 * YCELLS :, :] = picks(YCELLS, 3 * YCELLS, own_n, off_r.astype(F32))
    e_row = iota((16, n_cols), 0)
    e_col = jnp.where(e_row % 8 == 1, half_y, 0) + jnp.where(e_row >= 8, half_y - 1, 0)
    e_sel = (iota((16, n_cols), 1) == e_col).astype(F32).astype(B16)
    edge_pick[...] = (dot_t(e_sel, wide(own_m, n_gx)) == lane_agg).astype(F32).astype(B16)

    for copy in ex:
        copy.wait_recv()

    @pl.when(gx == 0)
    def _():
        for f in range(3):
            fld[f, 0] = jnp.zeros((YCELLS + 2 * PAD, PLANES), F32)

    @pl.when(gx == n_gx - 1)
    def _():
        for f in range(3):
            fld[f, XROWS + 1] = jnp.zeros((YCELLS + 2 * PAD, PLANES), F32)

    @pl.when(gy == 0)
    def _():
        for f in range(3):
            for x in range(XROWS + 2):
                fld[f, x, 0:PAD, :] = jnp.zeros((PAD, PLANES), F32)

    @pl.when(gy == n_gy - 1)
    def _():
        for f in range(3):
            for x in range(XROWS + 2):
                fld[f, x, last : last + PAD, :] = jnp.zeros((PAD, PLANES), F32)

    def edge_masks(rows_n):
        z = iota((rows_n, PLANES), 1)
        return z == 0, z == PLANES - 1

    def z_sum(value, low, high):
        return jnp.where(high, 0.0, pltpu.roll(value, PLANES - 1, 1)) + jnp.where(low, 0.0, pltpu.roll(value, 1, 1))

    def sweep_one(j, carry):
        base = 1 + 8 * j
        mid, up, dn = pl.ds(base, 8), pl.ds(base + 1, 8), pl.ds(base - 1, 8)
        low, high = edge_masks(8)
        mob = [fld[2, x, mid, :] for x in range(XROWS + 2)]
        face_x = [0.125 * (mob[x] + mob[x + 1]) for x in range(XROWS + 1)]
        for x in range(XROWS + 1):
            w_x[x, mid, :] = face_x[x]
        cc = [fld[0, x, mid, :] for x in range(XROWS + 2)]
        uu = [fld[1, x, mid, :] for x in range(XROWS + 2)]
        for x in range(1, XROWS + 1):
            m, c, u = mob[x], cc[x], uu[x]
            y_up = 0.125 * (m + fld[2, x, up, :])
            y_dn = 0.125 * (m + fld[2, x, dn, :])
            z_up = 0.125 * (m + jnp.where(high, 0.0, pltpu.roll(m, PLANES - 1, 1)))
            z_dn = jnp.where(low, 0.125 * m, pltpu.roll(z_up, 1, 1))
            diagonal = face_x[x - 1] + face_x[x] + y_up + y_dn + z_up + z_dn
            step = relax_fine / (1.0 + 4.0 * diagonal)
            z_w = jnp.where(high, 0.0, z_up)
            w_y[0, x - 1, mid, :] = y_dn
            w_y[1, x - 1, mid, :] = y_up
            w_z[x - 1, mid, :] = z_w
            w_d[x - 1, mid, :] = diagonal
            w_a[x - 1, mid, :] = step
            flow = face_x[x] * uu[x + 1] + face_x[x - 1] * uu[x - 1]
            flow = flow + y_up * fld[1, x, up, :] + y_dn * fld[1, x, dn, :]
            flow = flow + z_w * pltpu.roll(u, PLANES - 1, 1) + pltpu.roll(z_w * u, 1, 1)
            around = cc[x + 1] + cc[x - 1] + fld[0, x, up, :] + fld[0, x, dn, :] + z_sum(c, low, high)
            excess_mass = src[0, x - 1, mid, :] - c + flow - diagonal * u
            excess_pot = src[1, x - 1, mid, :] - u + 4.0 * c - 0.5 * around
            new[0, x, mid, :] = c + step * (excess_mass - diagonal * excess_pot)
            new[1, x, mid, :] = u + step * (excess_pot + 4.0 * excess_mass)
        return carry

    lax.fori_loop(0, (YCELLS + 8) // 8, sweep_one, 0)

    @pl.when(gy == 0)
    def _():
        for f in range(2):
            for x in range(1, XROWS + 1):
                new[f, x, 0:PAD, :] = jnp.zeros((PAD, PLANES), F32)

    @pl.when(gy == n_gy - 1)
    def _():
        for f in range(2):
            for x in range(1, XROWS + 1):
                new[f, x, last : last + PAD, :] = jnp.zeros((PAD, PLANES), F32)

    def excess(x, base, rows_n, low, high, cc, uu):
        mid, up, dn = pl.ds(base, rows_n), pl.ds(base + 1, rows_n), pl.ds(base - 1, rows_n)
        c, u = cc[x], uu[x]
        z_w, diagonal = w_z[x - 1, mid, :], w_d[x - 1, mid, :]
        flow = w_y[1, x - 1, mid, :] * new[1, x, up, :] + w_y[0, x - 1, mid, :] * new[1, x, dn, :]
        flow = flow + z_w * pltpu.roll(u, PLANES - 1, 1) + pltpu.roll(z_w * u, 1, 1)
        around = new[0, x, up, :] + new[0, x, dn, :] + z_sum(c, low, high)
        if (x + 1) in cc:
            flow = flow + w_x[x, mid, :] * uu[x + 1]
            around = around + cc[x + 1]
        if (x - 1) in cc:
            flow = flow + w_x[x - 1, mid, :] * uu[x - 1]
            around = around + cc[x - 1]
        excess_mass = src[0, x - 1, mid, :] - c + flow - diagonal * u
        excess_pot = src[1, x - 1, mid, :] - u + 4.0 * c - 0.5 * around
        return excess_mass, excess_pot, diagonal

    def collect(j, carry):
        base = pl.multiple_of(PAD + 16 * j, 8)
        mid = pl.ds(base, 16)
        low, high = edge_masks(16)
        cc = {x: new[0, x, mid, :] for x in range(1, XROWS + 1)}
        uu = {x: new[1, x, mid, :] for x in range(1, XROWS + 1)}
        got = [excess(x, base, 16, low, high, cc, uu) for x in range(1, XROWS + 1)]
        parts = [(w_x[0, mid, :] * uu[1], -0.5 * cc[1])]
        for i in range(half):
            parts.append((got[2 * i][0] + got[2 * i + 1][0], got[2 * i][1] + got[2 * i + 1][1]))
        parts.append((w_x[XROWS, mid, :] * uu[XROWS], -0.5 * cc[XROWS]))
        for block, pair in enumerate(parts):
            at = pl.ds(pl.multiple_of(block * YCELLS + 16 * j, 16), 16)
            for f in range(2):
                top, rest = halves(pair[f])
                r_hi[at, f * PLANES : (f + 1) * PLANES] = top
                r_mid[at, f * PLANES : (f + 1) * PLANES] = rest
        return carry

    lax.fori_loop(0, YCELLS // 16, collect, 0)

    fine = dot(place[...], r_hi[...]) + dot(place[...], r_mid[...])
    k = iota((2 * PLANES, PLANES), 0)
    pair_up = (iota((2 * PLANES, PLANES), 1) == (k // PLANES) * (PLANES // 2) + (k % PLANES) // 2).astype(F32).astype(B16)
    top, rest = halves(fine)
    totals[...] = (dot(top, pair_up) + dot(rest, pair_up)).reshape(ring, 8, PLANES)

    def scatter(i, carry):
        p = (r + 1 + i) % ring
        remote(totals.at[p], rs_buf.at[ring - 2 - i], g_send.at[0], g_recv.at[0], (q * ring + p, gy))
        return carry

    lax.fori_loop(0, ring - 1, scatter, 0)

    def all_of(ref, count, sem):
        pltpu.make_async_copy(ref.at[pl.ds(0, count)], ref.at[pl.ds(0, count)], sem).wait()

    tally = jnp.zeros((8, n_cols), F32)
    for j in range(8):
        hits = (owner_v[...] == r * 8 + j).astype(F32)
        tally = jnp.where(iota((8, n_cols), 0) == j, jnp.sum(hits, axis=0, keepdims=True), tally)
    count = dot(tally.astype(B16), jnp.ones((n_cols, PLANES), B16))
    count_v[...] = 1.0 / jnp.maximum(count, 1.0)

    all_of(rs_buf, ring - 1, g_recv.at[0])
    mine = totals[r]
    for i in range(ring - 1):
        mine = mine + rs_buf[i]
    part[...] = mine

    def swap(i, carry):
        p = (q + 1 + i) % XGROUP
        remote(part, ar_buf.at[XGROUP - 2 - i], g_send.at[1], g_recv.at[1], (p * ring + r, gy))
        return carry

    lax.fori_loop(0, XGROUP - 1, swap, 0)
    sides = [
        remote(new.at[:, 1, inner], new.at[:, XROWS + 1, inner], n_send.at[0], n_recv.at[0], (left, gy)),
        remote(new.at[:, XROWS, inner], new.at[:, 0, inner], n_send.at[1], n_recv.at[1], (right, gy)),
    ]
    all_of(ar_buf, XGROUP - 1, g_recv.at[1])
    for i in range(XGROUP - 1):
        mine = mine + ar_buf[i]
    mean = mine * count_v[...]

    hp = PLANES // 2
    z = iota((8, PLANES), 1)
    in_c = z < hp
    no_up = (z % hp) == hp - 1
    no_dn = (z % hp) == 0
    gap_pot = jnp.where(in_c, -2.0 * coarse_flux, 1.0 + 2.0 * coarse_bend)
    value = jnp.zeros((8, PLANES), F32)
    for step in range(CSWEEP):
        gap = mean
        if step:
            around = jnp.where(no_up, 0.0, pltpu.roll(value, PLANES - 1, 1)) + jnp.where(no_dn, 0.0, pltpu.roll(value, 1, 1))
            bend = 2.0 * value - around
            cross = jnp.where(in_c, value + coarse_bend * bend, coarse_flux * bend)
            moved = pltpu.roll(cross, hp, 1)
            gap = mean - value + jnp.where(in_c, -moved, moved)
        value = value + (relax_coarse / coarse_det) * (gap + gap_pot * pltpu.roll(gap, hp, 1))
    sol[ring - 1] = value
    part_out = sol.at[ring - 1]

    def gather(i, carry):
        p = (r + 1 + i) % ring
        remote(part_out, sol.at[ring - 2 - i], g_send.at[2], g_recv.at[2], (q * ring + p, gy))
        return carry

    lax.fori_loop(0, ring - 1, gather, 0)

    k = iota((2 * PLANES, 2 * PLANES), 0) % PLANES
    n = iota((2 * PLANES, 2 * PLANES), 1)
    widen = (k == (n // PLANES) * hp + (n % PLANES) // 2).astype(F32).astype(B16)

    all_of(sol, ring - 1, g_recv.at[2])
    solved = sol[...].reshape(n_gx, PLANES)
    both = jnp.concatenate(halves(solved), axis=1)

    edge = dot(edge_pick[...], both)
    edge = edge[:, :PLANES] + edge[:, PLANES:]
    y_out[...] = edge.reshape(2, 8, PLANES)
    ends = [
        remote(y_out.at[0], y_in.at[1], y_send.at[0], y_recv.at[0], (gx, below)),
        remote(y_out.at[1], y_in.at[0], y_send.at[1], y_recv.at[1], (gx, above)),
    ]
    corr[...] = dot(dot(pick[...], both).astype(B16), widen)

    for copy in sides:
        copy.wait()

    @pl.when(gx == 0)
    def _():
        for f in range(2):
            new[f, 0, inner, :] = jnp.zeros((YCELLS, PLANES), F32)

    @pl.when(gx == n_gx - 1)
    def _():
        for f in range(2):
            new[f, XROWS + 1, inner, :] = jnp.zeros((YCELLS, PLANES), F32)

    for x in range(XROWS + 2):
        block = (x + 1) // 2
        at = pl.ds(block * YCELLS, YCELLS)
        for f in range(2):
            new[f, x, inner, :] = new[f, x, inner, :] + corr[at, f * PLANES : (f + 1) * PLANES]

    for copy in ends:
        copy.wait()
    y_all = jnp.concatenate(halves(y_in[...].reshape(16, PLANES)), axis=1)
    y_fine = dot(y_all, widen)
    for side in range(2):
        row = PAD - 1 if side == 0 else last
        for x in range(1, XROWS + 1):
            for f in range(2):
                at = side * 8 + (x - 1) // 2
                add = y_fine[at : at + 1, f * PLANES : (f + 1) * PLANES]
                new[f, x, row : row + 1, :] = new[f, x, row : row + 1, :] + add

    @pl.when(gy == 0)
    def _():
        for f in range(2):
            for x in range(1, XROWS + 1):
                new[f, x, 0:PAD, :] = jnp.zeros((PAD, PLANES), F32)

    @pl.when(gy == n_gy - 1)
    def _():
        for f in range(2):
            for x in range(1, XROWS + 1):
                new[f, x, last : last + PAD, :] = jnp.zeros((PAD, PLANES), F32)

    def finish(j, carry):
        base = pl.multiple_of(PAD + 8 * j, 8)
        mid = pl.ds(base, 8)
        to = pl.ds(pl.multiple_of(8 * j, 8), 8)
        low, high = edge_masks(8)
        cc = {x: new[0, x, mid, :] for x in range(XROWS + 2)}
        uu = {x: new[1, x, mid, :] for x in range(XROWS + 2)}
        for x in range(1, XROWS + 1):
            excess_mass, excess_pot, diagonal = excess(x, base, 8, low, high, cc, uu)
            step = w_a[x - 1, mid, :]
            conc_o[x - 1, to, :] = cc[x] + step * (excess_mass - diagonal * excess_pot)
            pot_o[x - 1, to, :] = uu[x] + step * (excess_pot + 4.0 * excess_mass)
        return carry

    lax.fori_loop(0, YCELLS // 8, finish, 0)

    for copy in ex:
        copy.wait_send()
    all_of(rs_buf, ring - 1, g_send.at[0])
    all_of(ar_buf, XGROUP - 1, g_send.at[1])
    all_of(rs_buf, ring - 1, g_send.at[2])


def solution(mesh):
    n_gx, n_gy = mesh.shape["gx"], mesh.shape["gy"]
    ring = n_gx // XGROUP
    any_spec = pl.BlockSpec(memory_space=pl.ANY)
    y_pad = YCELLS + 2 * PAD
    k_all = 2 * XROWS // 2 * YCELLS

    def on_device(conc, pot, mass, psrc, mask, classes, table, owner):
        out = jax.ShapeDtypeStruct(conc.shape, F32)
        return pl.pallas_call(
            functools.partial(kernel, n_gx, n_gy),
            out_shape=(out, out),
            in_specs=[any_spec] * 6 + [pl.BlockSpec(memory_space=pltpu.SMEM), any_spec],
            out_specs=(pl.BlockSpec(memory_space=pltpu.VMEM),) * 2,
            scratch_shapes=[
                pltpu.VMEM((3, XROWS + 2, y_pad, PLANES), F32),
                pltpu.VMEM((2, XROWS, y_pad, PLANES), F32),
                pltpu.VMEM((XROWS, YCELLS, PLANES), jnp.int32),
                pltpu.VMEM((XROWS, YCELLS, PLANES), jnp.int32),
                pltpu.VMEM(owner.shape, jnp.int32),
                pltpu.VMEM((XROWS + 1, y_pad, PLANES), F32),
                pltpu.VMEM((2, XROWS, y_pad, PLANES), F32),
                pltpu.VMEM((XROWS, y_pad, PLANES), F32),
                pltpu.VMEM((XROWS, y_pad, PLANES), F32),
                pltpu.VMEM((XROWS, y_pad, PLANES), F32),
                pltpu.VMEM((2, XROWS + 2, y_pad, PLANES), F32),
                pltpu.VMEM((k_all, 2 * PLANES), B16),
                pltpu.VMEM((k_all, 2 * PLANES), B16),
                pltpu.VMEM((n_gx, k_all), B16),
                pltpu.VMEM((k_all, n_gx), B16),
                pltpu.VMEM((16, n_gx), B16),
                pltpu.VMEM((8, PLANES), F32),
                pltpu.VMEM((ring, 8, PLANES), F32),
                pltpu.VMEM((ring - 1, 8, PLANES), F32),
                pltpu.VMEM((8, PLANES), F32),
                pltpu.VMEM((XGROUP - 1, 8, PLANES), F32),
                pltpu.VMEM((ring, 8, PLANES), F32),
                pltpu.VMEM((2, 8, PLANES), F32),
                pltpu.VMEM((2, 8, PLANES), F32),
                pltpu.VMEM((k_all, 2 * PLANES), F32),
                pltpu.SemaphoreType.DMA((7,)),
                pltpu.SemaphoreType.DMA((10,)),
                pltpu.SemaphoreType.DMA((10,)),
                pltpu.SemaphoreType.DMA((2,)),
                pltpu.SemaphoreType.DMA((2,)),
                pltpu.SemaphoreType.DMA((3,)),
                pltpu.SemaphoreType.DMA((3,)),
                pltpu.SemaphoreType.DMA((2,)),
                pltpu.SemaphoreType.DMA((2,)),
            ],
            compiler_params=pltpu.CompilerParams(collective_id=0, has_side_effects=True, vmem_limit_bytes=60 << 20),
        )(conc, pot, mass, psrc, mask, classes, table, owner)

    field = P("gx", "gy", None)
    return jax.shard_map(
        on_device,
        mesh=mesh,
        in_specs=(field,) * 6 + (P(), P(None, "gy")),
        out_specs=(field, field),
        check_vma=False,
    )
```

```python
import functools

import jax
import jax.numpy as jnp
from jax import lax
from jax.experimental import pallas as pl
from jax.experimental.pallas import tpu as pltpu
from jax.sharding import PartitionSpec as P

NCLASS = 8
CSWEEP = 3
XROWS = 4
YCELLS = 64
PLANES = 128
PAD = 8
XGROUP = 8

relax_fine = 0.6
relax_coarse = 0.6
coarse_flux = 0.0625
coarse_bend = 0.125
coarse_det = 1.15625

F32 = jnp.float32
B16 = jnp.bfloat16
MESH = pl.DeviceIdType.MESH


def iota(shape, dim):
    return lax.broadcasted_iota(jnp.int32, shape, dim)


def halves(values):
    high = values.astype(B16)
    return high, (values - high.astype(F32)).astype(B16)


def dot(a, b):
    return jnp.dot(a, b, preferred_element_type=F32)


def dot_t(a, b):
    return lax.dot_general(a, b, (((1,), (1,)), ((), ())), preferred_element_type=F32)


def kernel(
    n_gx, n_gy,
    conc_h, pot_h, mass_h, psrc_h, mask_h, class_h, table_h, owner_h,
    conc_o, pot_o,
    fld, src, mask_v, class_v, owner_v, table,
    w_x, w_y, w_z, w_d, w_a, new,
    r_hi, r_mid, place, pick, edge_pick, count_v,
    totals, rs_buf, part, ar_buf, sol, y_out, y_in, corr,
    load_sem, ex_send, ex_recv, n_send, n_recv, g_send, g_recv, y_send, y_recv,
):
    ring = n_gx // XGROUP
    gx = lax.axis_index("gx")
    gy = lax.axis_index("gy")
    r = gx % ring
    q = gx // ring
    left, right = (gx + n_gx - 1) % n_gx, (gx + 1) % n_gx
    below, above = (gy + n_gy - 1) % n_gy, (gy + 1) % n_gy
    first, last = PAD, PAD + YCELLS

    chips = ring // 2
    y_chip, core = r // 2, r % 2

    def away(i, count):
        return count // 2 + ((i + 1) // 2) * (1 - 2 * (i % 2))

    def ring_at(offset, cross):
        return ((y_chip + offset) % chips) * 2 + (1 - core if cross else core)

    barrier = pltpu.get_barrier_semaphore()

    def greet(a, b):
        pl.semaphore_signal(barrier, inc=1, device_id=(a, b), device_id_type=MESH)

    def greet_ring(i, carry):
        for cross in range(2):
            greet(q * ring + ring_at(away(i, chips), cross), gy)
        return carry

    def greet_group(i, carry):
        greet(((q + away(i, XGROUP)) % XGROUP) * ring + r, gy)
        return carry

    lax.fori_loop(0, XGROUP - 1, greet_group, 0)
    lax.fori_loop(0, chips - 1, greet_ring, 0)
    for a in (left, right):
        for b in (below, above):
            greet(a, b)
        greet(a, gy)
    for b in (below, above):
        greet(gx, b)
    greet(q * ring + ring_at(0, 1), gy)

    def load(source, target, index):
        copy = pltpu.make_async_copy(source, target, load_sem.at[index])
        copy.start()
        return copy

    inner = pl.ds(PAD, YCELLS)
    l_table = load(table_h, table, 7)
    l_class = load(class_h, class_v, 1)
    l_mask = load(mask_h, mask_v, 0)
    l_conc = load(conc_h, fld.at[0, pl.ds(1, XROWS), inner, :], 2)
    l_pot = load(pot_h, fld.at[1, pl.ds(1, XROWS), inner, :], 3)
    l_mass = load(mass_h, src.at[0, :, inner, :], 4)
    l_psrc = load(psrc_h, src.at[1, :, inner, :], 5)
    l_owner = load(owner_h, owner_v, 6)

    l_table.wait()
    l_mask.wait()
    l_class.wait()
    for x in range(XROWS):
        classes = class_v[x]
        values = jnp.zeros(classes.shape, F32)
        for marker in range(NCLASS):
            values = jnp.where(classes == marker, table[marker], values)
        fld[2, x + 1, inner, :] = mask_v[x].astype(F32) * values
    for copy in (l_conc, l_pot, l_mass, l_psrc, l_owner):
        copy.wait()
    pl.semaphore_wait(barrier, 8 + ring - 1 + XGROUP - 1)

    def remote(source, target, send, recv, device):
        copy = pltpu.make_async_remote_copy(
            src_ref=source, dst_ref=target, send_sem=send, recv_sem=recv, device_id=device, device_id_type=MESH
        )
        copy.start()
        return copy

    head, tail = pl.ds(first, 2), pl.ds(last - 2, 2)
    over, under = pl.ds(last, 2), pl.ds(first - 2, 2)
    head_1, tail_1 = pl.ds(first, 1), pl.ds(last - 1, 1)
    over_1, under_1 = pl.ds(last, 1), pl.ds(first - 1, 1)
    rows = pl.ds(1, XROWS)
    plan = [
        (fld.at[:, 1, inner], fld.at[:, XROWS + 1, inner], (left, gy)),
        (fld.at[:, XROWS, inner], fld.at[:, 0, inner], (right, gy)),
        (fld.at[:, rows, head], fld.at[:, rows, over], (gx, below)),
        (fld.at[:, rows, tail], fld.at[:, rows, under], (gx, above)),
        (src.at[:, :, head_1], src.at[:, :, over_1], (gx, below)),
        (src.at[:, :, tail_1], src.at[:, :, under_1], (gx, above)),
        (fld.at[:, 1, head_1], fld.at[:, XROWS + 1, over_1], (left, below)),
        (fld.at[:, 1, tail_1], fld.at[:, XROWS + 1, under_1], (left, above)),
        (fld.at[:, XROWS, head_1], fld.at[:, 0, over_1], (right, below)),
        (fld.at[:, XROWS, tail_1], fld.at[:, 0, under_1], (right, above)),
    ]
    ex = [remote(a, b, ex_send.at[i], ex_recv.at[i], dev) for i, (a, b, dev) in enumerate(plan)]

    half = XROWS // 2
    lanes = half * YCELLS * 2
    half_y = YCELLS // 2
    n_cols = half * half_y

    def spread(rows_n, base):
        k = iota((rows_n, n_cols), 0) + base
        block = k // YCELLS
        column = jnp.where((block == 0) | (block == 2), half_y, 0) + (k % YCELLS) // 2
        return (iota((rows_n, n_cols), 1) == column).astype(F32).astype(B16)

    which = iota((8, n_gx), 0)
    chosen = jnp.where(which == 0, left, jnp.where(which == 1, gx, right))
    one_hot = (iota((8, n_gx), 1) == chosen).astype(F32).astype(B16)
    three = dot_t(one_hot, owner_v[...].astype(F32).astype(B16))
    own_p, own_m, own_n = three[0:1, :], three[1:2, :], three[2:3, :]
    off_l = jnp.where(gx == 0, 1, 0)
    off_r = jnp.where(gx == n_gx - 1, 1, 0)

    def wide(values, rows_n):
        return jnp.broadcast_to(values, (rows_n, n_cols)).astype(B16)

    all_rows = spread(lanes, 0)
    lane_block = iota((8, lanes), 1) // YCELLS
    row_p = dot_t(wide(own_p, 8), all_rows)
    row_m = dot_t(wide(own_m, 8), all_rows)
    row_n = dot_t(wide(own_n, 8), all_rows)
    lane_own = jnp.where(lane_block == 0, row_p - 1000.0 * off_l.astype(F32), row_m)
    lane_own = jnp.where(lane_block == 3, row_n - 1000.0 * off_r.astype(F32), lane_own)
    lane_own = lane_own[0:1, :].astype(jnp.int32)
    place[...] = jnp.where(iota((n_gx, lanes), 0) == lane_own, 0.125, 0.0).astype(B16)

    lane = iota((8, n_gx), 1)
    origin = jnp.where(lane // 8 == ring - 1, r, ring_at(0, 1))
    for k in range(chips - 1):
        for cross in range(2):
            origin = jnp.where(lane // 8 == 2 * k + cross, ring_at(chips - away(k, chips), cross), origin)
    lane_agg = (origin * 8 + lane % 8)[0:1, :].astype(F32)

    def picks(rows_n, base, values, off):
        column = dot_t(spread(rows_n, base), wide(values, n_gx)) - 1000.0 * off
        return (column == lane_agg).astype(F32).astype(B16)

    pick[0:YCELLS, :] = picks(YCELLS, 0, own_p, off_l.astype(F32))
    pick[YCELLS : 3 * YCELLS, :] = picks(2 * YCELLS, YCELLS, own_m, 0.0)
    pick[3 * YCELLS :, :] = picks(YCELLS, 3 * YCELLS, own_n, off_r.astype(F32))
    e_row = iota((16, n_cols), 0)
    e_col = jnp.where(e_row % 8 == 1, half_y, 0) + jnp.where(e_row >= 8, half_y - 1, 0)
    e_sel = (iota((16, n_cols), 1) == e_col).astype(F32).astype(B16)
    edge_pick[...] = (dot_t(e_sel, wide(own_m, n_gx)) == lane_agg).astype(F32).astype(B16)

    def edge_masks(rows_n):
        z = iota((rows_n, PLANES), 1)
        return z == 0, z == PLANES - 1

    def z_sum(value, low, high):
        return jnp.where(high, 0.0, pltpu.roll(value, PLANES - 1, 1)) + jnp.where(low, 0.0, pltpu.roll(value, 1, 1))

    def sweep(base, chosen):
        mid, up, dn = pl.ds(base, 8), pl.ds(base + 1, 8), pl.ds(base - 1, 8)
        low, high = edge_masks(8)
        need = sorted({x + d for x in chosen for d in (-1, 0, 1)})
        mob = {x: fld[2, x, mid, :] for x in need}
        cc = {x: fld[0, x, mid, :] for x in need}
        uu = {x: fld[1, x, mid, :] for x in need}
        face_x = {x: 0.125 * (mob[x] + mob[x + 1]) for x in need if x + 1 in mob}
        for x in chosen:
            w_x[x - 1, mid, :] = face_x[x - 1]
            if x + 1 not in chosen:
                w_x[x, mid, :] = face_x[x]
            m, c, u = mob[x], cc[x], uu[x]
            y_up = 0.125 * (m + fld[2, x, up, :])
            y_dn = 0.125 * (m + fld[2, x, dn, :])
            z_up = 0.125 * (m + jnp.where(high, 0.0, pltpu.roll(m, PLANES - 1, 1)))
            z_dn = jnp.where(low, 0.125 * m, pltpu.roll(z_up, 1, 1))
            diagonal = face_x[x - 1] + face_x[x] + y_up + y_dn + z_up + z_dn
            step = relax_fine / (1.0 + 4.0 * diagonal)
            z_w = jnp.where(high, 0.0, z_up)
            w_y[0, x - 1, mid, :] = y_dn
            w_y[1, x - 1, mid, :] = y_up
            w_z[x - 1, mid, :] = z_w
            w_d[x - 1, mid, :] = diagonal
            w_a[x - 1, mid, :] = step
            flow = face_x[x] * uu[x + 1] + face_x[x - 1] * uu[x - 1]
            flow = flow + y_up * fld[1, x, up, :] + y_dn * fld[1, x, dn, :]
            flow = flow + z_w * pltpu.roll(u, PLANES - 1, 1) + pltpu.roll(z_w * u, 1, 1)
            around = cc[x + 1] + cc[x - 1] + fld[0, x, up, :] + fld[0, x, dn, :] + z_sum(c, low, high)
            excess_mass = src[0, x - 1, mid, :] - c + flow - diagonal * u
            excess_pot = src[1, x - 1, mid, :] - u + 4.0 * c - 0.5 * around
            new[0, x, mid, :] = c + step * (excess_mass - diagonal * excess_pot)
            new[1, x, mid, :] = u + step * (excess_pot + 4.0 * excess_mass)

    def sweeps(count, base, stride, chosen):
        def body(j, carry):
            sweep(base + stride * j, chosen)
            return carry

        lax.fori_loop(0, count, body, 0)

    middle = tuple(range(2, XROWS))
    sweeps((YCELLS - 8) // 8, first + 1, 8, middle)
    sweeps(1, last - 9, 8, middle)

    for copy in ex:
        copy.wait_recv()

    @pl.when(gx == 0)
    def _():
        for f in range(3):
            fld[f, 0] = jnp.zeros((YCELLS + 2 * PAD, PLANES), F32)

    @pl.when(gx == n_gx - 1)
    def _():
        for f in range(3):
            fld[f, XROWS + 1] = jnp.zeros((YCELLS + 2 * PAD, PLANES), F32)

    @pl.when(gy == 0)
    def _():
        for f in range(3):
            for x in range(XROWS + 2):
                fld[f, x, 0:PAD, :] = jnp.zeros((PAD, PLANES), F32)

    @pl.when(gy == n_gy - 1)
    def _():
        for f in range(3):
            for x in range(XROWS + 2):
                fld[f, x, last : last + PAD, :] = jnp.zeros((PAD, PLANES), F32)

    sweeps((YCELLS + 8) // 8, 1, 8, (1, XROWS))
    sweeps(2, 1, YCELLS, middle)

    @pl.when(gy == 0)
    def _():
        for f in range(2):
            for x in range(1, XROWS + 1):
                new[f, x, 0:PAD, :] = jnp.zeros((PAD, PLANES), F32)

    @pl.when(gy == n_gy - 1)
    def _():
        for f in range(2):
            for x in range(1, XROWS + 1):
                new[f, x, last : last + PAD, :] = jnp.zeros((PAD, PLANES), F32)

    def excess(x, base, rows_n, low, high, cc, uu):
        mid, up, dn = pl.ds(base, rows_n), pl.ds(base + 1, rows_n), pl.ds(base - 1, rows_n)
        c, u = cc[x], uu[x]
        z_w, diagonal = w_z[x - 1, mid, :], w_d[x - 1, mid, :]
        flow = w_y[1, x - 1, mid, :] * new[1, x, up, :] + w_y[0, x - 1, mid, :] * new[1, x, dn, :]
        flow = flow + z_w * pltpu.roll(u, PLANES - 1, 1) + pltpu.roll(z_w * u, 1, 1)
        around = new[0, x, up, :] + new[0, x, dn, :] + z_sum(c, low, high)
        if (x + 1) in cc:
            flow = flow + w_x[x, mid, :] * uu[x + 1]
            around = around + cc[x + 1]
        if (x - 1) in cc:
            flow = flow + w_x[x - 1, mid, :] * uu[x - 1]
            around = around + cc[x - 1]
        excess_mass = src[0, x - 1, mid, :] - c + flow - diagonal * u
        excess_pot = src[1, x - 1, mid, :] - u + 4.0 * c - 0.5 * around
        return excess_mass, excess_pot, diagonal

    def collect(j, carry):
        base = pl.multiple_of(PAD + 16 * j, 8)
        mid = pl.ds(base, 16)
        low, high = edge_masks(16)
        cc = {x: new[0, x, mid, :] for x in range(1, XROWS + 1)}
        uu = {x: new[1, x, mid, :] for x in range(1, XROWS + 1)}
        got = [excess(x, base, 16, low, high, cc, uu) for x in range(1, XROWS + 1)]
        parts = [(w_x[0, mid, :] * uu[1], -0.5 * cc[1])]
        for i in range(half):
            parts.append((got[2 * i][0] + got[2 * i + 1][0], got[2 * i][1] + got[2 * i + 1][1]))
        parts.append((w_x[XROWS, mid, :] * uu[XROWS], -0.5 * cc[XROWS]))
        for block, pair in enumerate(parts):
            at = pl.ds(pl.multiple_of(block * YCELLS + 16 * j, 16), 16)
            for f in range(2):
                top, rest = halves(pair[f])
                r_hi[at, f * PLANES : (f + 1) * PLANES] = top
                r_mid[at, f * PLANES : (f + 1) * PLANES] = rest
        return carry

    lax.fori_loop(0, YCELLS // 16, collect, 0)

    fine = dot(place[...], r_hi[...]) + dot(place[...], r_mid[...])
    k = iota((2 * PLANES, PLANES), 0)
    pair_up = (iota((2 * PLANES, PLANES), 1) == (k // PLANES) * (PLANES // 2) + (k % PLANES) // 2).astype(F32).astype(B16)
    top, rest = halves(fine)
    totals[...] = (dot(top, pair_up) + dot(rest, pair_up)).reshape(ring, 8, PLANES)

    def to_ring(source, target, index):
        def one(offset, cross, slot):
            p = ring_at(offset, cross)
            remote(source(p), target.at[slot], g_send.at[index], g_recv.at[index], (q * ring + p, gy))

        def body(i, carry):
            for cross in range(2):
                one(away(i, chips), cross, 2 * i + cross)
            return carry

        lax.fori_loop(0, chips - 1, body, 0)
        one(0, 1, ring - 2)

    to_ring(lambda p: totals.at[p], rs_buf, 0)

    def all_of(ref, count, sem):
        pltpu.make_async_copy(ref.at[pl.ds(0, count)], ref.at[pl.ds(0, count)], sem).wait()

    tally = jnp.zeros((8, n_gx), F32)
    for j in range(8):
        hits = (owner_v[...] == r * 8 + j).astype(F32)
        tally = jnp.where(iota((8, n_gx), 0) == j, jnp.sum(hits, axis=0, keepdims=True), tally)
    count = dot(tally.astype(B16), jnp.ones((n_gx, PLANES), B16))
    count_v[...] = 1.0 / jnp.maximum(count, 1.0)

    all_of(rs_buf, ring - 1, g_recv.at[0])
    mine = totals[r]
    for i in range(ring - 1):
        mine = mine + rs_buf[i]
    part[...] = mine

    def swap(i, carry):
        p = (q + away(i, XGROUP)) % XGROUP
        remote(part, ar_buf.at[i], g_send.at[1], g_recv.at[1], (p * ring + r, gy))
        return carry

    lax.fori_loop(0, XGROUP - 1, swap, 0)
    sides = [
        remote(new.at[:, 1, inner], new.at[:, XROWS + 1, inner], n_send.at[0], n_recv.at[0], (left, gy)),
        remote(new.at[:, XROWS, inner], new.at[:, 0, inner], n_send.at[1], n_recv.at[1], (right, gy)),
    ]
    all_of(ar_buf, XGROUP - 1, g_recv.at[1])
    for i in range(XGROUP - 1):
        mine = mine + ar_buf[i]
    mean = mine * count_v[...]

    hp = PLANES // 2
    z = iota((8, PLANES), 1)
    in_c = z < hp
    no_up = (z % hp) == hp - 1
    no_dn = (z % hp) == 0
    gap_pot = jnp.where(in_c, -2.0 * coarse_flux, 1.0 + 2.0 * coarse_bend)
    value = jnp.zeros((8, PLANES), F32)
    for step in range(CSWEEP):
        gap = mean
        if step:
            around = jnp.where(no_up, 0.0, pltpu.roll(value, PLANES - 1, 1)) + jnp.where(no_dn, 0.0, pltpu.roll(value, 1, 1))
            bend = 2.0 * value - around
            cross = jnp.where(in_c, value + coarse_bend * bend, coarse_flux * bend)
            moved = pltpu.roll(cross, hp, 1)
            gap = mean - value + jnp.where(in_c, -moved, moved)
        value = value + (relax_coarse / coarse_det) * (gap + gap_pot * pltpu.roll(gap, hp, 1))
    sol[ring - 1] = value
    to_ring(lambda p: sol.at[ring - 1], sol, 2)

    k = iota((2 * PLANES, 2 * PLANES), 0) % PLANES
    n = iota((2 * PLANES, 2 * PLANES), 1)
    widen = (k == (n // PLANES) * hp + (n % PLANES) // 2).astype(F32).astype(B16)

    all_of(sol, ring - 1, g_recv.at[2])
    solved = sol[...].reshape(n_gx, PLANES)
    both = jnp.concatenate(halves(solved), axis=1)

    edge = dot(edge_pick[...], both)
    edge = edge[:, :PLANES] + edge[:, PLANES:]
    y_out[...] = edge.reshape(2, 8, PLANES)
    ends = [
        remote(y_out.at[0], y_in.at[1], y_send.at[0], y_recv.at[0], (gx, below)),
        remote(y_out.at[1], y_in.at[0], y_send.at[1], y_recv.at[1], (gx, above)),
    ]
    corr[...] = dot(dot(pick[...], both).astype(B16), widen)

    for copy in sides:
        copy.wait()

    @pl.when(gx == 0)
    def _():
        for f in range(2):
            new[f, 0, inner, :] = jnp.zeros((YCELLS, PLANES), F32)

    @pl.when(gx == n_gx - 1)
    def _():
        for f in range(2):
            new[f, XROWS + 1, inner, :] = jnp.zeros((YCELLS, PLANES), F32)

    for x in range(XROWS + 2):
        block = (x + 1) // 2
        at = pl.ds(block * YCELLS, YCELLS)
        for f in range(2):
            new[f, x, inner, :] = new[f, x, inner, :] + corr[at, f * PLANES : (f + 1) * PLANES]

    def finish(j, carry):
        base = pl.multiple_of(PAD + 8 * j, 8)
        mid = pl.ds(base, 8)
        to = pl.ds(pl.multiple_of(8 * j, 8), 8)
        low, high = edge_masks(8)
        cc = {x: new[0, x, mid, :] for x in range(XROWS + 2)}
        uu = {x: new[1, x, mid, :] for x in range(XROWS + 2)}
        for x in range(1, XROWS + 1):
            excess_mass, excess_pot, diagonal = excess(x, base, 8, low, high, cc, uu)
            step = w_a[x - 1, mid, :]
            conc_o[x - 1, to, :] = cc[x] + step * (excess_mass - diagonal * excess_pot)
            pot_o[x - 1, to, :] = uu[x] + step * (excess_pot + 4.0 * excess_mass)
        return carry

    lax.fori_loop(1, YCELLS // 8 - 1, finish, 0)

    for copy in ends:
        copy.wait()
    y_all = jnp.concatenate(halves(y_in[...].reshape(16, PLANES)), axis=1)
    y_fine = dot(y_all, widen)
    for side in range(2):
        row = PAD - 1 if side == 0 else last
        for x in range(1, XROWS + 1):
            for f in range(2):
                at = side * 8 + (x - 1) // 2
                add = y_fine[at : at + 1, f * PLANES : (f + 1) * PLANES]
                new[f, x, row : row + 1, :] = new[f, x, row : row + 1, :] + add

    @pl.when(gy == 0)
    def _():
        for f in range(2):
            for x in range(1, XROWS + 1):
                new[f, x, 0:PAD, :] = jnp.zeros((PAD, PLANES), F32)

    @pl.when(gy == n_gy - 1)
    def _():
        for f in range(2):
            for x in range(1, XROWS + 1):
                new[f, x, last : last + PAD, :] = jnp.zeros((PAD, PLANES), F32)

    def finish_ends(j, carry):
        return finish(j * (YCELLS // 8 - 1), carry)

    lax.fori_loop(0, 2, finish_ends, 0)

    for copy in ex:
        copy.wait_send()
    all_of(rs_buf, ring - 1, g_send.at[0])
    all_of(ar_buf, XGROUP - 1, g_send.at[1])
    all_of(rs_buf, ring - 1, g_send.at[2])


def hand_out(conc_v, pot_v, conc_o, pot_o, sem):
    copies = [
        pltpu.make_async_copy(conc_v, conc_o, sem.at[0]),
        pltpu.make_async_copy(pot_v, pot_o, sem.at[1]),
    ]
    for copy in copies:
        copy.start()
    for copy in copies:
        copy.wait()


def solution(mesh):
    n_gx, n_gy = mesh.shape["gx"], mesh.shape["gy"]
    ring = n_gx // XGROUP
    any_spec = pl.BlockSpec(memory_space=pl.ANY)
    y_pad = YCELLS + 2 * PAD
    k_all = 2 * XROWS // 2 * YCELLS

    def on_device(conc, pot, mass, psrc, mask, classes, table, owner):
        out = jax.ShapeDtypeStruct(conc.shape, F32)
        held = pl.pallas_call(
            functools.partial(kernel, n_gx, n_gy),
            out_shape=(out, out),
            in_specs=[any_spec] * 8,
            out_specs=(pl.BlockSpec(memory_space=pltpu.VMEM),) * 2,
            scratch_shapes=[
                pltpu.VMEM((3, XROWS + 2, y_pad, PLANES), F32),
                pltpu.VMEM((2, XROWS, y_pad, PLANES), F32),
                pltpu.VMEM((XROWS, YCELLS, PLANES), jnp.int32),
                pltpu.VMEM((XROWS, YCELLS, PLANES), jnp.int32),
                pltpu.VMEM((owner.shape[1], owner.shape[0]), jnp.int32),
                pltpu.SMEM((NCLASS,), F32),
                pltpu.VMEM((XROWS + 1, y_pad, PLANES), F32),
                pltpu.VMEM((2, XROWS, y_pad, PLANES), F32),
                pltpu.VMEM((XROWS, y_pad, PLANES), F32),
                pltpu.VMEM((XROWS, y_pad, PLANES), F32),
                pltpu.VMEM((XROWS, y_pad, PLANES), F32),
                pltpu.VMEM((2, XROWS + 2, y_pad, PLANES), F32),
                pltpu.VMEM((k_all, 2 * PLANES), B16),
                pltpu.VMEM((k_all, 2 * PLANES), B16),
                pltpu.VMEM((n_gx, k_all), B16),
                pltpu.VMEM((k_all, n_gx), B16),
                pltpu.VMEM((16, n_gx), B16),
                pltpu.VMEM((8, PLANES), F32),
                pltpu.VMEM((ring, 8, PLANES), F32),
                pltpu.VMEM((ring - 1, 8, PLANES), F32),
                pltpu.VMEM((8, PLANES), F32),
                pltpu.VMEM((XGROUP - 1, 8, PLANES), F32),
                pltpu.VMEM((ring, 8, PLANES), F32),
                pltpu.VMEM((2, 8, PLANES), F32),
                pltpu.VMEM((2, 8, PLANES), F32),
                pltpu.VMEM((k_all, 2 * PLANES), F32),
                pltpu.SemaphoreType.DMA((8,)),
                pltpu.SemaphoreType.DMA((10,)),
                pltpu.SemaphoreType.DMA((10,)),
                pltpu.SemaphoreType.DMA((2,)),
                pltpu.SemaphoreType.DMA((2,)),
                pltpu.SemaphoreType.DMA((3,)),
                pltpu.SemaphoreType.DMA((3,)),
                pltpu.SemaphoreType.DMA((2,)),
                pltpu.SemaphoreType.DMA((2,)),
            ],
            compiler_params=pltpu.CompilerParams(collective_id=0, has_side_effects=True, vmem_limit_bytes=54912 << 10),
        )(conc, pot, mass, psrc, mask, classes, table, owner.T)
        return pl.pallas_call(
            hand_out,
            out_shape=(out, out),
            in_specs=[pl.BlockSpec(memory_space=pltpu.VMEM)] * 2,
            out_specs=(any_spec, any_spec),
            scratch_shapes=[pltpu.SemaphoreType.DMA((2,))],
            compiler_params=pltpu.CompilerParams(vmem_limit_bytes=1 << 20),
        )(*held)

    field = P("gx", "gy", None)
    return jax.shard_map(
        on_device,
        mesh=mesh,
        in_specs=(field,) * 6 + (P(), P(None, "gy")),
        out_specs=(field, field),
        check_vma=False,
    )
```

```python
import functools

import jax
import jax.numpy as jnp
from jax import lax
from jax.experimental import pallas as pl
from jax.experimental.pallas import tpu as pltpu
from jax.sharding import PartitionSpec as P

NCLASS = 8
CSWEEP = 3
XROWS = 4
YCELLS = 64
PLANES = 128
PAD = 8
XGROUP = 8

relax_fine = 0.6
relax_coarse = 0.6
coarse_flux = 0.0625
coarse_bend = 0.125
coarse_det = 1.15625

F32 = jnp.float32
B16 = jnp.bfloat16
MESH = pl.DeviceIdType.MESH


def iota(shape, dim):
    return lax.broadcasted_iota(jnp.int32, shape, dim)


def halves(values):
    high = values.astype(B16)
    return high, (values - high.astype(F32)).astype(B16)


def dot(a, b):
    return jnp.dot(a, b, preferred_element_type=F32)


def dot_t(a, b):
    return lax.dot_general(a, b, (((1,), (1,)), ((), ())), preferred_element_type=F32)


def kernel(
    n_gx, n_gy,
    conc_h, pot_h, mass_h, psrc_h, mask_h, class_h, table_h, owner_h,
    conc_o, pot_o,
    fld, src, mask_v, class_v, owner_v, table,
    w_x, w_y, w_z, w_d, w_a, new,
    r_hi, r_mid, place, pick, edge_pick, count_v,
    totals, rs_buf, part, ar_buf, sol, y_out, y_in, corr,
    load_sem, ex_send, ex_recv, n_send, n_recv, g_send, g_recv, y_send, y_recv,
):
    ring = n_gx // XGROUP
    gx = lax.axis_index("gx")
    gy = lax.axis_index("gy")
    r = gx % ring
    q = gx // ring
    left, right = (gx + n_gx - 1) % n_gx, (gx + 1) % n_gx
    below, above = (gy + n_gy - 1) % n_gy, (gy + 1) % n_gy
    first, last = PAD, PAD + YCELLS

    chips = ring // 2
    y_chip, core = r // 2, r % 2

    def away(i, count):
        return count // 2 + ((i + 1) // 2) * (1 - 2 * (i % 2))

    def ring_at(offset, cross):
        return ((y_chip + offset) % chips) * 2 + (1 - core if cross else core)

    barrier = pltpu.get_barrier_semaphore()

    def greet(a, b):
        pl.semaphore_signal(barrier, inc=1, device_id=(a, b), device_id_type=MESH)

    def greet_ring(i, carry):
        for cross in range(2):
            greet(q * ring + ring_at(away(i, chips), cross), gy)
        return carry

    def greet_group(i, carry):
        greet(((q + away(i, XGROUP)) % XGROUP) * ring + r, gy)
        return carry

    lax.fori_loop(0, XGROUP - 1, greet_group, 0)
    lax.fori_loop(0, chips - 1, greet_ring, 0)
    for a in (left, right):
        for b in (below, above):
            greet(a, b)
        greet(a, gy)
    for b in (below, above):
        greet(gx, b)
    greet(q * ring + ring_at(0, 1), gy)

    def load(source, target, index):
        copy = pltpu.make_async_copy(source, target, load_sem.at[index])
        copy.start()
        return copy

    inner = pl.ds(PAD, YCELLS)
    l_table = load(table_h, table, 7)
    l_class = load(class_h, class_v, 1)
    l_mask = load(mask_h, mask_v, 0)
    l_conc = load(conc_h, fld.at[0, pl.ds(1, XROWS), inner, :], 2)
    l_pot = load(pot_h, fld.at[1, pl.ds(1, XROWS), inner, :], 3)
    l_mass = load(mass_h, src.at[0, :, inner, :], 4)
    l_psrc = load(psrc_h, src.at[1, :, inner, :], 5)
    l_owner = load(owner_h, owner_v, 6)

    l_table.wait()
    l_mask.wait()
    l_class.wait()
    for x in range(XROWS):
        classes = class_v[x]
        values = jnp.zeros(classes.shape, F32)
        for marker in range(NCLASS):
            values = jnp.where(classes == marker, table[marker], values)
        fld[2, x + 1, inner, :] = mask_v[x].astype(F32) * values
    for copy in (l_conc, l_pot, l_mass, l_psrc, l_owner):
        copy.wait()
    pl.semaphore_wait(barrier, 8 + ring - 1 + XGROUP - 1)

    def remote(source, target, send, recv, device):
        copy = pltpu.make_async_remote_copy(
            src_ref=source, dst_ref=target, send_sem=send, recv_sem=recv, device_id=device, device_id_type=MESH
        )
        copy.start()
        return copy

    head, tail = pl.ds(first, 2), pl.ds(last - 2, 2)
    over, under = pl.ds(last, 2), pl.ds(first - 2, 2)
    head_1, tail_1 = pl.ds(first, 1), pl.ds(last - 1, 1)
    over_1, under_1 = pl.ds(last, 1), pl.ds(first - 1, 1)
    rows = pl.ds(1, XROWS)
    plan = [
        (fld.at[:, 1, head_1], fld.at[:, XROWS + 1, over_1], (left, below)),
        (fld.at[:, 1, tail_1], fld.at[:, XROWS + 1, under_1], (left, above)),
        (fld.at[:, XROWS, head_1], fld.at[:, 0, over_1], (right, below)),
        (fld.at[:, XROWS, tail_1], fld.at[:, 0, under_1], (right, above)),
        (fld.at[:, 1, inner], fld.at[:, XROWS + 1, inner], (left, gy)),
        (fld.at[:, XROWS, inner], fld.at[:, 0, inner], (right, gy)),
        (fld.at[:, rows, head], fld.at[:, rows, over], (gx, below)),
        (fld.at[:, rows, tail], fld.at[:, rows, under], (gx, above)),
        (src.at[:, :, head_1], src.at[:, :, over_1], (gx, below)),
        (src.at[:, :, tail_1], src.at[:, :, under_1], (gx, above)),
    ]
    ex = [remote(a, b, ex_send.at[i], ex_recv.at[i], dev) for i, (a, b, dev) in enumerate(plan)]

    half = XROWS // 2
    lanes = half * YCELLS * 2
    half_y = YCELLS // 2
    n_cols = half * half_y

    def spread(rows_n, base):
        k = iota((rows_n, n_cols), 0) + base
        block = k // YCELLS
        column = jnp.where((block == 0) | (block == 2), half_y, 0) + (k % YCELLS) // 2
        return (iota((rows_n, n_cols), 1) == column).astype(F32).astype(B16)

    which = iota((8, n_gx), 0)
    chosen = jnp.where(which == 0, left, jnp.where(which == 1, gx, right))
    one_hot = (iota((8, n_gx), 1) == chosen).astype(F32).astype(B16)
    three = dot_t(one_hot, owner_v[...].astype(F32).astype(B16))
    own_p, own_m, own_n = three[0:1, :], three[1:2, :], three[2:3, :]
    off_l = jnp.where(gx == 0, 1, 0)
    off_r = jnp.where(gx == n_gx - 1, 1, 0)

    def wide(values, rows_n):
        return jnp.broadcast_to(values, (rows_n, n_cols)).astype(B16)

    all_rows = spread(lanes, 0)
    lane_block = iota((8, lanes), 1) // YCELLS
    row_p = dot_t(wide(own_p, 8), all_rows)
    row_m = dot_t(wide(own_m, 8), all_rows)
    row_n = dot_t(wide(own_n, 8), all_rows)
    lane_own = jnp.where(lane_block == 0, row_p - 1000.0 * off_l.astype(F32), row_m)
    lane_own = jnp.where(lane_block == 3, row_n - 1000.0 * off_r.astype(F32), lane_own)
    lane_own = lane_own[0:1, :].astype(jnp.int32)
    place[...] = jnp.where(iota((n_gx, lanes), 0) == lane_own, 0.125, 0.0).astype(B16)

    lane = iota((8, n_gx), 1)
    origin = jnp.where(lane // 8 == ring - 1, r, ring_at(0, 1))
    for k in range(chips - 1):
        for cross in range(2):
            origin = jnp.where(lane // 8 == 2 * k + cross, ring_at(chips - away(k, chips), cross), origin)
    lane_agg = (origin * 8 + lane % 8)[0:1, :].astype(F32)

    def picks(rows_n, base, values, off):
        column = dot_t(spread(rows_n, base), wide(values, n_gx)) - 1000.0 * off
        return (column == lane_agg).astype(F32).astype(B16)

    pick[0:YCELLS, :] = picks(YCELLS, 0, own_p, off_l.astype(F32))
    pick[YCELLS : 3 * YCELLS, :] = picks(2 * YCELLS, YCELLS, own_m, 0.0)
    pick[3 * YCELLS :, :] = picks(YCELLS, 3 * YCELLS, own_n, off_r.astype(F32))
    e_row = iota((16, n_cols), 0)
    e_col = jnp.where(e_row % 8 == 1, half_y, 0) + jnp.where(e_row >= 8, half_y - 1, 0)
    e_sel = (iota((16, n_cols), 1) == e_col).astype(F32).astype(B16)
    edge_pick[...] = (dot_t(e_sel, wide(own_m, n_gx)) == lane_agg).astype(F32).astype(B16)

    def edge_masks(rows_n):
        z = iota((rows_n, PLANES), 1)
        return z == 0, z == PLANES - 1

    def z_sum(value, low, high):
        return jnp.where(high, 0.0, pltpu.roll(value, PLANES - 1, 1)) + jnp.where(low, 0.0, pltpu.roll(value, 1, 1))

    def settle(x, mid, c, u, diagonal, mass_part, pot_part):
        step = relax_fine / (1.0 + 4.0 * diagonal)
        w_d[x - 1, mid, :] = diagonal
        w_a[x - 1, mid, :] = step
        excess_mass = mass_part - diagonal * u
        new[0, x, mid, :] = c + step * (excess_mass - diagonal * pot_part)
        new[1, x, mid, :] = u + step * (pot_part + 4.0 * excess_mass)

    def sweep(base, with_sides):
        mid, up, dn = pl.ds(base, 8), pl.ds(base + 1, 8), pl.ds(base - 1, 8)
        low, high = edge_masks(8)
        need = range(XROWS + 2) if with_sides else range(1, XROWS + 1)
        mob = {x: fld[2, x, mid, :] for x in need}
        cc = {x: fld[0, x, mid, :] for x in need}
        uu = {x: fld[1, x, mid, :] for x in need}
        face_x = {x: 0.125 * (mob[x] + mob[x + 1]) for x in need if x + 1 in mob}
        for x, face in face_x.items():
            w_x[x, mid, :] = face
        for x in range(1, XROWS + 1):
            m, c, u = mob[x], cc[x], uu[x]
            y_up = 0.125 * (m + fld[2, x, up, :])
            y_dn = 0.125 * (m + fld[2, x, dn, :])
            z_up = 0.125 * (m + jnp.where(high, 0.0, pltpu.roll(m, PLANES - 1, 1)))
            z_dn = jnp.where(low, 0.125 * m, pltpu.roll(z_up, 1, 1))
            z_w = jnp.where(high, 0.0, z_up)
            w_y[0, x - 1, mid, :] = y_dn
            w_y[1, x - 1, mid, :] = y_up
            w_z[x - 1, mid, :] = z_w
            diagonal = (y_up + y_dn) + (z_up + z_dn)
            flow = y_up * fld[1, x, up, :] + y_dn * fld[1, x, dn, :]
            flow = flow + (z_w * pltpu.roll(u, PLANES - 1, 1) + pltpu.roll(z_w * u, 1, 1))
            around = (fld[0, x, up, :] + fld[0, x, dn, :]) + z_sum(c, low, high)
            for face, other in ((x, x + 1), (x - 1, x - 1)):
                if face in face_x:
                    diagonal = diagonal + face_x[face]
                    flow = flow + face_x[face] * uu[other]
                    around = around + cc[other]
            mass_part = (src[0, x - 1, mid, :] - c) + flow
            pot_part = (src[1, x - 1, mid, :] - u + 4.0 * c) - 0.5 * around
            if x in face_x and x - 1 in face_x:
                settle(x, mid, c, u, diagonal, mass_part, pot_part)
            else:
                w_d[x - 1, mid, :] = diagonal
                new[0, x, mid, :] = mass_part
                new[1, x, mid, :] = pot_part

    def add_sides(base):
        mid = pl.ds(base, 8)
        for x, face, other in ((1, 0, 0), (XROWS, XROWS, XROWS + 1)):
            weight = 0.125 * (fld[2, x, mid, :] + fld[2, other, mid, :])
            w_x[face, mid, :] = weight
            diagonal = w_d[x - 1, mid, :] + weight
            mass_part = new[0, x, mid, :] + weight * fld[1, other, mid, :]
            pot_part = new[1, x, mid, :] - 0.5 * fld[0, other, mid, :]
            settle(x, mid, fld[0, x, mid, :], fld[1, x, mid, :], diagonal, mass_part, pot_part)

    def over_rows(count, base, stride, do):
        def body(j, carry):
            do(base + stride * j)
            return carry

        lax.fori_loop(0, count, body, 0)

    n_mid = (YCELLS - 8) // 8
    over_rows(n_mid, first + 1, 8, lambda base: sweep(base, False))

    for copy in ex:
        copy.wait_recv()

    @pl.when(gx == 0)
    def _():
        for f in range(3):
            fld[f, 0] = jnp.zeros((YCELLS + 2 * PAD, PLANES), F32)

    @pl.when(gx == n_gx - 1)
    def _():
        for f in range(3):
            fld[f, XROWS + 1] = jnp.zeros((YCELLS + 2 * PAD, PLANES), F32)

    @pl.when(gy == 0)
    def _():
        for f in range(3):
            for x in range(XROWS + 2):
                fld[f, x, 0:PAD, :] = jnp.zeros((PAD, PLANES), F32)

    @pl.when(gy == n_gy - 1)
    def _():
        for f in range(3):
            for x in range(XROWS + 2):
                fld[f, x, last : last + PAD, :] = jnp.zeros((PAD, PLANES), F32)

    over_rows(n_mid, first + 1, 8, add_sides)
    over_rows(2, 1, YCELLS, lambda base: sweep(base, True))

    @pl.when(gy == 0)
    def _():
        for f in range(2):
            for x in range(1, XROWS + 1):
                new[f, x, 0:PAD, :] = jnp.zeros((PAD, PLANES), F32)

    @pl.when(gy == n_gy - 1)
    def _():
        for f in range(2):
            for x in range(1, XROWS + 1):
                new[f, x, last : last + PAD, :] = jnp.zeros((PAD, PLANES), F32)

    def mass_excess(x, base, rows_n, cc, uu):
        mid, up, dn = pl.ds(base, rows_n), pl.ds(base + 1, rows_n), pl.ds(base - 1, rows_n)
        u, z_w = uu[x], w_z[x - 1, mid, :]
        flow = w_y[1, x - 1, mid, :] * new[1, x, up, :] + w_y[0, x - 1, mid, :] * new[1, x, dn, :]
        flow = flow + (z_w * pltpu.roll(u, PLANES - 1, 1) + pltpu.roll(z_w * u, 1, 1))
        if (x + 1) in uu:
            flow = flow + w_x[x, mid, :] * uu[x + 1]
        if (x - 1) in uu:
            flow = flow + w_x[x - 1, mid, :] * uu[x - 1]
        return (src[0, x - 1, mid, :] - cc[x]) + (flow - w_d[x - 1, mid, :] * u)

    def collect(j, carry):
        base = pl.multiple_of(PAD + 16 * j, 8)
        mid = pl.ds(base, 16)
        low, high = edge_masks(16)
        cc = {x: new[0, x, mid, :] for x in range(1, XROWS + 1)}
        uu = {x: new[1, x, mid, :] for x in range(1, XROWS + 1)}
        mass = {x: mass_excess(x, base, 16, cc, uu) for x in cc}
        up, dn = pl.ds(base + 1, 16), pl.ds(base - 1, 16)
        parts = [(w_x[0, mid, :] * uu[1], -0.5 * cc[1])]
        for a in range(1, XROWS, 2):
            conc = cc[a] + cc[a + 1]
            around = (new[0, a, up, :] + new[0, a + 1, up, :]) + (new[0, a, dn, :] + new[0, a + 1, dn, :])
            around = around + z_sum(conc, low, high)
            for other in (a - 1, a + 2):
                if other in cc:
                    around = around + cc[other]
            psrc = src[1, a - 1, mid, :] + src[1, a, mid, :]
            parts.append((mass[a] + mass[a + 1], psrc - (uu[a] + uu[a + 1]) + 3.5 * conc - 0.5 * around))
        parts.append((w_x[XROWS, mid, :] * uu[XROWS], -0.5 * cc[XROWS]))
        for block, pair in enumerate(parts):
            at = pl.ds(pl.multiple_of(block * YCELLS + 16 * j, 16), 16)
            for f in range(2):
                top, rest = halves(pair[f])
                r_hi[at, f * PLANES : (f + 1) * PLANES] = top
                r_mid[at, f * PLANES : (f + 1) * PLANES] = rest
        return carry

    lax.fori_loop(0, YCELLS // 16, collect, 0)

    fine = dot(place[...], r_hi[...]) + dot(place[...], r_mid[...])
    k = iota((2 * PLANES, PLANES), 0)
    pair_up = (iota((2 * PLANES, PLANES), 1) == (k // PLANES) * (PLANES // 2) + (k % PLANES) // 2).astype(F32).astype(B16)
    top, rest = halves(fine)
    totals[...] = (dot(top, pair_up) + dot(rest, pair_up)).reshape(ring, 8, PLANES)

    def to_ring(source, target, index):
        def one(offset, cross, slot):
            p = ring_at(offset, cross)
            remote(source(p), target.at[slot], g_send.at[index], g_recv.at[index], (q * ring + p, gy))

        def body(i, carry):
            for cross in range(2):
                one(away(i, chips), cross, 2 * i + cross)
            return carry

        lax.fori_loop(0, chips - 1, body, 0)
        one(0, 1, ring - 2)

    to_ring(lambda p: totals.at[p], rs_buf, 0)

    def all_of(ref, count, sem):
        pltpu.make_async_copy(ref.at[pl.ds(0, count)], ref.at[pl.ds(0, count)], sem).wait()

    tally = jnp.zeros((8, n_gx), F32)
    for j in range(8):
        hits = (owner_v[...] == r * 8 + j).astype(F32)
        tally = jnp.where(iota((8, n_gx), 0) == j, jnp.sum(hits, axis=0, keepdims=True), tally)
    count = dot(tally.astype(B16), jnp.ones((n_gx, PLANES), B16))
    count_v[...] = 1.0 / jnp.maximum(count, 1.0)

    all_of(rs_buf, ring - 1, g_recv.at[0])
    mine = totals[r]
    for i in range(ring - 1):
        mine = mine + rs_buf[i]
    part[...] = mine

    def swap(i, carry):
        p = (q + away(i, XGROUP)) % XGROUP
        remote(part, ar_buf.at[i], g_send.at[1], g_recv.at[1], (p * ring + r, gy))
        return carry

    lax.fori_loop(0, XGROUP - 1, swap, 0)
    sides = [
        remote(new.at[:, 1, inner], new.at[:, XROWS + 1, inner], n_send.at[0], n_recv.at[0], (left, gy)),
        remote(new.at[:, XROWS, inner], new.at[:, 0, inner], n_send.at[1], n_recv.at[1], (right, gy)),
    ]
    all_of(ar_buf, XGROUP - 1, g_recv.at[1])
    for i in range(XGROUP - 1):
        mine = mine + ar_buf[i]
    mean = mine * count_v[...]

    hp = PLANES // 2
    z = iota((8, PLANES), 1)
    in_c = z < hp
    no_up = (z % hp) == hp - 1
    no_dn = (z % hp) == 0
    gap_pot = jnp.where(in_c, -2.0 * coarse_flux, 1.0 + 2.0 * coarse_bend)
    value = jnp.zeros((8, PLANES), F32)
    for step in range(CSWEEP):
        gap = mean
        if step:
            around = jnp.where(no_up, 0.0, pltpu.roll(value, PLANES - 1, 1)) + jnp.where(no_dn, 0.0, pltpu.roll(value, 1, 1))
            bend = 2.0 * value - around
            cross = jnp.where(in_c, value + coarse_bend * bend, coarse_flux * bend)
            moved = pltpu.roll(cross, hp, 1)
            gap = mean - value + jnp.where(in_c, -moved, moved)
        value = value + (relax_coarse / coarse_det) * (gap + gap_pot * pltpu.roll(gap, hp, 1))
    sol[ring - 1] = value
    to_ring(lambda p: sol.at[ring - 1], sol, 2)

    k = iota((2 * PLANES, 2 * PLANES), 0) % PLANES
    n = iota((2 * PLANES, 2 * PLANES), 1)
    widen = (k == (n // PLANES) * hp + (n % PLANES) // 2).astype(F32).astype(B16)

    all_of(sol, ring - 1, g_recv.at[2])
    solved = sol[...].reshape(n_gx, PLANES)
    both = jnp.concatenate(halves(solved), axis=1)

    edge = dot(edge_pick[...], both)
    edge = edge[:, :PLANES] + edge[:, PLANES:]
    y_out[...] = edge.reshape(2, 8, PLANES)
    ends = [
        remote(y_out.at[0], y_in.at[1], y_send.at[0], y_recv.at[0], (gx, below)),
        remote(y_out.at[1], y_in.at[0], y_send.at[1], y_recv.at[1], (gx, above)),
    ]
    corr[...] = dot(dot(pick[...], both).astype(B16), widen)

    for copy in sides:
        copy.wait()

    @pl.when(gx == 0)
    def _():
        for f in range(2):
            new[f, 0, inner, :] = jnp.zeros((YCELLS, PLANES), F32)

    @pl.when(gx == n_gx - 1)
    def _():
        for f in range(2):
            new[f, XROWS + 1, inner, :] = jnp.zeros((YCELLS, PLANES), F32)

    for x in range(XROWS + 2):
        block = (x + 1) // 2
        at = pl.ds(block * YCELLS, YCELLS)
        for f in range(2):
            new[f, x, inner, :] = new[f, x, inner, :] + corr[at, f * PLANES : (f + 1) * PLANES]

    def finish(j, carry):
        base = pl.multiple_of(PAD + 8 * j, 8)
        mid = pl.ds(base, 8)
        to = pl.ds(pl.multiple_of(8 * j, 8), 8)
        low, high = edge_masks(8)
        cc = {x: new[0, x, mid, :] for x in range(XROWS + 2)}
        uu = {x: new[1, x, mid, :] for x in range(XROWS + 2)}
        for x in range(1, XROWS + 1):
            around = cc[x + 1] + cc[x - 1] + new[0, x, pl.ds(base + 1, 8), :] + new[0, x, pl.ds(base - 1, 8), :]
            around = around + z_sum(cc[x], low, high)
            excess_mass = mass_excess(x, base, 8, cc, uu)
            excess_pot = src[1, x - 1, mid, :] - uu[x] + 4.0 * cc[x] - 0.5 * around
            step, diagonal = w_a[x - 1, mid, :], w_d[x - 1, mid, :]
            conc_o[x - 1, to, :] = cc[x] + step * (excess_mass - diagonal * excess_pot)
            pot_o[x - 1, to, :] = uu[x] + step * (excess_pot + 4.0 * excess_mass)
        return carry

    lax.fori_loop(0, YCELLS // 8, finish, 0)

    for copy in ends:
        copy.wait()
    y_fine = dot(jnp.concatenate(halves(y_in[...].reshape(16, PLANES)), axis=1), widen)
    inside = (jnp.where(gy == 0, 0.0, 1.0), jnp.where(gy == n_gy - 1, 0.0, 1.0))
    for side in range(2):
        row, out_row = (first, 0) if side == 0 else (last - 1, YCELLS - 1)
        for x in range(XROWS):
            at = side * 8 + x // 2
            add_conc = y_fine[at : at + 1, :PLANES] * inside[side]
            add_pot = y_fine[at : at + 1, PLANES:] * inside[side]
            step = w_a[x, row : row + 1, :]
            mass = w_y[side, x, row : row + 1, :] * add_pot
            pot = -0.5 * add_conc
            spot = slice(out_row, out_row + 1)
            conc_o[x, spot, :] = conc_o[x, spot, :] + step * (mass - w_d[x, row : row + 1, :] * pot)
            pot_o[x, spot, :] = pot_o[x, spot, :] + step * (pot + 4.0 * mass)

    for copy in ex:
        copy.wait_send()
    all_of(rs_buf, ring - 1, g_send.at[0])
    all_of(ar_buf, XGROUP - 1, g_send.at[1])
    all_of(rs_buf, ring - 1, g_send.at[2])


def hand_out(conc_v, pot_v, conc_o, pot_o, sem):
    copies = [
        pltpu.make_async_copy(conc_v, conc_o, sem.at[0]),
        pltpu.make_async_copy(pot_v, pot_o, sem.at[1]),
    ]
    for copy in copies:
        copy.start()
    for copy in copies:
        copy.wait()


def solution(mesh):
    n_gx, n_gy = mesh.shape["gx"], mesh.shape["gy"]
    ring = n_gx // XGROUP
    any_spec = pl.BlockSpec(memory_space=pl.ANY)
    y_pad = YCELLS + 2 * PAD
    k_all = 2 * XROWS // 2 * YCELLS

    def on_device(conc, pot, mass, psrc, mask, classes, table, owner):
        out = jax.ShapeDtypeStruct(conc.shape, F32)
        held = pl.pallas_call(
            functools.partial(kernel, n_gx, n_gy),
            out_shape=(out, out),
            in_specs=[any_spec] * 8,
            out_specs=(pl.BlockSpec(memory_space=pltpu.VMEM),) * 2,
            scratch_shapes=[
                pltpu.VMEM((3, XROWS + 2, y_pad, PLANES), F32),
                pltpu.VMEM((2, XROWS, y_pad, PLANES), F32),
                pltpu.VMEM((XROWS, YCELLS, PLANES), jnp.int32),
                pltpu.VMEM((XROWS, YCELLS, PLANES), jnp.int32),
                pltpu.VMEM((owner.shape[1], owner.shape[0]), jnp.int32),
                pltpu.SMEM((NCLASS,), F32),
                pltpu.VMEM((XROWS + 1, y_pad, PLANES), F32),
                pltpu.VMEM((2, XROWS, y_pad, PLANES), F32),
                pltpu.VMEM((XROWS, y_pad, PLANES), F32),
                pltpu.VMEM((XROWS, y_pad, PLANES), F32),
                pltpu.VMEM((XROWS, y_pad, PLANES), F32),
                pltpu.VMEM((2, XROWS + 2, y_pad, PLANES), F32),
                pltpu.VMEM((k_all, 2 * PLANES), B16),
                pltpu.VMEM((k_all, 2 * PLANES), B16),
                pltpu.VMEM((n_gx, k_all), B16),
                pltpu.VMEM((k_all, n_gx), B16),
                pltpu.VMEM((16, n_gx), B16),
                pltpu.VMEM((8, PLANES), F32),
                pltpu.VMEM((ring, 8, PLANES), F32),
                pltpu.VMEM((ring - 1, 8, PLANES), F32),
                pltpu.VMEM((8, PLANES), F32),
                pltpu.VMEM((XGROUP - 1, 8, PLANES), F32),
                pltpu.VMEM((ring, 8, PLANES), F32),
                pltpu.VMEM((2, 8, PLANES), F32),
                pltpu.VMEM((2, 8, PLANES), F32),
                pltpu.VMEM((k_all, 2 * PLANES), F32),
                pltpu.SemaphoreType.DMA((8,)),
                pltpu.SemaphoreType.DMA((10,)),
                pltpu.SemaphoreType.DMA((10,)),
                pltpu.SemaphoreType.DMA((2,)),
                pltpu.SemaphoreType.DMA((2,)),
                pltpu.SemaphoreType.DMA((3,)),
                pltpu.SemaphoreType.DMA((3,)),
                pltpu.SemaphoreType.DMA((2,)),
                pltpu.SemaphoreType.DMA((2,)),
            ],
            compiler_params=pltpu.CompilerParams(collective_id=0, has_side_effects=True, vmem_limit_bytes=24 << 20),
        )(*(pltpu.with_memory_space_constraint(a, pltpu.HBM) for a in (conc, pot, mass, psrc, mask, classes, table, owner.T)))
        return pl.pallas_call(
            hand_out,
            out_shape=(out, out),
            in_specs=[pl.BlockSpec(memory_space=pltpu.VMEM)] * 2,
            out_specs=(any_spec, any_spec),
            scratch_shapes=[pltpu.SemaphoreType.DMA((2,))],
            compiler_params=pltpu.CompilerParams(vmem_limit_bytes=1 << 20),
        )(*held)

    field = P("gx", "gy", None)
    return jax.shard_map(
        on_device,
        mesh=mesh,
        in_specs=(field,) * 6 + (P(), P(None, "gy")),
        out_specs=(field, field),
        check_vma=False,
    )
```

```python
import functools

import jax
import jax.numpy as jnp
from jax import lax
from jax.experimental import pallas as pl
from jax.experimental.pallas import tpu as pltpu
from jax.sharding import PartitionSpec as P

NCLASS = 8
CSWEEP = 3
XROWS = 4
YCELLS = 64
PLANES = 128
PAD = 8
XGROUP = 8

relax_fine = 0.6
relax_coarse = 0.6
coarse_flux = 0.0625
coarse_bend = 0.125
coarse_det = 1.15625

F32 = jnp.float32
B16 = jnp.bfloat16
MESH = pl.DeviceIdType.MESH


def iota(shape, dim):
    return lax.broadcasted_iota(jnp.int32, shape, dim)


def halves(values):
    high = values.astype(B16)
    return high, (values - high.astype(F32)).astype(B16)


def dot(a, b):
    return jnp.dot(a, b, preferred_element_type=F32)


def dot_t(a, b):
    return lax.dot_general(a, b, (((1,), (1,)), ((), ())), preferred_element_type=F32)


def kernel(
    n_gx, n_gy,
    conc_h, pot_h, mass_h, psrc_h, mask_h, class_h, table_h, owner_h,
    conc_o, pot_o,
    fld, src, mask_v, class_v, owner_v, table,
    w_x, w_y, w_z, w_d, w_a, new,
    r_hi, r_mid, place, pick, edge_pick, count_v,
    totals, mate_buf, mixed, rs_buf, part, ar_buf, sol, y_out, y_in, corr,
    load_sem, ex_send, ex_recv, n_send, n_recv, g_send, g_recv, y_send, y_recv,
):
    ring = n_gx // XGROUP
    gx = lax.axis_index("gx")
    gy = lax.axis_index("gy")
    r = gx % ring
    q = gx // ring
    left, right = (gx + n_gx - 1) % n_gx, (gx + 1) % n_gx
    below, above = (gy + n_gy - 1) % n_gy, (gy + 1) % n_gy
    first, last = PAD, PAD + YCELLS

    chips = ring // 2
    y_chip, core = r // 2, r % 2

    def away(i, count):
        return count // 2 + ((i + 1) // 2) * (1 - 2 * (i % 2))

    def ring_at(offset):
        return ((y_chip + offset) % chips) * 2 + core

    barrier = pltpu.get_barrier_semaphore()

    def greet(a, b):
        pl.semaphore_signal(barrier, inc=1, device_id=(a, b), device_id_type=MESH)

    def greet_far(i, carry):
        greet(((q + away(i, XGROUP)) % XGROUP) * ring + r, gy)
        if chips == XGROUP:
            greet(q * ring + ring_at(away(i, chips)), gy)
        return carry

    def greet_ring(i, carry):
        greet(q * ring + ring_at(away(i, chips)), gy)
        return carry

    lax.fori_loop(0, XGROUP - 1, greet_far, 0)
    if chips != XGROUP:
        lax.fori_loop(0, chips - 1, greet_ring, 0)
    for a in (left, right):
        for b in (below, above):
            greet(a, b)
        greet(a, gy)
    for b in (below, above):
        greet(gx, b)

    def load(source, target, index):
        copy = pltpu.make_async_copy(source, target, load_sem.at[index])
        copy.start()
        return copy

    inner = pl.ds(PAD, YCELLS)
    l_table = load(table_h, table, 7)
    l_class = load(class_h, class_v, 1)
    l_mask = load(mask_h, mask_v, 0)
    l_conc = load(conc_h, fld.at[0, pl.ds(1, XROWS), inner, :], 2)
    l_pot = load(pot_h, fld.at[1, pl.ds(1, XROWS), inner, :], 3)
    l_mass = load(mass_h, src.at[0, :, inner, :], 4)
    l_psrc = load(psrc_h, src.at[1, :, inner, :], 5)
    l_owner = load(owner_h, owner_v, 6)

    l_table.wait()
    l_mask.wait()
    l_class.wait()
    for x in range(XROWS):
        classes = class_v[x]
        values = jnp.zeros(classes.shape, F32)
        for marker in range(NCLASS):
            values = jnp.where(classes == marker, table[marker], values)
        fld[2, x + 1, inner, :] = mask_v[x].astype(F32) * values
    for copy in (l_conc, l_pot, l_mass, l_psrc, l_owner):
        copy.wait()
    pl.semaphore_wait(barrier, 8 + chips - 1 + XGROUP - 1)

    def remote(source, target, send, recv, device):
        copy = pltpu.make_async_remote_copy(
            src_ref=source, dst_ref=target, send_sem=send, recv_sem=recv, device_id=device, device_id_type=MESH
        )
        copy.start()
        return copy

    head, tail = pl.ds(first, 2), pl.ds(last - 2, 2)
    over, under = pl.ds(last, 2), pl.ds(first - 2, 2)
    head_1, tail_1 = pl.ds(first, 1), pl.ds(last - 1, 1)
    over_1, under_1 = pl.ds(last, 1), pl.ds(first - 1, 1)
    rows = pl.ds(1, XROWS)
    out_row, out_far, out_dev = 1 + (XROWS - 1) * core, (XROWS + 1) * (1 - core), (gx + n_gx + 2 * core - 1) % n_gx
    in_row, in_far, in_dev = XROWS - (XROWS - 1) * core, (XROWS + 1) * core, (gx + n_gx + 1 - 2 * core) % n_gx
    plan = [
        (fld.at[:, 1, head_1], fld.at[:, XROWS + 1, over_1], (left, below)),
        (fld.at[:, 1, tail_1], fld.at[:, XROWS + 1, under_1], (left, above)),
        (fld.at[:, XROWS, head_1], fld.at[:, 0, over_1], (right, below)),
        (fld.at[:, XROWS, tail_1], fld.at[:, 0, under_1], (right, above)),
        (fld.at[:, out_row, inner], fld.at[:, out_far, inner], (out_dev, gy)),
        (fld.at[:, in_row, inner], fld.at[:, in_far, inner], (in_dev, gy)),
        (fld.at[:, rows, head], fld.at[:, rows, over], (gx, below)),
        (fld.at[:, rows, tail], fld.at[:, rows, under], (gx, above)),
        (src.at[:, :, head_1], src.at[:, :, over_1], (gx, below)),
        (src.at[:, :, tail_1], src.at[:, :, under_1], (gx, above)),
    ]
    ex = [remote(a, b, ex_send.at[i], ex_recv.at[i], dev) for i, (a, b, dev) in enumerate(plan)]

    half = XROWS // 2
    lanes = half * YCELLS * 2
    half_y = YCELLS // 2
    n_cols = half * half_y

    def spread(rows_n, base):
        k = iota((rows_n, n_cols), 0) + base
        block = k // YCELLS
        column = jnp.where((block == 0) | (block == 2), half_y, 0) + (k % YCELLS) // 2
        return (iota((rows_n, n_cols), 1) == column).astype(F32).astype(B16)

    which = iota((8, n_gx), 0)
    chosen = jnp.where(which == 0, left, jnp.where(which == 1, gx, right))
    one_hot = (iota((8, n_gx), 1) == chosen).astype(F32).astype(B16)
    three = dot_t(one_hot, owner_v[...].astype(F32).astype(B16))
    own_p, own_m, own_n = three[0:1, :], three[1:2, :], three[2:3, :]
    off_l = jnp.where(gx == 0, 1, 0)
    off_r = jnp.where(gx == n_gx - 1, 1, 0)

    def wide(values, rows_n):
        return jnp.broadcast_to(values, (rows_n, n_cols)).astype(B16)

    all_rows = spread(lanes, 0)
    lane_block = iota((8, lanes), 1) // YCELLS
    row_p = dot_t(wide(own_p, 8), all_rows)
    row_m = dot_t(wide(own_m, 8), all_rows)
    row_n = dot_t(wide(own_n, 8), all_rows)
    lane_own = jnp.where(lane_block == 0, row_p - 1000.0 * off_l.astype(F32), row_m)
    lane_own = jnp.where(lane_block == 3, row_n - 1000.0 * off_r.astype(F32), lane_own)
    lane_own = lane_own[0:1, :].astype(jnp.int32)
    place[...] = jnp.where(iota((n_gx, lanes), 0) == lane_own, 0.125, 0.0).astype(B16)

    lane = iota((8, n_gx), 1)
    at = (lane // 8) % chips
    origin = jnp.where(at == chips - 1, r, 0)
    for k in range(chips - 1):
        origin = jnp.where(at == k, ring_at(chips - away(k, chips)), origin)
    origin = jnp.where(lane // 8 >= chips, origin + 1 - 2 * core, origin)
    lane_agg = (origin * 8 + lane % 8)[0:1, :].astype(F32)

    def picks(rows_n, base, values, off):
        column = dot_t(spread(rows_n, base), wide(values, n_gx)) - 1000.0 * off
        return (column == lane_agg).astype(F32).astype(B16)

    pick[0:YCELLS, :] = picks(YCELLS, 0, own_p, off_l.astype(F32))
    pick[YCELLS : 3 * YCELLS, :] = picks(2 * YCELLS, YCELLS, own_m, 0.0)
    pick[3 * YCELLS :, :] = picks(YCELLS, 3 * YCELLS, own_n, off_r.astype(F32))
    e_row = iota((16, n_cols), 0)
    e_col = jnp.where(e_row % 8 == 1, half_y, 0) + jnp.where(e_row >= 8, half_y - 1, 0)
    e_sel = (iota((16, n_cols), 1) == e_col).astype(F32).astype(B16)
    edge_pick[...] = (dot_t(e_sel, wide(own_m, n_gx)) == lane_agg).astype(F32).astype(B16)

    def edge_masks(rows_n):
        z = iota((rows_n, PLANES), 1)
        return z == 0, z == PLANES - 1

    def z_sum(value, low, high):
        return jnp.where(high, 0.0, pltpu.roll(value, PLANES - 1, 1)) + jnp.where(low, 0.0, pltpu.roll(value, 1, 1))

    def settle(x, mid, c, u, diagonal, mass_part, pot_part):
        step = relax_fine / (1.0 + 4.0 * diagonal)
        w_d[x - 1, mid, :] = diagonal
        w_a[x - 1, mid, :] = step
        excess_mass = mass_part - diagonal * u
        new[0, x, mid, :] = c + step * (excess_mass - diagonal * pot_part)
        new[1, x, mid, :] = u + step * (pot_part + 4.0 * excess_mass)

    def sweep(base, with_sides):
        mid, up, dn = pl.ds(base, 8), pl.ds(base + 1, 8), pl.ds(base - 1, 8)
        low, high = edge_masks(8)
        need = range(XROWS + 2) if with_sides else range(1, XROWS + 1)
        mob = {x: fld[2, x, mid, :] for x in need}
        cc = {x: fld[0, x, mid, :] for x in need}
        uu = {x: fld[1, x, mid, :] for x in need}
        face_x = {x: 0.125 * (mob[x] + mob[x + 1]) for x in need if x + 1 in mob}
        for x, face in face_x.items():
            w_x[x, mid, :] = face
        for x in range(1, XROWS + 1):
            m, c, u = mob[x], cc[x], uu[x]
            y_up = 0.125 * (m + fld[2, x, up, :])
            y_dn = 0.125 * (m + fld[2, x, dn, :])
            z_up = 0.125 * (m + jnp.where(high, 0.0, pltpu.roll(m, PLANES - 1, 1)))
            z_dn = jnp.where(low, 0.125 * m, pltpu.roll(z_up, 1, 1))
            z_w = jnp.where(high, 0.0, z_up)
            w_y[0, x - 1, mid, :] = y_dn
            w_y[1, x - 1, mid, :] = y_up
            w_z[x - 1, mid, :] = z_w
            diagonal = (y_up + y_dn) + (z_up + z_dn)
            flow = y_up * fld[1, x, up, :] + y_dn * fld[1, x, dn, :]
            flow = flow + (z_w * pltpu.roll(u, PLANES - 1, 1) + pltpu.roll(z_w * u, 1, 1))
            around = (fld[0, x, up, :] + fld[0, x, dn, :]) + z_sum(c, low, high)
            for face, other in ((x, x + 1), (x - 1, x - 1)):
                if face in face_x:
                    diagonal = diagonal + face_x[face]
                    flow = flow + face_x[face] * uu[other]
                    around = around + cc[other]
            mass_part = (src[0, x - 1, mid, :] - c) + flow
            pot_part = (src[1, x - 1, mid, :] - u + 4.0 * c) - 0.5 * around
            if x in face_x and x - 1 in face_x:
                settle(x, mid, c, u, diagonal, mass_part, pot_part)
            else:
                w_d[x - 1, mid, :] = diagonal
                new[0, x, mid, :] = mass_part
                new[1, x, mid, :] = pot_part

    def add_sides(base):
        mid = pl.ds(base, 8)
        for x, face, other in ((1, 0, 0), (XROWS, XROWS, XROWS + 1)):
            weight = 0.125 * (fld[2, x, mid, :] + fld[2, other, mid, :])
            w_x[face, mid, :] = weight
            diagonal = w_d[x - 1, mid, :] + weight
            mass_part = new[0, x, mid, :] + weight * fld[1, other, mid, :]
            pot_part = new[1, x, mid, :] - 0.5 * fld[0, other, mid, :]
            settle(x, mid, fld[0, x, mid, :], fld[1, x, mid, :], diagonal, mass_part, pot_part)

    def over_rows(count, base, stride, do):
        def body(j, carry):
            do(base + stride * j)
            return carry

        lax.fori_loop(0, count, body, 0)

    n_mid = (YCELLS - 8) // 8
    over_rows(n_mid, first + 1, 8, lambda base: sweep(base, False))

    for copy in ex:
        copy.wait_recv()

    @pl.when(gx == 0)
    def _():
        for f in range(3):
            fld[f, 0] = jnp.zeros((YCELLS + 2 * PAD, PLANES), F32)

    @pl.when(gx == n_gx - 1)
    def _():
        for f in range(3):
            fld[f, XROWS + 1] = jnp.zeros((YCELLS + 2 * PAD, PLANES), F32)

    @pl.when(gy == 0)
    def _():
        for f in range(3):
            for x in range(XROWS + 2):
                fld[f, x, 0:PAD, :] = jnp.zeros((PAD, PLANES), F32)

    @pl.when(gy == n_gy - 1)
    def _():
        for f in range(3):
            for x in range(XROWS + 2):
                fld[f, x, last : last + PAD, :] = jnp.zeros((PAD, PLANES), F32)

    over_rows(n_mid, first + 1, 8, add_sides)
    over_rows(2, 1, YCELLS, lambda base: sweep(base, True))

    @pl.when(gy == 0)
    def _():
        for f in range(2):
            for x in range(1, XROWS + 1):
                new[f, x, 0:PAD, :] = jnp.zeros((PAD, PLANES), F32)

    @pl.when(gy == n_gy - 1)
    def _():
        for f in range(2):
            for x in range(1, XROWS + 1):
                new[f, x, last : last + PAD, :] = jnp.zeros((PAD, PLANES), F32)

    def mass_excess(x, base, rows_n, cc, uu):
        mid, up, dn = pl.ds(base, rows_n), pl.ds(base + 1, rows_n), pl.ds(base - 1, rows_n)
        u, z_w = uu[x], w_z[x - 1, mid, :]
        flow = w_y[1, x - 1, mid, :] * new[1, x, up, :] + w_y[0, x - 1, mid, :] * new[1, x, dn, :]
        flow = flow + (z_w * pltpu.roll(u, PLANES - 1, 1) + pltpu.roll(z_w * u, 1, 1))
        if (x + 1) in uu:
            flow = flow + w_x[x, mid, :] * uu[x + 1]
        if (x - 1) in uu:
            flow = flow + w_x[x - 1, mid, :] * uu[x - 1]
        return (src[0, x - 1, mid, :] - cc[x]) + (flow - w_d[x - 1, mid, :] * u)

    def collect(j, carry):
        base = pl.multiple_of(PAD + 16 * j, 8)
        mid = pl.ds(base, 16)
        low, high = edge_masks(16)
        cc = {x: new[0, x, mid, :] for x in range(1, XROWS + 1)}
        uu = {x: new[1, x, mid, :] for x in range(1, XROWS + 1)}
        mass = {x: mass_excess(x, base, 16, cc, uu) for x in cc}
        up, dn = pl.ds(base + 1, 16), pl.ds(base - 1, 16)
        parts = [(w_x[0, mid, :] * uu[1], -0.5 * cc[1])]
        for a in range(1, XROWS, 2):
            conc = cc[a] + cc[a + 1]
            around = (new[0, a, up, :] + new[0, a + 1, up, :]) + (new[0, a, dn, :] + new[0, a + 1, dn, :])
            around = around + z_sum(conc, low, high)
            for other in (a - 1, a + 2):
                if other in cc:
                    around = around + cc[other]
            psrc = src[1, a - 1, mid, :] + src[1, a, mid, :]
            parts.append((mass[a] + mass[a + 1], psrc - (uu[a] + uu[a + 1]) + 3.5 * conc - 0.5 * around))
        parts.append((w_x[XROWS, mid, :] * uu[XROWS], -0.5 * cc[XROWS]))
        for block, pair in enumerate(parts):
            at = pl.ds(pl.multiple_of(block * YCELLS + 16 * j, 16), 16)
            for f in range(2):
                top, rest = halves(pair[f])
                r_hi[at, f * PLANES : (f + 1) * PLANES] = top
                r_mid[at, f * PLANES : (f + 1) * PLANES] = rest
        return carry

    lax.fori_loop(0, YCELLS // 16, collect, 0)

    fine = dot(place[...], r_hi[...]) + dot(place[...], r_mid[...])
    k = iota((2 * PLANES, PLANES), 0)
    pair_up = (iota((2 * PLANES, PLANES), 1) == (k // PLANES) * (PLANES // 2) + (k % PLANES) // 2).astype(F32).astype(B16)
    top, rest = halves(fine)
    totals[...] = (dot(top, pair_up) + dot(rest, pair_up)).reshape(chips, 2, 8, PLANES)

    def to_ring(source, target, index):
        def body(i, carry):
            p = (y_chip + away(i, chips)) % chips
            remote(source(p), target.at[i], g_send.at[index], g_recv.at[index], (q * ring + p * 2 + core, gy))
            return carry

        lax.fori_loop(0, chips - 1, body, 0)

    def all_of(ref, count, sem):
        if count:
            pltpu.make_async_copy(ref.at[pl.ds(0, count)], ref.at[pl.ds(0, count)], sem).wait()

    mate = (in_dev, gy)
    swap_0 = remote(totals.at[:, 1 - core], mate_buf, g_send.at[0], g_recv.at[0], mate)
    swap_0.wait_recv()
    mixed[...] = totals[:, core] + mate_buf[...]
    to_ring(lambda p: mixed.at[p], rs_buf, 1)

    tally = jnp.zeros((8, n_gx), F32)
    for j in range(8):
        hits = (owner_v[...] == r * 8 + j).astype(F32)
        tally = jnp.where(iota((8, n_gx), 0) == j, jnp.sum(hits, axis=0, keepdims=True), tally)
    count = dot(tally.astype(B16), jnp.ones((n_gx, PLANES), B16))
    count_v[...] = 1.0 / jnp.maximum(count, 1.0)

    all_of(rs_buf, chips - 1, g_recv.at[1])
    mine = mixed[y_chip]
    for i in range(chips - 1):
        mine = mine + rs_buf[i]
    part[...] = mine

    def swap(i, carry):
        p = (q + away(i, XGROUP)) % XGROUP
        remote(part, ar_buf.at[i], g_send.at[2], g_recv.at[2], (p * ring + r, gy))
        return carry

    lax.fori_loop(0, XGROUP - 1, swap, 0)
    sides = [
        remote(new.at[:, 1, inner], new.at[:, XROWS + 1, inner], n_send.at[0], n_recv.at[0], (left, gy)),
        remote(new.at[:, XROWS, inner], new.at[:, 0, inner], n_send.at[1], n_recv.at[1], (right, gy)),
    ]
    all_of(ar_buf, XGROUP - 1, g_recv.at[2])
    for i in range(XGROUP - 1):
        mine = mine + ar_buf[i]
    mean = mine * count_v[...]

    hp = PLANES // 2
    z = iota((8, PLANES), 1)
    in_c = z < hp
    no_up = (z % hp) == hp - 1
    no_dn = (z % hp) == 0
    gap_pot = jnp.where(in_c, -2.0 * coarse_flux, 1.0 + 2.0 * coarse_bend)
    value = jnp.zeros((8, PLANES), F32)
    for step in range(CSWEEP):
        gap = mean
        if step:
            around = jnp.where(no_up, 0.0, pltpu.roll(value, PLANES - 1, 1)) + jnp.where(no_dn, 0.0, pltpu.roll(value, 1, 1))
            bend = 2.0 * value - around
            cross = jnp.where(in_c, value + coarse_bend * bend, coarse_flux * bend)
            moved = pltpu.roll(cross, hp, 1)
            gap = mean - value + jnp.where(in_c, -moved, moved)
        value = value + (relax_coarse / coarse_det) * (gap + gap_pot * pltpu.roll(gap, hp, 1))
    sol[0, chips - 1] = value
    to_ring(lambda p: sol.at[0, chips - 1], sol.at[0], 3)

    k = iota((2 * PLANES, 2 * PLANES), 0) % PLANES
    n = iota((2 * PLANES, 2 * PLANES), 1)
    widen = (k == (n // PLANES) * hp + (n % PLANES) // 2).astype(F32).astype(B16)

    all_of(sol.at[0], chips - 1, g_recv.at[3])
    swap_1 = remote(sol.at[0], sol.at[1], g_send.at[4], g_recv.at[4], mate)
    swap_1.wait_recv()
    solved = sol[...].reshape(n_gx, PLANES)
    both = jnp.concatenate(halves(solved), axis=1)

    edge = dot(edge_pick[...], both)
    edge = edge[:, :PLANES] + edge[:, PLANES:]
    y_out[...] = edge.reshape(2, 8, PLANES)
    ends = [
        remote(y_out.at[0], y_in.at[1], y_send.at[0], y_recv.at[0], (gx, below)),
        remote(y_out.at[1], y_in.at[0], y_send.at[1], y_recv.at[1], (gx, above)),
    ]
    corr[...] = dot(dot(pick[...], both).astype(B16), widen)

    for copy in sides:
        copy.wait()

    @pl.when(gx == 0)
    def _():
        for f in range(2):
            new[f, 0, inner, :] = jnp.zeros((YCELLS, PLANES), F32)

    @pl.when(gx == n_gx - 1)
    def _():
        for f in range(2):
            new[f, XROWS + 1, inner, :] = jnp.zeros((YCELLS, PLANES), F32)

    for x in range(XROWS + 2):
        block = (x + 1) // 2
        at = pl.ds(block * YCELLS, YCELLS)
        for f in range(2):
            new[f, x, inner, :] = new[f, x, inner, :] + corr[at, f * PLANES : (f + 1) * PLANES]

    def finish(j, carry):
        base = pl.multiple_of(PAD + 8 * j, 8)
        mid = pl.ds(base, 8)
        to = pl.ds(pl.multiple_of(8 * j, 8), 8)
        low, high = edge_masks(8)
        cc = {x: new[0, x, mid, :] for x in range(XROWS + 2)}
        uu = {x: new[1, x, mid, :] for x in range(XROWS + 2)}
        for x in range(1, XROWS + 1):
            around = cc[x + 1] + cc[x - 1] + new[0, x, pl.ds(base + 1, 8), :] + new[0, x, pl.ds(base - 1, 8), :]
            around = around + z_sum(cc[x], low, high)
            excess_mass = mass_excess(x, base, 8, cc, uu)
            excess_pot = src[1, x - 1, mid, :] - uu[x] + 4.0 * cc[x] - 0.5 * around
            step, diagonal = w_a[x - 1, mid, :], w_d[x - 1, mid, :]
            conc_o[x - 1, to, :] = cc[x] + step * (excess_mass - diagonal * excess_pot)
            pot_o[x - 1, to, :] = uu[x] + step * (excess_pot + 4.0 * excess_mass)
        return carry

    lax.fori_loop(0, YCELLS // 8, finish, 0)

    for copy in ends:
        copy.wait()
    y_fine = dot(jnp.concatenate(halves(y_in[...].reshape(16, PLANES)), axis=1), widen)
    inside = (jnp.where(gy == 0, 0.0, 1.0), jnp.where(gy == n_gy - 1, 0.0, 1.0))
    for side in range(2):
        row, out_row = (first, 0) if side == 0 else (last - 1, YCELLS - 1)
        for x in range(XROWS):
            at = side * 8 + x // 2
            add_conc = y_fine[at : at + 1, :PLANES] * inside[side]
            add_pot = y_fine[at : at + 1, PLANES:] * inside[side]
            step = w_a[x, row : row + 1, :]
            mass = w_y[side, x, row : row + 1, :] * add_pot
            pot = -0.5 * add_conc
            spot = slice(out_row, out_row + 1)
            conc_o[x, spot, :] = conc_o[x, spot, :] + step * (mass - w_d[x, row : row + 1, :] * pot)
            pot_o[x, spot, :] = pot_o[x, spot, :] + step * (pot + 4.0 * mass)

    for copy in ex:
        copy.wait_send()
    swap_0.wait_send()
    all_of(rs_buf, chips - 1, g_send.at[1])
    all_of(ar_buf, XGROUP - 1, g_send.at[2])
    all_of(rs_buf, chips - 1, g_send.at[3])
    swap_1.wait_send()


def hand_out(conc_v, pot_v, conc_o, pot_o, sem):
    copies = [
        pltpu.make_async_copy(conc_v, conc_o, sem.at[0]),
        pltpu.make_async_copy(pot_v, pot_o, sem.at[1]),
    ]
    for copy in copies:
        copy.start()
    for copy in copies:
        copy.wait()


def solution(mesh):
    n_gx, n_gy = mesh.shape["gx"], mesh.shape["gy"]
    ring = n_gx // XGROUP
    any_spec = pl.BlockSpec(memory_space=pl.ANY)
    y_pad = YCELLS + 2 * PAD
    k_all = 2 * XROWS // 2 * YCELLS

    def on_device(conc, pot, mass, psrc, mask, classes, table, owner):
        out = jax.ShapeDtypeStruct(conc.shape, F32)
        held = pl.pallas_call(
            functools.partial(kernel, n_gx, n_gy),
            out_shape=(out, out),
            in_specs=[any_spec] * 8,
            out_specs=(pl.BlockSpec(memory_space=pltpu.VMEM),) * 2,
            scratch_shapes=[
                pltpu.VMEM((3, XROWS + 2, y_pad, PLANES), F32),
                pltpu.VMEM((2, XROWS, y_pad, PLANES), F32),
                pltpu.VMEM((XROWS, YCELLS, PLANES), jnp.int32),
                pltpu.VMEM((XROWS, YCELLS, PLANES), jnp.int32),
                pltpu.VMEM((owner.shape[1], owner.shape[0]), jnp.int32),
                pltpu.SMEM((NCLASS,), F32),
                pltpu.VMEM((XROWS + 1, y_pad, PLANES), F32),
                pltpu.VMEM((2, XROWS, y_pad, PLANES), F32),
                pltpu.VMEM((XROWS, y_pad, PLANES), F32),
                pltpu.VMEM((XROWS, y_pad, PLANES), F32),
                pltpu.VMEM((XROWS, y_pad, PLANES), F32),
                pltpu.VMEM((2, XROWS + 2, y_pad, PLANES), F32),
                pltpu.VMEM((k_all, 2 * PLANES), B16),
                pltpu.VMEM((k_all, 2 * PLANES), B16),
                pltpu.VMEM((n_gx, k_all), B16),
                pltpu.VMEM((k_all, n_gx), B16),
                pltpu.VMEM((16, n_gx), B16),
                pltpu.VMEM((8, PLANES), F32),
                pltpu.VMEM((ring // 2, 2, 8, PLANES), F32),
                pltpu.VMEM((ring // 2, 8, PLANES), F32),
                pltpu.VMEM((ring // 2, 8, PLANES), F32),
                pltpu.VMEM((max(ring // 2 - 1, 1), 8, PLANES), F32),
                pltpu.VMEM((8, PLANES), F32),
                pltpu.VMEM((XGROUP - 1, 8, PLANES), F32),
                pltpu.VMEM((2, ring // 2, 8, PLANES), F32),
                pltpu.VMEM((2, 8, PLANES), F32),
                pltpu.VMEM((2, 8, PLANES), F32),
                pltpu.VMEM((k_all, 2 * PLANES), F32),
                pltpu.SemaphoreType.DMA((8,)),
                pltpu.SemaphoreType.DMA((10,)),
                pltpu.SemaphoreType.DMA((10,)),
                pltpu.SemaphoreType.DMA((2,)),
                pltpu.SemaphoreType.DMA((2,)),
                pltpu.SemaphoreType.DMA((5,)),
                pltpu.SemaphoreType.DMA((5,)),
                pltpu.SemaphoreType.DMA((2,)),
                pltpu.SemaphoreType.DMA((2,)),
            ],
            compiler_params=pltpu.CompilerParams(collective_id=0, has_side_effects=True, vmem_limit_bytes=24 << 20),
        )(*(pltpu.with_memory_space_constraint(a, pltpu.HBM) for a in (conc, pot, mass, psrc, mask, classes, table, owner.T)))
        return pl.pallas_call(
            hand_out,
            out_shape=(out, out),
            in_specs=[pl.BlockSpec(memory_space=pltpu.VMEM)] * 2,
            out_specs=(any_spec, any_spec),
            scratch_shapes=[pltpu.SemaphoreType.DMA((2,))],
            compiler_params=pltpu.CompilerParams(vmem_limit_bytes=1 << 20),
        )(*held)

    field = P("gx", "gy", None)
    return jax.shard_map(
        on_device,
        mesh=mesh,
        in_specs=(field,) * 6 + (P(), P(None, "gy")),
        out_specs=(field, field),
        check_vma=False,
    )
```

```python
import functools

import jax
import jax.numpy as jnp
from jax import lax
from jax.experimental import pallas as pl
from jax.experimental.pallas import tpu as pltpu
from jax.sharding import PartitionSpec as P

NCLASS = 8
CSWEEP = 3
XROWS = 4
YCELLS = 64
PLANES = 128
PAD = 8
XGROUP = 8

relax_fine = 0.6
relax_coarse = 0.6
coarse_flux = 0.0625
coarse_bend = 0.125
coarse_det = 1.15625

F32 = jnp.float32
B16 = jnp.bfloat16
MESH = pl.DeviceIdType.MESH


def iota(shape, dim):
    return lax.broadcasted_iota(jnp.int32, shape, dim)


def halves(values):
    high = values.astype(B16)
    return high, (values - high.astype(F32)).astype(B16)


def dot(a, b):
    return jnp.dot(a, b, preferred_element_type=F32)


def dot_t(a, b):
    return lax.dot_general(a, b, (((1,), (1,)), ((), ())), preferred_element_type=F32)


def kernel(
    n_gx, n_gy,
    conc_h, pot_h, mass_h, psrc_h, mask_h, class_h, table_h, owner_h,
    conc_o, pot_o,
    fld, src, mask_v, class_v, owner_v, table,
    w_x, w_y, w_z, w_d, w_a, new,
    r_hi, r_mid, place, pick, edge_pick, count_v,
    totals, rs_buf, part, ar_buf, sol, y_out, y_in, corr,
    load_sem, ex_send, ex_recv, n_send, n_recv, g_send, g_recv, y_send, y_recv, relay,
):
    ring = n_gx // XGROUP
    gx = lax.axis_index("gx")
    gy = lax.axis_index("gy")
    r = gx % ring
    q = gx // ring
    left, right = (gx + n_gx - 1) % n_gx, (gx + 1) % n_gx
    below, above = (gy + n_gy - 1) % n_gy, (gy + 1) % n_gy
    first, last = PAD, PAD + YCELLS

    chips = ring // 2
    y_chip, core = r // 2, r % 2

    def away(i, count):
        return count // 2 + ((i + 1) // 2) * (1 - 2 * (i % 2))

    def ring_at(offset, cross):
        return ((y_chip + offset) % chips) * 2 + (1 - core if cross else core)

    barrier = pltpu.get_barrier_semaphore()

    def greet(a, b):
        pl.semaphore_signal(barrier, inc=1, device_id=(a, b), device_id_type=MESH)

    def near(count):
        return [d for d in (2, count - 2, 1, count - 1) if 0 < d < count] if count > 3 else list(range(1, count))

    group_near, ring_near = near(XGROUP), near(chips)
    for d in group_near[:2]:
        greet(((q + d) % XGROUP) * ring + r, gy)
    for d in ring_near[:2]:
        for cross in range(2):
            greet(q * ring + ring_at(d, cross), gy)
    for a in (left, right):
        for b in (below, above):
            greet(a, b)
    for d in group_near[2:]:
        greet(((q + d) % XGROUP) * ring + r, gy)
    for d in ring_near[2:]:
        for cross in range(2):
            greet(q * ring + ring_at(d, cross), gy)
    for a in (left, right):
        greet(a, gy)
    for b in (below, above):
        greet(gx, b)
    n_greet = 8 + len(group_near) + 2 * len(ring_near)

    def load(source, target, index):
        copy = pltpu.make_async_copy(source, target, load_sem.at[index])
        copy.start()
        return copy

    inner = pl.ds(PAD, YCELLS)
    l_table = load(table_h, table, 7)
    l_class = load(class_h, class_v, 1)
    l_mask = load(mask_h, mask_v, 0)
    l_conc = load(conc_h, fld.at[0, pl.ds(1, XROWS), inner, :], 2)
    l_pot = load(pot_h, fld.at[1, pl.ds(1, XROWS), inner, :], 3)
    l_mass = load(mass_h, src.at[0, :, inner, :], 4)
    l_psrc = load(psrc_h, src.at[1, :, inner, :], 5)
    l_owner = load(owner_h, owner_v, 6)

    l_table.wait()
    l_mask.wait()
    l_class.wait()
    for x in range(XROWS):
        classes = class_v[x]
        values = jnp.zeros(classes.shape, F32)
        for marker in range(NCLASS):
            values = jnp.where(classes == marker, table[marker], values)
        fld[2, x + 1, inner, :] = mask_v[x].astype(F32) * values
    for copy in (l_conc, l_pot, l_mass, l_psrc, l_owner):
        copy.wait()
    pl.semaphore_wait(barrier, n_greet)

    def remote(source, target, send, recv, device):
        copy = pltpu.make_async_remote_copy(
            src_ref=source, dst_ref=target, send_sem=send, recv_sem=recv, device_id=device, device_id_type=MESH
        )
        copy.start()
        return copy

    head, tail = pl.ds(first, 2), pl.ds(last - 2, 2)
    over, under = pl.ds(last, 2), pl.ds(first - 2, 2)
    head_1, tail_1 = pl.ds(first, 1), pl.ds(last - 1, 1)
    over_1, under_1 = pl.ds(last, 1), pl.ds(first - 1, 1)
    rows = pl.ds(1, XROWS)
    plan = [
        (fld.at[:, 1, head_1], fld.at[:, XROWS + 1, over_1], (left, below)),
        (fld.at[:, 1, tail_1], fld.at[:, XROWS + 1, under_1], (left, above)),
        (fld.at[:, XROWS, head_1], fld.at[:, 0, over_1], (right, below)),
        (fld.at[:, XROWS, tail_1], fld.at[:, 0, under_1], (right, above)),
        (fld.at[:, 1, inner], fld.at[:, XROWS + 1, inner], (left, gy)),
        (fld.at[:, XROWS, inner], fld.at[:, 0, inner], (right, gy)),
        (fld.at[:, rows, head], fld.at[:, rows, over], (gx, below)),
        (fld.at[:, rows, tail], fld.at[:, rows, under], (gx, above)),
        (src.at[:, :, head_1], src.at[:, :, over_1], (gx, below)),
        (src.at[:, :, tail_1], src.at[:, :, under_1], (gx, above)),
    ]
    ex = [remote(a, b, ex_send.at[i], ex_recv.at[i], dev) for i, (a, b, dev) in enumerate(plan)]

    ring_relay = chips > 4
    for i, d in enumerate((2, XGROUP - 2)):
        pl.semaphore_signal(relay.at[i], inc=1, device_id=(((q + d) % XGROUP) * ring + r, gy), device_id_type=MESH)
    if ring_relay:
        for i, d in enumerate((2, chips - 2)):
            there = q * ring + ring_at(d, 0)
            pl.semaphore_signal(relay.at[2 + i], inc=1, device_id=(there, gy), device_id_type=MESH)

    half = XROWS // 2
    lanes = half * YCELLS * 2
    half_y = YCELLS // 2
    n_cols = half * half_y

    def spread(rows_n, base):
        k = iota((rows_n, n_cols), 0) + base
        block = k // YCELLS
        column = jnp.where((block == 0) | (block == 2), half_y, 0) + (k % YCELLS) // 2
        return (iota((rows_n, n_cols), 1) == column).astype(F32).astype(B16)

    which = iota((8, n_gx), 0)
    chosen = jnp.where(which == 0, left, jnp.where(which == 1, gx, right))
    one_hot = (iota((8, n_gx), 1) == chosen).astype(F32).astype(B16)
    three = dot_t(one_hot, owner_v[...].astype(F32).astype(B16))
    own_p, own_m, own_n = three[0:1, :], three[1:2, :], three[2:3, :]
    off_l = jnp.where(gx == 0, 1, 0)
    off_r = jnp.where(gx == n_gx - 1, 1, 0)

    def wide(values, rows_n):
        return jnp.broadcast_to(values, (rows_n, n_cols)).astype(B16)

    all_rows = spread(lanes, 0)
    lane_block = iota((8, lanes), 1) // YCELLS
    row_p = dot_t(wide(own_p, 8), all_rows)
    row_m = dot_t(wide(own_m, 8), all_rows)
    row_n = dot_t(wide(own_n, 8), all_rows)
    lane_own = jnp.where(lane_block == 0, row_p - 1000.0 * off_l.astype(F32), row_m)
    lane_own = jnp.where(lane_block == 3, row_n - 1000.0 * off_r.astype(F32), lane_own)
    lane_own = lane_own[0:1, :].astype(jnp.int32)
    place[...] = jnp.where(iota((n_gx, lanes), 0) == lane_own, 0.125, 0.0).astype(B16)

    lane = iota((8, n_gx), 1)
    origin = jnp.where(lane // 8 == ring - 1, r, ring_at(0, 1))
    for k in range(chips - 1):
        for cross in range(2):
            origin = jnp.where(lane // 8 == 2 * k + cross, ring_at(chips - away(k, chips), cross), origin)
    lane_agg = (origin * 8 + lane % 8)[0:1, :].astype(F32)

    def picks(rows_n, base, values, off):
        column = dot_t(spread(rows_n, base), wide(values, n_gx)) - 1000.0 * off
        return (column == lane_agg).astype(F32).astype(B16)

    pick[0:YCELLS, :] = picks(YCELLS, 0, own_p, off_l.astype(F32))
    pick[YCELLS : 3 * YCELLS, :] = picks(2 * YCELLS, YCELLS, own_m, 0.0)
    pick[3 * YCELLS :, :] = picks(YCELLS, 3 * YCELLS, own_n, off_r.astype(F32))
    e_row = iota((16, n_cols), 0)
    e_col = jnp.where(e_row % 8 == 1, half_y, 0) + jnp.where(e_row >= 8, half_y - 1, 0)
    e_sel = (iota((16, n_cols), 1) == e_col).astype(F32).astype(B16)
    edge_pick[...] = (dot_t(e_sel, wide(own_m, n_gx)) == lane_agg).astype(F32).astype(B16)

    def edge_masks(rows_n):
        z = iota((rows_n, PLANES), 1)
        return z == 0, z == PLANES - 1

    def z_sum(value, low, high):
        return jnp.where(high, 0.0, pltpu.roll(value, PLANES - 1, 1)) + jnp.where(low, 0.0, pltpu.roll(value, 1, 1))

    def settle(x, mid, c, u, diagonal, mass_part, pot_part):
        step = relax_fine / (1.0 + 4.0 * diagonal)
        w_d[x - 1, mid, :] = diagonal
        w_a[x - 1, mid, :] = step
        excess_mass = mass_part - diagonal * u
        new[0, x, mid, :] = c + step * (excess_mass - diagonal * pot_part)
        new[1, x, mid, :] = u + step * (pot_part + 4.0 * excess_mass)

    def sweep(base, with_sides):
        mid, up, dn = pl.ds(base, 8), pl.ds(base + 1, 8), pl.ds(base - 1, 8)
        low, high = edge_masks(8)
        need = range(XROWS + 2) if with_sides else range(1, XROWS + 1)
        mob = {x: fld[2, x, mid, :] for x in need}
        cc = {x: fld[0, x, mid, :] for x in need}
        uu = {x: fld[1, x, mid, :] for x in need}
        face_x = {x: 0.125 * (mob[x] + mob[x + 1]) for x in need if x + 1 in mob}
        for x, face in face_x.items():
            w_x[x, mid, :] = face
        for x in range(1, XROWS + 1):
            m, c, u = mob[x], cc[x], uu[x]
            y_up = 0.125 * (m + fld[2, x, up, :])
            y_dn = 0.125 * (m + fld[2, x, dn, :])
            z_up = 0.125 * (m + jnp.where(high, 0.0, pltpu.roll(m, PLANES - 1, 1)))
            z_dn = jnp.where(low, 0.125 * m, pltpu.roll(z_up, 1, 1))
            z_w = jnp.where(high, 0.0, z_up)
            w_y[0, x - 1, mid, :] = y_dn
            w_y[1, x - 1, mid, :] = y_up
            w_z[x - 1, mid, :] = z_w
            diagonal = (y_up + y_dn) + (z_up + z_dn)
            flow = y_up * fld[1, x, up, :] + y_dn * fld[1, x, dn, :]
            flow = flow + (z_w * pltpu.roll(u, PLANES - 1, 1) + pltpu.roll(z_w * u, 1, 1))
            around = (fld[0, x, up, :] + fld[0, x, dn, :]) + z_sum(c, low, high)
            for face, other in ((x, x + 1), (x - 1, x - 1)):
                if face in face_x:
                    diagonal = diagonal + face_x[face]
                    flow = flow + face_x[face] * uu[other]
                    around = around + cc[other]
            mass_part = (src[0, x - 1, mid, :] - c) + flow
            pot_part = (src[1, x - 1, mid, :] - u + 4.0 * c) - 0.5 * around
            if x in face_x and x - 1 in face_x:
                settle(x, mid, c, u, diagonal, mass_part, pot_part)
            else:
                w_d[x - 1, mid, :] = diagonal
                new[0, x, mid, :] = mass_part
                new[1, x, mid, :] = pot_part

    def add_sides(base):
        mid = pl.ds(base, 8)
        for x, face, other in ((1, 0, 0), (XROWS, XROWS, XROWS + 1)):
            weight = 0.125 * (fld[2, x, mid, :] + fld[2, other, mid, :])
            w_x[face, mid, :] = weight
            diagonal = w_d[x - 1, mid, :] + weight
            mass_part = new[0, x, mid, :] + weight * fld[1, other, mid, :]
            pot_part = new[1, x, mid, :] - 0.5 * fld[0, other, mid, :]
            settle(x, mid, fld[0, x, mid, :], fld[1, x, mid, :], diagonal, mass_part, pot_part)

    def over_rows(count, base, stride, do):
        def body(j, carry):
            do(base + stride * j)
            return carry

        lax.fori_loop(0, count, body, 0)

    n_mid = (YCELLS - 8) // 8
    over_rows(n_mid, first + 1, 8, lambda base: sweep(base, False))

    for copy in ex:
        copy.wait_recv()

    @pl.when(gx == 0)
    def _():
        for f in range(3):
            fld[f, 0] = jnp.zeros((YCELLS + 2 * PAD, PLANES), F32)

    @pl.when(gx == n_gx - 1)
    def _():
        for f in range(3):
            fld[f, XROWS + 1] = jnp.zeros((YCELLS + 2 * PAD, PLANES), F32)

    @pl.when(gy == 0)
    def _():
        for f in range(3):
            for x in range(XROWS + 2):
                fld[f, x, 0:PAD, :] = jnp.zeros((PAD, PLANES), F32)

    @pl.when(gy == n_gy - 1)
    def _():
        for f in range(3):
            for x in range(XROWS + 2):
                fld[f, x, last : last + PAD, :] = jnp.zeros((PAD, PLANES), F32)

    over_rows(n_mid, first + 1, 8, add_sides)
    over_rows(2, 1, YCELLS, lambda base: sweep(base, True))

    @pl.when(gy == 0)
    def _():
        for f in range(2):
            for x in range(1, XROWS + 1):
                new[f, x, 0:PAD, :] = jnp.zeros((PAD, PLANES), F32)

    @pl.when(gy == n_gy - 1)
    def _():
        for f in range(2):
            for x in range(1, XROWS + 1):
                new[f, x, last : last + PAD, :] = jnp.zeros((PAD, PLANES), F32)

    def mass_excess(x, base, rows_n, cc, uu):
        mid, up, dn = pl.ds(base, rows_n), pl.ds(base + 1, rows_n), pl.ds(base - 1, rows_n)
        u, z_w = uu[x], w_z[x - 1, mid, :]
        flow = w_y[1, x - 1, mid, :] * new[1, x, up, :] + w_y[0, x - 1, mid, :] * new[1, x, dn, :]
        flow = flow + (z_w * pltpu.roll(u, PLANES - 1, 1) + pltpu.roll(z_w * u, 1, 1))
        if (x + 1) in uu:
            flow = flow + w_x[x, mid, :] * uu[x + 1]
        if (x - 1) in uu:
            flow = flow + w_x[x - 1, mid, :] * uu[x - 1]
        return (src[0, x - 1, mid, :] - cc[x]) + (flow - w_d[x - 1, mid, :] * u)

    def collect(j, carry):
        base = pl.multiple_of(PAD + 16 * j, 8)
        mid = pl.ds(base, 16)
        low, high = edge_masks(16)
        cc = {x: new[0, x, mid, :] for x in range(1, XROWS + 1)}
        uu = {x: new[1, x, mid, :] for x in range(1, XROWS + 1)}
        mass = {x: mass_excess(x, base, 16, cc, uu) for x in cc}
        up, dn = pl.ds(base + 1, 16), pl.ds(base - 1, 16)
        parts = [(w_x[0, mid, :] * uu[1], -0.5 * cc[1])]
        for a in range(1, XROWS, 2):
            conc = cc[a] + cc[a + 1]
            around = (new[0, a, up, :] + new[0, a + 1, up, :]) + (new[0, a, dn, :] + new[0, a + 1, dn, :])
            around = around + z_sum(conc, low, high)
            for other in (a - 1, a + 2):
                if other in cc:
                    around = around + cc[other]
            psrc = src[1, a - 1, mid, :] + src[1, a, mid, :]
            parts.append((mass[a] + mass[a + 1], psrc - (uu[a] + uu[a + 1]) + 3.5 * conc - 0.5 * around))
        parts.append((w_x[XROWS, mid, :] * uu[XROWS], -0.5 * cc[XROWS]))
        for block, pair in enumerate(parts):
            at = pl.ds(pl.multiple_of(block * YCELLS + 16 * j, 16), 16)
            for f in range(2):
                top, rest = halves(pair[f])
                r_hi[at, f * PLANES : (f + 1) * PLANES] = top
                r_mid[at, f * PLANES : (f + 1) * PLANES] = rest
        return carry

    lax.fori_loop(0, YCELLS // 16, collect, 0)

    fine = dot(place[...], r_hi[...]) + dot(place[...], r_mid[...])
    k = iota((2 * PLANES, PLANES), 0)
    pair_up = (iota((2 * PLANES, PLANES), 1) == (k // PLANES) * (PLANES // 2) + (k % PLANES) // 2).astype(F32).astype(B16)
    top, rest = halves(fine)
    totals[...] = (dot(top, pair_up) + dot(rest, pair_up)).reshape(ring, 8, PLANES)

    def to_ring(source, target, index):
        def one(offset, cross, slot):
            p = ring_at(offset, cross)
            remote(source(p), target.at[slot], g_send.at[index], g_recv.at[index], (q * ring + p, gy))

        def body(i, carry):
            for cross in range(2):
                one(away(i, chips), cross, 2 * i + cross)
            return carry

        lax.fori_loop(0, chips - 1, body, 0)
        one(0, 1, ring - 2)

    if ring_relay:
        for i in range(2):
            pl.semaphore_wait(relay.at[2 + i], 1)
    to_ring(lambda p: totals.at[p], rs_buf, 0)

    def all_of(ref, count, sem):
        pltpu.make_async_copy(ref.at[pl.ds(0, count)], ref.at[pl.ds(0, count)], sem).wait()

    tally = jnp.zeros((8, n_gx), F32)
    for j in range(8):
        hits = (owner_v[...] == r * 8 + j).astype(F32)
        tally = jnp.where(iota((8, n_gx), 0) == j, jnp.sum(hits, axis=0, keepdims=True), tally)
    count = dot(tally.astype(B16), jnp.ones((n_gx, PLANES), B16))
    count_v[...] = 1.0 / jnp.maximum(count, 1.0)

    all_of(rs_buf, ring - 1, g_recv.at[0])
    mine = totals[r]
    for i in range(ring - 1):
        mine = mine + rs_buf[i]
    part[...] = mine

    def swap(i, carry):
        p = (q + away(i, XGROUP)) % XGROUP
        remote(part, ar_buf.at[i], g_send.at[1], g_recv.at[1], (p * ring + r, gy))
        return carry

    for i in range(2):
        pl.semaphore_wait(relay.at[i], 1)
    lax.fori_loop(0, XGROUP - 1, swap, 0)
    sides = [
        remote(new.at[:, 1, inner], new.at[:, XROWS + 1, inner], n_send.at[0], n_recv.at[0], (left, gy)),
        remote(new.at[:, XROWS, inner], new.at[:, 0, inner], n_send.at[1], n_recv.at[1], (right, gy)),
    ]
    all_of(ar_buf, XGROUP - 1, g_recv.at[1])
    for i in range(XGROUP - 1):
        mine = mine + ar_buf[i]
    mean = mine * count_v[...]

    hp = PLANES // 2
    z = iota((8, PLANES), 1)
    in_c = z < hp
    no_up = (z % hp) == hp - 1
    no_dn = (z % hp) == 0
    gap_pot = jnp.where(in_c, -2.0 * coarse_flux, 1.0 + 2.0 * coarse_bend)
    value = jnp.zeros((8, PLANES), F32)
    for step in range(CSWEEP):
        gap = mean
        if step:
            around = jnp.where(no_up, 0.0, pltpu.roll(value, PLANES - 1, 1)) + jnp.where(no_dn, 0.0, pltpu.roll(value, 1, 1))
            bend = 2.0 * value - around
            cross = jnp.where(in_c, value + coarse_bend * bend, coarse_flux * bend)
            moved = pltpu.roll(cross, hp, 1)
            gap = mean - value + jnp.where(in_c, -moved, moved)
        value = value + (relax_coarse / coarse_det) * (gap + gap_pot * pltpu.roll(gap, hp, 1))
    sol[ring - 1] = value
    to_ring(lambda p: sol.at[ring - 1], sol, 2)

    k = iota((2 * PLANES, 2 * PLANES), 0) % PLANES
    n = iota((2 * PLANES, 2 * PLANES), 1)
    widen = (k == (n // PLANES) * hp + (n % PLANES) // 2).astype(F32).astype(B16)

    all_of(sol, ring - 1, g_recv.at[2])
    solved = sol[...].reshape(n_gx, PLANES)
    both = jnp.concatenate(halves(solved), axis=1)

    edge = dot(edge_pick[...], both)
    edge = edge[:, :PLANES] + edge[:, PLANES:]
    y_out[...] = edge.reshape(2, 8, PLANES)
    ends = [
        remote(y_out.at[0], y_in.at[1], y_send.at[0], y_recv.at[0], (gx, below)),
        remote(y_out.at[1], y_in.at[0], y_send.at[1], y_recv.at[1], (gx, above)),
    ]
    corr[...] = dot(dot(pick[...], both).astype(B16), widen)

    for copy in sides:
        copy.wait()

    @pl.when(gx == 0)
    def _():
        for f in range(2):
            new[f, 0, inner, :] = jnp.zeros((YCELLS, PLANES), F32)

    @pl.when(gx == n_gx - 1)
    def _():
        for f in range(2):
            new[f, XROWS + 1, inner, :] = jnp.zeros((YCELLS, PLANES), F32)

    for x in range(XROWS + 2):
        block = (x + 1) // 2
        at = pl.ds(block * YCELLS, YCELLS)
        for f in range(2):
            new[f, x, inner, :] = new[f, x, inner, :] + corr[at, f * PLANES : (f + 1) * PLANES]

    def finish(j, carry):
        base = pl.multiple_of(PAD + 8 * j, 8)
        mid = pl.ds(base, 8)
        to = pl.ds(pl.multiple_of(8 * j, 8), 8)
        low, high = edge_masks(8)
        cc = {x: new[0, x, mid, :] for x in range(XROWS + 2)}
        uu = {x: new[1, x, mid, :] for x in range(XROWS + 2)}
        for x in range(1, XROWS + 1):
            around = cc[x + 1] + cc[x - 1] + new[0, x, pl.ds(base + 1, 8), :] + new[0, x, pl.ds(base - 1, 8), :]
            around = around + z_sum(cc[x], low, high)
            excess_mass = mass_excess(x, base, 8, cc, uu)
            excess_pot = src[1, x - 1, mid, :] - uu[x] + 4.0 * cc[x] - 0.5 * around
            step, diagonal = w_a[x - 1, mid, :], w_d[x - 1, mid, :]
            conc_o[x - 1, to, :] = cc[x] + step * (excess_mass - diagonal * excess_pot)
            pot_o[x - 1, to, :] = uu[x] + step * (excess_pot + 4.0 * excess_mass)
        return carry

    lax.fori_loop(0, YCELLS // 8, finish, 0)

    for copy in ends:
        copy.wait()
    y_fine = dot(jnp.concatenate(halves(y_in[...].reshape(16, PLANES)), axis=1), widen)
    inside = (jnp.where(gy == 0, 0.0, 1.0), jnp.where(gy == n_gy - 1, 0.0, 1.0))
    for side in range(2):
        row, out_row = (first, 0) if side == 0 else (last - 1, YCELLS - 1)
        for x in range(XROWS):
            at = side * 8 + x // 2
            add_conc = y_fine[at : at + 1, :PLANES] * inside[side]
            add_pot = y_fine[at : at + 1, PLANES:] * inside[side]
            step = w_a[x, row : row + 1, :]
            mass = w_y[side, x, row : row + 1, :] * add_pot
            pot = -0.5 * add_conc
            spot = slice(out_row, out_row + 1)
            conc_o[x, spot, :] = conc_o[x, spot, :] + step * (mass - w_d[x, row : row + 1, :] * pot)
            pot_o[x, spot, :] = pot_o[x, spot, :] + step * (pot + 4.0 * mass)

    for copy in ex:
        copy.wait_send()
    all_of(rs_buf, ring - 1, g_send.at[0])
    all_of(ar_buf, XGROUP - 1, g_send.at[1])
    all_of(rs_buf, ring - 1, g_send.at[2])


def hand_out(conc_v, pot_v, conc_o, pot_o, sem):
    copies = [
        pltpu.make_async_copy(conc_v, conc_o, sem.at[0]),
        pltpu.make_async_copy(pot_v, pot_o, sem.at[1]),
    ]
    for copy in copies:
        copy.start()
    for copy in copies:
        copy.wait()


def solution(mesh):
    n_gx, n_gy = mesh.shape["gx"], mesh.shape["gy"]
    ring = n_gx // XGROUP
    any_spec = pl.BlockSpec(memory_space=pl.ANY)
    y_pad = YCELLS + 2 * PAD
    k_all = 2 * XROWS // 2 * YCELLS

    def on_device(conc, pot, mass, psrc, mask, classes, table, owner):
        out = jax.ShapeDtypeStruct(conc.shape, F32)
        held = pl.pallas_call(
            functools.partial(kernel, n_gx, n_gy),
            out_shape=(out, out),
            in_specs=[any_spec] * 8,
            out_specs=(pl.BlockSpec(memory_space=pltpu.VMEM),) * 2,
            scratch_shapes=[
                pltpu.VMEM((3, XROWS + 2, y_pad, PLANES), F32),
                pltpu.VMEM((2, XROWS, y_pad, PLANES), F32),
                pltpu.VMEM((XROWS, YCELLS, PLANES), jnp.int32),
                pltpu.VMEM((XROWS, YCELLS, PLANES), jnp.int32),
                pltpu.VMEM((owner.shape[1], owner.shape[0]), jnp.int32),
                pltpu.SMEM((NCLASS,), F32),
                pltpu.VMEM((XROWS + 1, y_pad, PLANES), F32),
                pltpu.VMEM((2, XROWS, y_pad, PLANES), F32),
                pltpu.VMEM((XROWS, y_pad, PLANES), F32),
                pltpu.VMEM((XROWS, y_pad, PLANES), F32),
                pltpu.VMEM((XROWS, y_pad, PLANES), F32),
                pltpu.VMEM((2, XROWS + 2, y_pad, PLANES), F32),
                pltpu.VMEM((k_all, 2 * PLANES), B16),
                pltpu.VMEM((k_all, 2 * PLANES), B16),
                pltpu.VMEM((n_gx, k_all), B16),
                pltpu.VMEM((k_all, n_gx), B16),
                pltpu.VMEM((16, n_gx), B16),
                pltpu.VMEM((8, PLANES), F32),
                pltpu.VMEM((ring, 8, PLANES), F32),
                pltpu.VMEM((ring - 1, 8, PLANES), F32),
                pltpu.VMEM((8, PLANES), F32),
                pltpu.VMEM((XGROUP - 1, 8, PLANES), F32),
                pltpu.VMEM((ring, 8, PLANES), F32),
                pltpu.VMEM((2, 8, PLANES), F32),
                pltpu.VMEM((2, 8, PLANES), F32),
                pltpu.VMEM((k_all, 2 * PLANES), F32),
                pltpu.SemaphoreType.DMA((8,)),
                pltpu.SemaphoreType.DMA((10,)),
                pltpu.SemaphoreType.DMA((10,)),
                pltpu.SemaphoreType.DMA((2,)),
                pltpu.SemaphoreType.DMA((2,)),
                pltpu.SemaphoreType.DMA((3,)),
                pltpu.SemaphoreType.DMA((3,)),
                pltpu.SemaphoreType.DMA((2,)),
                pltpu.SemaphoreType.DMA((2,)),
                pltpu.SemaphoreType.REGULAR((4,)),
            ],
            compiler_params=pltpu.CompilerParams(collective_id=0, has_side_effects=True, vmem_limit_bytes=24 << 20),
        )(*(pltpu.with_memory_space_constraint(a, pltpu.HBM) for a in (conc, pot, mass, psrc, mask, classes, table, owner.T)))
        return pl.pallas_call(
            hand_out,
            out_shape=(out, out),
            in_specs=[pl.BlockSpec(memory_space=pltpu.VMEM)] * 2,
            out_specs=(any_spec, any_spec),
            scratch_shapes=[pltpu.SemaphoreType.DMA((2,))],
            compiler_params=pltpu.CompilerParams(vmem_limit_bytes=1 << 20),
        )(*held)

    field = P("gx", "gy", None)
    return jax.shard_map(
        on_device,
        mesh=mesh,
        in_specs=(field,) * 6 + (P(), P(None, "gy")),
        out_specs=(field, field),
        check_vma=False,
    )
```

```python
import functools

import jax
import jax.numpy as jnp
from jax import lax
from jax.experimental import pallas as pl
from jax.experimental.pallas import tpu as pltpu
from jax.sharding import PartitionSpec as P

NCLASS = 8
CSWEEP = 3
XROWS = 4
YCELLS = 64
PLANES = 128
PAD = 8
XGROUP = 8

relax_fine = 0.6
relax_coarse = 0.6
coarse_flux = 0.0625
coarse_bend = 0.125
coarse_det = 1.15625

F32 = jnp.float32
B16 = jnp.bfloat16
MESH = pl.DeviceIdType.MESH


def iota(shape, dim):
    return lax.broadcasted_iota(jnp.int32, shape, dim)


def halves(values):
    high = values.astype(B16)
    return high, (values - high.astype(F32)).astype(B16)


def dot(a, b):
    return jnp.dot(a, b, preferred_element_type=F32)


def dot_t(a, b):
    return lax.dot_general(a, b, (((1,), (1,)), ((), ())), preferred_element_type=F32)


def kernel(
    n_gx, n_gy,
    conc_h, pot_h, mass_h, psrc_h, mask_h, class_h, table_h, owner_h,
    conc_o, pot_o,
    fld, src, mask_v, class_v, owner_v, table,
    w_x, w_y, w_z, w_d, w_a, new,
    r_hi, r_mid, place, pick, edge_pick, count_v,
    totals, rs_buf, part, ar_buf, sol, y_out, y_in, corr, solve_v,
    load_sem, ex_send, ex_recv, n_send, n_recv, g_send, g_recv, y_send, y_recv, relay,
):
    ring = n_gx // XGROUP
    gx = lax.axis_index("gx")
    gy = lax.axis_index("gy")
    r = gx % ring
    q = gx // ring
    left, right = (gx + n_gx - 1) % n_gx, (gx + 1) % n_gx
    below, above = (gy + n_gy - 1) % n_gy, (gy + 1) % n_gy
    first, last = PAD, PAD + YCELLS

    chips = ring // 2
    y_chip, core = r // 2, r % 2

    def away(i, count):
        return count // 2 + ((i + 1) // 2) * (1 - 2 * (i % 2))

    def ring_at(offset, cross):
        return ((y_chip + offset) % chips) * 2 + (1 - core if cross else core)

    barrier = pltpu.get_barrier_semaphore()

    def greet(a, b):
        pl.semaphore_signal(barrier, inc=1, device_id=(a, b), device_id_type=MESH)

    def near(count):
        return [d for d in (2, count - 2, 1, count - 1) if 0 < d < count] if count > 3 else list(range(1, count))

    group_near, ring_near = near(XGROUP), near(chips)
    for d in group_near[:2]:
        greet(((q + d) % XGROUP) * ring + r, gy)
    for d in ring_near[:2]:
        for cross in range(2):
            greet(q * ring + ring_at(d, cross), gy)
    for a in (left, right):
        for b in (below, above):
            greet(a, b)
    for d in group_near[2:]:
        greet(((q + d) % XGROUP) * ring + r, gy)
    for d in ring_near[2:]:
        for cross in range(2):
            greet(q * ring + ring_at(d, cross), gy)
    for a in (left, right):
        greet(a, gy)
    for b in (below, above):
        greet(gx, b)
    n_greet = 8 + len(group_near) + 2 * len(ring_near)

    def load(source, target, index):
        copy = pltpu.make_async_copy(source, target, load_sem.at[index])
        copy.start()
        return copy

    inner = pl.ds(PAD, YCELLS)
    l_table = load(table_h, table, 7)
    l_class = load(class_h, class_v, 1)
    l_mask = load(mask_h, mask_v, 0)
    l_conc = load(conc_h, fld.at[0, pl.ds(1, XROWS), inner, :], 2)
    l_pot = load(pot_h, fld.at[1, pl.ds(1, XROWS), inner, :], 3)
    l_mass = load(mass_h, src.at[0, :, inner, :], 4)
    l_psrc = load(psrc_h, src.at[1, :, inner, :], 5)
    l_owner = load(owner_h, owner_v, 6)

    l_table.wait()
    l_mask.wait()
    l_class.wait()
    for x in range(XROWS):
        classes = class_v[x]
        values = jnp.zeros(classes.shape, F32)
        for marker in range(NCLASS):
            values = jnp.where(classes == marker, table[marker], values)
        fld[2, x + 1, inner, :] = mask_v[x].astype(F32) * values
    for copy in (l_conc, l_pot, l_mass, l_psrc, l_owner):
        copy.wait()
    pl.semaphore_wait(barrier, n_greet)

    def remote(source, target, send, recv, device):
        copy = pltpu.make_async_remote_copy(
            src_ref=source, dst_ref=target, send_sem=send, recv_sem=recv, device_id=device, device_id_type=MESH
        )
        copy.start()
        return copy

    head, tail = pl.ds(first, 2), pl.ds(last - 2, 2)
    over, under = pl.ds(last, 2), pl.ds(first - 2, 2)
    head_1, tail_1 = pl.ds(first, 1), pl.ds(last - 1, 1)
    over_1, under_1 = pl.ds(last, 1), pl.ds(first - 1, 1)
    rows = pl.ds(1, XROWS)
    plan = [
        (fld.at[:, 1, head_1], fld.at[:, XROWS + 1, over_1], (left, below)),
        (fld.at[:, 1, tail_1], fld.at[:, XROWS + 1, under_1], (left, above)),
        (fld.at[:, XROWS, head_1], fld.at[:, 0, over_1], (right, below)),
        (fld.at[:, XROWS, tail_1], fld.at[:, 0, under_1], (right, above)),
        (fld.at[:, 1, inner], fld.at[:, XROWS + 1, inner], (left, gy)),
        (fld.at[:, XROWS, inner], fld.at[:, 0, inner], (right, gy)),
        (fld.at[:, rows, head], fld.at[:, rows, over], (gx, below)),
        (fld.at[:, rows, tail], fld.at[:, rows, under], (gx, above)),
        (src.at[:, :, head_1], src.at[:, :, over_1], (gx, below)),
        (src.at[:, :, tail_1], src.at[:, :, under_1], (gx, above)),
    ]
    ex = [remote(a, b, ex_send.at[i], ex_recv.at[i], dev) for i, (a, b, dev) in enumerate(plan)]

    ring_relay = chips > 4
    for i, d in enumerate((2, XGROUP - 2)):
        pl.semaphore_signal(relay.at[i], inc=1, device_id=(((q + d) % XGROUP) * ring + r, gy), device_id_type=MESH)
    if ring_relay:
        for i, d in enumerate((2, chips - 2)):
            there = q * ring + ring_at(d, 0)
            pl.semaphore_signal(relay.at[2 + i], inc=1, device_id=(there, gy), device_id_type=MESH)

    half = XROWS // 2
    lanes = half * YCELLS * 2
    half_y = YCELLS // 2
    n_cols = half * half_y

    def spread(rows_n, base):
        k = iota((rows_n, n_cols), 0) + base
        block = k // YCELLS
        column = jnp.where((block == 0) | (block == 2), half_y, 0) + (k % YCELLS) // 2
        return (iota((rows_n, n_cols), 1) == column).astype(F32).astype(B16)

    which = iota((8, n_gx), 0)
    chosen = jnp.where(which == 0, left, jnp.where(which == 1, gx, right))
    one_hot = (iota((8, n_gx), 1) == chosen).astype(F32).astype(B16)
    three = dot_t(one_hot, owner_v[...].astype(F32).astype(B16))
    own_p, own_m, own_n = three[0:1, :], three[1:2, :], three[2:3, :]
    off_l = jnp.where(gx == 0, 1, 0)
    off_r = jnp.where(gx == n_gx - 1, 1, 0)

    def wide(values, rows_n):
        return jnp.broadcast_to(values, (rows_n, n_cols)).astype(B16)

    all_rows = spread(lanes, 0)
    lane_block = iota((8, lanes), 1) // YCELLS
    row_p = dot_t(wide(own_p, 8), all_rows)
    row_m = dot_t(wide(own_m, 8), all_rows)
    row_n = dot_t(wide(own_n, 8), all_rows)
    lane_own = jnp.where(lane_block == 0, row_p - 1000.0 * off_l.astype(F32), row_m)
    lane_own = jnp.where(lane_block == 3, row_n - 1000.0 * off_r.astype(F32), lane_own)
    lane_own = lane_own[0:1, :].astype(jnp.int32)
    place[...] = jnp.where(iota((n_gx, lanes), 0) == lane_own, 0.125, 0.0).astype(B16)

    lane = iota((8, n_gx), 1)
    origin = jnp.where(lane // 8 == ring - 1, r, ring_at(0, 1))
    for k in range(chips - 1):
        for cross in range(2):
            origin = jnp.where(lane // 8 == 2 * k + cross, ring_at(chips - away(k, chips), cross), origin)
    lane_agg = (origin * 8 + lane % 8)[0:1, :].astype(F32)

    def picks(rows_n, base, values, off):
        column = dot_t(spread(rows_n, base), wide(values, n_gx)) - 1000.0 * off
        return (column == lane_agg).astype(F32).astype(B16)

    pick[0:YCELLS, :] = picks(YCELLS, 0, own_p, off_l.astype(F32))
    pick[YCELLS : 3 * YCELLS, :] = picks(2 * YCELLS, YCELLS, own_m, 0.0)
    pick[3 * YCELLS :, :] = picks(YCELLS, 3 * YCELLS, own_n, off_r.astype(F32))
    e_row = iota((16, n_cols), 0)
    e_col = jnp.where(e_row % 8 == 1, half_y, 0) + jnp.where(e_row >= 8, half_y - 1, 0)
    e_sel = (iota((16, n_cols), 1) == e_col).astype(F32).astype(B16)
    edge_pick[...] = (dot_t(e_sel, wide(own_m, n_gx)) == lane_agg).astype(F32).astype(B16)

    def edge_masks(rows_n):
        z = iota((rows_n, PLANES), 1)
        return z == 0, z == PLANES - 1

    def z_sum(value, low, high):
        return jnp.where(high, 0.0, pltpu.roll(value, PLANES - 1, 1)) + jnp.where(low, 0.0, pltpu.roll(value, 1, 1))

    def settle(x, mid, c, u, diagonal, mass_part, pot_part):
        step = relax_fine / (1.0 + 4.0 * diagonal)
        w_d[x - 1, mid, :] = diagonal
        w_a[x - 1, mid, :] = step
        excess_mass = mass_part - diagonal * u
        new[0, x, mid, :] = c + step * (excess_mass - diagonal * pot_part)
        new[1, x, mid, :] = u + step * (pot_part + 4.0 * excess_mass)

    def sweep(base, with_sides):
        mid, up, dn = pl.ds(base, 8), pl.ds(base + 1, 8), pl.ds(base - 1, 8)
        low, high = edge_masks(8)
        need = range(XROWS + 2) if with_sides else range(1, XROWS + 1)
        mob = {x: fld[2, x, mid, :] for x in need}
        cc = {x: fld[0, x, mid, :] for x in need}
        uu = {x: fld[1, x, mid, :] for x in need}
        face_x = {x: 0.125 * (mob[x] + mob[x + 1]) for x in need if x + 1 in mob}
        for x, face in face_x.items():
            w_x[x, mid, :] = face
        for x in range(1, XROWS + 1):
            m, c, u = mob[x], cc[x], uu[x]
            y_up = 0.125 * (m + fld[2, x, up, :])
            y_dn = 0.125 * (m + fld[2, x, dn, :])
            z_up = 0.125 * (m + jnp.where(high, 0.0, pltpu.roll(m, PLANES - 1, 1)))
            z_dn = jnp.where(low, 0.125 * m, pltpu.roll(z_up, 1, 1))
            z_w = jnp.where(high, 0.0, z_up)
            w_y[0, x - 1, mid, :] = y_dn
            w_y[1, x - 1, mid, :] = y_up
            w_z[x - 1, mid, :] = z_w
            diagonal = (y_up + y_dn) + (z_up + z_dn)
            flow = y_up * fld[1, x, up, :] + y_dn * fld[1, x, dn, :]
            flow = flow + (z_w * pltpu.roll(u, PLANES - 1, 1) + pltpu.roll(z_w * u, 1, 1))
            around = (fld[0, x, up, :] + fld[0, x, dn, :]) + z_sum(c, low, high)
            for face, other in ((x, x + 1), (x - 1, x - 1)):
                if face in face_x:
                    diagonal = diagonal + face_x[face]
                    flow = flow + face_x[face] * uu[other]
                    around = around + cc[other]
            mass_part = (src[0, x - 1, mid, :] - c) + flow
            pot_part = (src[1, x - 1, mid, :] - u + 4.0 * c) - 0.5 * around
            if x in face_x and x - 1 in face_x:
                settle(x, mid, c, u, diagonal, mass_part, pot_part)
            else:
                w_d[x - 1, mid, :] = diagonal
                new[0, x, mid, :] = mass_part
                new[1, x, mid, :] = pot_part

    def add_sides(base):
        mid = pl.ds(base, 8)
        for x, face, other in ((1, 0, 0), (XROWS, XROWS, XROWS + 1)):
            weight = 0.125 * (fld[2, x, mid, :] + fld[2, other, mid, :])
            w_x[face, mid, :] = weight
            diagonal = w_d[x - 1, mid, :] + weight
            mass_part = new[0, x, mid, :] + weight * fld[1, other, mid, :]
            pot_part = new[1, x, mid, :] - 0.5 * fld[0, other, mid, :]
            settle(x, mid, fld[0, x, mid, :], fld[1, x, mid, :], diagonal, mass_part, pot_part)

    def over_rows(count, base, stride, do):
        def body(j, carry):
            do(base + stride * j)
            return carry

        lax.fori_loop(0, count, body, 0)

    n_mid = (YCELLS - 8) // 8
    over_rows(n_mid, first + 1, 8, lambda base: sweep(base, False))

    for copy in ex:
        copy.wait_recv()

    @pl.when(gx == 0)
    def _():
        for f in range(3):
            fld[f, 0] = jnp.zeros((YCELLS + 2 * PAD, PLANES), F32)

    @pl.when(gx == n_gx - 1)
    def _():
        for f in range(3):
            fld[f, XROWS + 1] = jnp.zeros((YCELLS + 2 * PAD, PLANES), F32)

    @pl.when(gy == 0)
    def _():
        for f in range(3):
            for x in range(XROWS + 2):
                fld[f, x, 0:PAD, :] = jnp.zeros((PAD, PLANES), F32)

    @pl.when(gy == n_gy - 1)
    def _():
        for f in range(3):
            for x in range(XROWS + 2):
                fld[f, x, last : last + PAD, :] = jnp.zeros((PAD, PLANES), F32)

    over_rows(n_mid, first + 1, 8, add_sides)
    over_rows(2, 1, YCELLS, lambda base: sweep(base, True))

    @pl.when(gy == 0)
    def _():
        for f in range(2):
            for x in range(1, XROWS + 1):
                new[f, x, 0:PAD, :] = jnp.zeros((PAD, PLANES), F32)

    @pl.when(gy == n_gy - 1)
    def _():
        for f in range(2):
            for x in range(1, XROWS + 1):
                new[f, x, last : last + PAD, :] = jnp.zeros((PAD, PLANES), F32)

    def mass_excess(x, base, rows_n, cc, uu):
        mid, up, dn = pl.ds(base, rows_n), pl.ds(base + 1, rows_n), pl.ds(base - 1, rows_n)
        u, z_w = uu[x], w_z[x - 1, mid, :]
        flow = w_y[1, x - 1, mid, :] * new[1, x, up, :] + w_y[0, x - 1, mid, :] * new[1, x, dn, :]
        flow = flow + (z_w * pltpu.roll(u, PLANES - 1, 1) + pltpu.roll(z_w * u, 1, 1))
        if (x + 1) in uu:
            flow = flow + w_x[x, mid, :] * uu[x + 1]
        if (x - 1) in uu:
            flow = flow + w_x[x - 1, mid, :] * uu[x - 1]
        return (src[0, x - 1, mid, :] - cc[x]) + (flow - w_d[x - 1, mid, :] * u)

    def collect(j, carry):
        base = pl.multiple_of(PAD + 16 * j, 8)
        mid = pl.ds(base, 16)
        low, high = edge_masks(16)
        cc = {x: new[0, x, mid, :] for x in range(1, XROWS + 1)}
        uu = {x: new[1, x, mid, :] for x in range(1, XROWS + 1)}
        mass = {x: mass_excess(x, base, 16, cc, uu) for x in cc}
        up, dn = pl.ds(base + 1, 16), pl.ds(base - 1, 16)
        parts = [(w_x[0, mid, :] * uu[1], -0.5 * cc[1])]
        for a in range(1, XROWS, 2):
            conc = cc[a] + cc[a + 1]
            around = (new[0, a, up, :] + new[0, a + 1, up, :]) + (new[0, a, dn, :] + new[0, a + 1, dn, :])
            around = around + z_sum(conc, low, high)
            for other in (a - 1, a + 2):
                if other in cc:
                    around = around + cc[other]
            psrc = src[1, a - 1, mid, :] + src[1, a, mid, :]
            parts.append((mass[a] + mass[a + 1], psrc - (uu[a] + uu[a + 1]) + 3.5 * conc - 0.5 * around))
        parts.append((w_x[XROWS, mid, :] * uu[XROWS], -0.5 * cc[XROWS]))
        for block, pair in enumerate(parts):
            at = pl.ds(pl.multiple_of(block * YCELLS + 16 * j, 16), 16)
            for f in range(2):
                top, rest = halves(pair[f])
                r_hi[at, f * PLANES : (f + 1) * PLANES] = top
                r_mid[at, f * PLANES : (f + 1) * PLANES] = rest
        return carry

    lax.fori_loop(0, YCELLS // 16, collect, 0)

    fine = dot(place[...], r_hi[...]) + dot(place[...], r_mid[...])
    k = iota((2 * PLANES, PLANES), 0)
    pair_up = (iota((2 * PLANES, PLANES), 1) == (k // PLANES) * (PLANES // 2) + (k % PLANES) // 2).astype(F32).astype(B16)
    top, rest = halves(fine)
    totals[...] = (dot(top, pair_up) + dot(rest, pair_up)).reshape(ring, 8, PLANES)

    def to_ring(source, target, index):
        def one(offset, cross, slot):
            p = ring_at(offset, cross)
            remote(source(p), target.at[slot], g_send.at[index], g_recv.at[index], (q * ring + p, gy))

        def body(i, carry):
            for cross in range(2):
                one(away(i, chips), cross, 2 * i + cross)
            return carry

        lax.fori_loop(0, chips - 1, body, 0)
        one(0, 1, ring - 2)

    if ring_relay:
        for i in range(2):
            pl.semaphore_wait(relay.at[2 + i], 1)
    to_ring(lambda p: totals.at[p], rs_buf, 0)

    def all_of(ref, count, sem):
        pltpu.make_async_copy(ref.at[pl.ds(0, count)], ref.at[pl.ds(0, count)], sem).wait()

    tally = jnp.zeros((8, n_gx), F32)
    for j in range(8):
        hits = (owner_v[...] == r * 8 + j).astype(F32)
        tally = jnp.where(iota((8, n_gx), 0) == j, jnp.sum(hits, axis=0, keepdims=True), tally)
    count = dot(tally.astype(B16), jnp.ones((n_gx, PLANES), B16))
    count_v[...] = 1.0 / jnp.maximum(count, 1.0)

    hp = PLANES // 2
    z = iota((PLANES, PLANES), 1)
    in_c = z < hp
    no_up = (z % hp) == hp - 1
    no_dn = (z % hp) == 0
    gap_pot = jnp.where(in_c, -2.0 * coarse_flux, 1.0 + 2.0 * coarse_bend)
    unit = (iota((PLANES, PLANES), 0) == z).astype(F32)
    value = jnp.zeros((PLANES, PLANES), F32)
    for sweep_at in range(CSWEEP):
        gap = unit
        if sweep_at:
            around = jnp.where(no_up, 0.0, pltpu.roll(value, PLANES - 1, 1)) + jnp.where(no_dn, 0.0, pltpu.roll(value, 1, 1))
            bend = 2.0 * value - around
            cross = jnp.where(in_c, value + coarse_bend * bend, coarse_flux * bend)
            moved = pltpu.roll(cross, hp, 1)
            gap = unit - value + jnp.where(in_c, -moved, moved)
        value = value + (relax_coarse / coarse_det) * (gap + gap_pot * pltpu.roll(gap, hp, 1))
    k = iota((PLANES, 2 * PLANES), 0)
    n = iota((PLANES, 2 * PLANES), 1)
    widen = (k == (n // PLANES) * hp + (n % PLANES) // 2).astype(F32).astype(B16)
    for i, piece in enumerate(halves(value)):
        solve_v[i] = dot(piece, widen).astype(B16)

    def correct(high_mid):
        high, rest = high_mid[:, :PLANES], high_mid[:, PLANES:]
        return dot(high, solve_v[0]) + (dot(rest, solve_v[0]) + dot(high, solve_v[1]))

    all_of(rs_buf, ring - 1, g_recv.at[0])
    mine = totals[r]
    for i in range(ring - 1):
        mine = mine + rs_buf[i]
    part[...] = mine

    def swap(i, carry):
        p = (q + away(i, XGROUP)) % XGROUP
        remote(part, ar_buf.at[i], g_send.at[1], g_recv.at[1], (p * ring + r, gy))
        return carry

    for i in range(2):
        pl.semaphore_wait(relay.at[i], 1)
    lax.fori_loop(0, XGROUP - 1, swap, 0)
    sides = [
        remote(new.at[:, 1, inner], new.at[:, XROWS + 1, inner], n_send.at[0], n_recv.at[0], (left, gy)),
        remote(new.at[:, XROWS, inner], new.at[:, 0, inner], n_send.at[1], n_recv.at[1], (right, gy)),
    ]
    all_of(ar_buf, XGROUP - 1, g_recv.at[1])
    for i in range(XGROUP - 1):
        mine = mine + ar_buf[i]
    mean = mine * count_v[...]

    sol[ring - 1] = mean
    to_ring(lambda p: sol.at[ring - 1], sol, 2)

    all_of(sol, ring - 1, g_recv.at[2])
    solved = sol[...].reshape(n_gx, PLANES)
    both = jnp.concatenate(halves(solved), axis=1)

    edge = dot(edge_pick[...], both)
    edge = edge[:, :PLANES] + edge[:, PLANES:]
    y_out[...] = edge.reshape(2, 8, PLANES)
    ends = [
        remote(y_out.at[0], y_in.at[1], y_send.at[0], y_recv.at[0], (gx, below)),
        remote(y_out.at[1], y_in.at[0], y_send.at[1], y_recv.at[1], (gx, above)),
    ]
    corr[...] = correct(dot(pick[...], both).astype(B16))

    for copy in sides:
        copy.wait()

    @pl.when(gx == 0)
    def _():
        for f in range(2):
            new[f, 0, inner, :] = jnp.zeros((YCELLS, PLANES), F32)

    @pl.when(gx == n_gx - 1)
    def _():
        for f in range(2):
            new[f, XROWS + 1, inner, :] = jnp.zeros((YCELLS, PLANES), F32)

    for x in range(XROWS + 2):
        block = (x + 1) // 2
        at = pl.ds(block * YCELLS, YCELLS)
        for f in range(2):
            new[f, x, inner, :] = new[f, x, inner, :] + corr[at, f * PLANES : (f + 1) * PLANES]

    def finish(j, carry):
        base = pl.multiple_of(PAD + 8 * j, 8)
        mid = pl.ds(base, 8)
        to = pl.ds(pl.multiple_of(8 * j, 8), 8)
        low, high = edge_masks(8)
        cc = {x: new[0, x, mid, :] for x in range(XROWS + 2)}
        uu = {x: new[1, x, mid, :] for x in range(XROWS + 2)}
        for x in range(1, XROWS + 1):
            around = cc[x + 1] + cc[x - 1] + new[0, x, pl.ds(base + 1, 8), :] + new[0, x, pl.ds(base - 1, 8), :]
            around = around + z_sum(cc[x], low, high)
            excess_mass = mass_excess(x, base, 8, cc, uu)
            excess_pot = src[1, x - 1, mid, :] - uu[x] + 4.0 * cc[x] - 0.5 * around
            step, diagonal = w_a[x - 1, mid, :], w_d[x - 1, mid, :]
            conc_o[x - 1, to, :] = cc[x] + step * (excess_mass - diagonal * excess_pot)
            pot_o[x - 1, to, :] = uu[x] + step * (excess_pot + 4.0 * excess_mass)
        return carry

    lax.fori_loop(0, YCELLS // 8, finish, 0)

    for copy in ends:
        copy.wait()
    y_fine = correct(jnp.concatenate(halves(y_in[...].reshape(16, PLANES)), axis=1))
    inside = (jnp.where(gy == 0, 0.0, 1.0), jnp.where(gy == n_gy - 1, 0.0, 1.0))
    for side in range(2):
        row, out_row = (first, 0) if side == 0 else (last - 1, YCELLS - 1)
        for x in range(XROWS):
            at = side * 8 + x // 2
            add_conc = y_fine[at : at + 1, :PLANES] * inside[side]
            add_pot = y_fine[at : at + 1, PLANES:] * inside[side]
            step = w_a[x, row : row + 1, :]
            mass = w_y[side, x, row : row + 1, :] * add_pot
            pot = -0.5 * add_conc
            spot = slice(out_row, out_row + 1)
            conc_o[x, spot, :] = conc_o[x, spot, :] + step * (mass - w_d[x, row : row + 1, :] * pot)
            pot_o[x, spot, :] = pot_o[x, spot, :] + step * (pot + 4.0 * mass)

    for copy in ex:
        copy.wait_send()
    all_of(rs_buf, ring - 1, g_send.at[0])
    all_of(ar_buf, XGROUP - 1, g_send.at[1])
    all_of(rs_buf, ring - 1, g_send.at[2])


def hand_out(conc_v, pot_v, conc_o, pot_o, sem):
    copies = [
        pltpu.make_async_copy(conc_v, conc_o, sem.at[0]),
        pltpu.make_async_copy(pot_v, pot_o, sem.at[1]),
    ]
    for copy in copies:
        copy.start()
    for copy in copies:
        copy.wait()


def solution(mesh):
    n_gx, n_gy = mesh.shape["gx"], mesh.shape["gy"]
    ring = n_gx // XGROUP
    any_spec = pl.BlockSpec(memory_space=pl.ANY)
    y_pad = YCELLS + 2 * PAD
    k_all = 2 * XROWS // 2 * YCELLS

    def on_device(conc, pot, mass, psrc, mask, classes, table, owner):
        out = jax.ShapeDtypeStruct(conc.shape, F32)
        held = pl.pallas_call(
            functools.partial(kernel, n_gx, n_gy),
            out_shape=(out, out),
            in_specs=[any_spec] * 8,
            out_specs=(pl.BlockSpec(memory_space=pltpu.VMEM),) * 2,
            scratch_shapes=[
                pltpu.VMEM((3, XROWS + 2, y_pad, PLANES), F32),
                pltpu.VMEM((2, XROWS, y_pad, PLANES), F32),
                pltpu.VMEM((XROWS, YCELLS, PLANES), jnp.int32),
                pltpu.VMEM((XROWS, YCELLS, PLANES), jnp.int32),
                pltpu.VMEM((owner.shape[1], owner.shape[0]), jnp.int32),
                pltpu.SMEM((NCLASS,), F32),
                pltpu.VMEM((XROWS + 1, y_pad, PLANES), F32),
                pltpu.VMEM((2, XROWS, y_pad, PLANES), F32),
                pltpu.VMEM((XROWS, y_pad, PLANES), F32),
                pltpu.VMEM((XROWS, y_pad, PLANES), F32),
                pltpu.VMEM((XROWS, y_pad, PLANES), F32),
                pltpu.VMEM((2, XROWS + 2, y_pad, PLANES), F32),
                pltpu.VMEM((k_all, 2 * PLANES), B16),
                pltpu.VMEM((k_all, 2 * PLANES), B16),
                pltpu.VMEM((n_gx, k_all), B16),
                pltpu.VMEM((k_all, n_gx), B16),
                pltpu.VMEM((16, n_gx), B16),
                pltpu.VMEM((8, PLANES), F32),
                pltpu.VMEM((ring, 8, PLANES), F32),
                pltpu.VMEM((ring - 1, 8, PLANES), F32),
                pltpu.VMEM((8, PLANES), F32),
                pltpu.VMEM((XGROUP - 1, 8, PLANES), F32),
                pltpu.VMEM((ring, 8, PLANES), F32),
                pltpu.VMEM((2, 8, PLANES), F32),
                pltpu.VMEM((2, 8, PLANES), F32),
                pltpu.VMEM((k_all, 2 * PLANES), F32),
                pltpu.VMEM((2, PLANES, 2 * PLANES), B16),
                pltpu.SemaphoreType.DMA((8,)),
                pltpu.SemaphoreType.DMA((10,)),
                pltpu.SemaphoreType.DMA((10,)),
                pltpu.SemaphoreType.DMA((2,)),
                pltpu.SemaphoreType.DMA((2,)),
                pltpu.SemaphoreType.DMA((3,)),
                pltpu.SemaphoreType.DMA((3,)),
                pltpu.SemaphoreType.DMA((2,)),
                pltpu.SemaphoreType.DMA((2,)),
                pltpu.SemaphoreType.REGULAR((4,)),
            ],
            compiler_params=pltpu.CompilerParams(collective_id=0, has_side_effects=True, vmem_limit_bytes=24 << 20),
        )(*(pltpu.with_memory_space_constraint(a, pltpu.HBM) for a in (conc, pot, mass, psrc, mask, classes, table, owner.T)))
        return pl.pallas_call(
            hand_out,
            out_shape=(out, out),
            in_specs=[pl.BlockSpec(memory_space=pltpu.VMEM)] * 2,
            out_specs=(any_spec, any_spec),
            scratch_shapes=[pltpu.SemaphoreType.DMA((2,))],
            compiler_params=pltpu.CompilerParams(vmem_limit_bytes=1 << 20),
        )(*held)

    field = P("gx", "gy", None)
    return jax.shard_map(
        on_device,
        mesh=mesh,
        in_specs=(field,) * 6 + (P(), P(None, "gy")),
        out_specs=(field, field),
        check_vma=False,
    )
```

```python
import functools

import jax
import jax.numpy as jnp
from jax import lax
from jax.experimental import pallas as pl
from jax.experimental.pallas import tpu as pltpu
from jax.sharding import PartitionSpec as P

NCLASS = 8
CSWEEP = 3
XROWS = 4
YCELLS = 64
PLANES = 128
PAD = 8
XGROUP = 8

relax_fine = 0.6
relax_coarse = 0.6
coarse_flux = 0.0625
coarse_bend = 0.125
coarse_det = 1.15625

F32 = jnp.float32
B16 = jnp.bfloat16
MESH = pl.DeviceIdType.MESH


def iota(shape, dim):
    return lax.broadcasted_iota(jnp.int32, shape, dim)


def halves(values):
    high = values.astype(B16)
    return high, (values - high.astype(F32)).astype(B16)


def dot(a, b):
    return jnp.dot(a, b, preferred_element_type=F32)


def dot_t(a, b):
    return lax.dot_general(a, b, (((1,), (1,)), ((), ())), preferred_element_type=F32)


def kernel(
    n_gx, n_gy,
    conc_h, pot_h, mass_h, psrc_h, mask_h, class_h, table_h, owner_h,
    conc_o, pot_o,
    fld, src, mask_v, class_v, owner_v, table,
    w_x, w_y, w_z, w_d, w_a, new,
    r_hi, r_mid, place, pick, edge_pick, count_v,
    totals, rs_buf, part, ar_buf, sol, y_out, y_in, corr, solve_v,
    load_sem, ex_send, ex_recv, n_send, n_recv, g_send, g_recv, y_send, y_recv, relay,
):
    ring = n_gx // XGROUP
    gx = lax.axis_index("gx")
    gy = lax.axis_index("gy")
    r = gx % ring
    q = gx // ring
    left, right = (gx + n_gx - 1) % n_gx, (gx + 1) % n_gx
    below, above = (gy + n_gy - 1) % n_gy, (gy + 1) % n_gy
    first, last = PAD, PAD + YCELLS

    chips = ring // 2
    y_chip, core = r // 2, r % 2

    def away(i, count):
        return count // 2 + ((i + 1) // 2) * (1 - 2 * (i % 2))

    def ring_at(offset, cross):
        return ((y_chip + offset) % chips) * 2 + (1 - core if cross else core)

    barrier = pltpu.get_barrier_semaphore()

    def greet(a, b):
        pl.semaphore_signal(barrier, inc=1, device_id=(a, b), device_id_type=MESH)

    def near(count):
        return [d for d in (2, count - 2, 1, count - 1) if 0 < d < count] if count > 3 else list(range(1, count))

    group_near, ring_near = near(XGROUP), near(chips)
    for d in group_near[:2]:
        greet(((q + d) % XGROUP) * ring + r, gy)
    for d in ring_near[:2]:
        for cross in range(2):
            greet(q * ring + ring_at(d, cross), gy)
    for a in (left, right):
        for b in (below, above):
            greet(a, b)
    for d in group_near[2:]:
        greet(((q + d) % XGROUP) * ring + r, gy)
    for d in ring_near[2:]:
        for cross in range(2):
            greet(q * ring + ring_at(d, cross), gy)
    for a in (left, right):
        greet(a, gy)
    for b in (below, above):
        greet(gx, b)
    n_greet = 8 + len(group_near) + 2 * len(ring_near)

    def load(source, target, index):
        copy = pltpu.make_async_copy(source, target, load_sem.at[index])
        copy.start()
        return copy

    inner = pl.ds(PAD, YCELLS)
    l_table = load(table_h, table, 7)
    l_class = load(class_h, class_v, 1)
    l_mask = load(mask_h, mask_v, 0)
    l_conc = load(conc_h, fld.at[0, pl.ds(1, XROWS), inner, :], 2)
    l_pot = load(pot_h, fld.at[1, pl.ds(1, XROWS), inner, :], 3)
    l_mass = load(mass_h, src.at[0, :, inner, :], 4)
    l_psrc = load(psrc_h, src.at[1, :, inner, :], 5)
    l_owner = load(owner_h, owner_v, 6)

    l_table.wait()
    l_mask.wait()
    l_class.wait()
    for x in range(XROWS):
        classes = class_v[x]
        values = jnp.zeros(classes.shape, F32)
        for marker in range(NCLASS):
            values = jnp.where(classes == marker, table[marker], values)
        fld[2, x + 1, inner, :] = mask_v[x].astype(F32) * values
    for copy in (l_conc, l_pot, l_mass, l_psrc, l_owner):
        copy.wait()
    pl.semaphore_wait(barrier, n_greet)

    def remote(source, target, send, recv, device):
        copy = pltpu.make_async_remote_copy(
            src_ref=source, dst_ref=target, send_sem=send, recv_sem=recv, device_id=device, device_id_type=MESH
        )
        copy.start()
        return copy

    head, tail = pl.ds(first, 2), pl.ds(last - 2, 2)
    over, under = pl.ds(last, 2), pl.ds(first - 2, 2)
    head_1, tail_1 = pl.ds(first, 1), pl.ds(last - 1, 1)
    over_1, under_1 = pl.ds(last, 1), pl.ds(first - 1, 1)
    rows = pl.ds(1, XROWS)
    out_row, out_far, out_dev = 1 + (XROWS - 1) * core, (XROWS + 1) * (1 - core), (gx + n_gx + 2 * core - 1) % n_gx
    in_row, in_far, in_dev = XROWS - (XROWS - 1) * core, (XROWS + 1) * core, (gx + n_gx + 1 - 2 * core) % n_gx
    plan = [
        (fld.at[:, out_row, inner], fld.at[:, out_far, inner], (out_dev, gy)),
        (fld.at[:, 1, head_1], fld.at[:, XROWS + 1, over_1], (left, below)),
        (fld.at[:, 1, tail_1], fld.at[:, XROWS + 1, under_1], (left, above)),
        (fld.at[:, XROWS, head_1], fld.at[:, 0, over_1], (right, below)),
        (fld.at[:, XROWS, tail_1], fld.at[:, 0, under_1], (right, above)),
        (fld.at[:, rows, head], fld.at[:, rows, over], (gx, below)),
        (fld.at[:, rows, tail], fld.at[:, rows, under], (gx, above)),
        (src.at[:, :, head_1], src.at[:, :, over_1], (gx, below)),
        (src.at[:, :, tail_1], src.at[:, :, under_1], (gx, above)),
        (fld.at[:, in_row, inner], fld.at[:, in_far, inner], (in_dev, gy)),
    ]
    ex = [remote(a, b, ex_send.at[i], ex_recv.at[i], dev) for i, (a, b, dev) in enumerate(plan)]

    ring_relay = chips > 4
    for i, d in enumerate((2, XGROUP - 2)):
        pl.semaphore_signal(relay.at[i], inc=1, device_id=(((q + d) % XGROUP) * ring + r, gy), device_id_type=MESH)
    if ring_relay:
        for i, d in enumerate((2, chips - 2)):
            there = q * ring + ring_at(d, 0)
            pl.semaphore_signal(relay.at[2 + i], inc=1, device_id=(there, gy), device_id_type=MESH)

    half = XROWS // 2
    lanes = half * YCELLS * 2
    half_y = YCELLS // 2
    n_cols = half * half_y

    def spread(rows_n, base):
        k = iota((rows_n, n_cols), 0) + base
        block = k // YCELLS
        column = jnp.where((block == 0) | (block == 2), half_y, 0) + (k % YCELLS) // 2
        return (iota((rows_n, n_cols), 1) == column).astype(F32).astype(B16)

    which = iota((8, n_gx), 0)
    chosen = jnp.where(which == 0, left, jnp.where(which == 1, gx, right))
    one_hot = (iota((8, n_gx), 1) == chosen).astype(F32).astype(B16)
    three = dot_t(one_hot, owner_v[...].astype(F32).astype(B16))
    own_p, own_m, own_n = three[0:1, :], three[1:2, :], three[2:3, :]
    off_l = jnp.where(gx == 0, 1, 0)
    off_r = jnp.where(gx == n_gx - 1, 1, 0)

    def wide(values, rows_n):
        return jnp.broadcast_to(values, (rows_n, n_cols)).astype(B16)

    all_rows = spread(lanes, 0)
    lane_block = iota((8, lanes), 1) // YCELLS
    row_p = dot_t(wide(own_p, 8), all_rows)
    row_m = dot_t(wide(own_m, 8), all_rows)
    row_n = dot_t(wide(own_n, 8), all_rows)
    lane_own = jnp.where(lane_block == 0, row_p - 1000.0 * off_l.astype(F32), row_m)
    lane_own = jnp.where(lane_block == 3, row_n - 1000.0 * off_r.astype(F32), lane_own)
    lane_own = lane_own[0:1, :].astype(jnp.int32)
    place[...] = jnp.where(iota((n_gx, lanes), 0) == lane_own, 0.125, 0.0).astype(B16)

    lane = iota((8, n_gx), 1)
    origin = jnp.where(lane // 8 == ring - 1, r, ring_at(0, 1))
    for k in range(chips - 1):
        for cross in range(2):
            origin = jnp.where(lane // 8 == 2 * k + cross, ring_at(chips - away(k, chips), cross), origin)
    lane_agg = (origin * 8 + lane % 8)[0:1, :].astype(F32)

    def picks(rows_n, base, values, off):
        column = dot_t(spread(rows_n, base), wide(values, n_gx)) - 1000.0 * off
        return (column == lane_agg).astype(F32).astype(B16)

    pick[0:YCELLS, :] = picks(YCELLS, 0, own_p, off_l.astype(F32))
    pick[YCELLS : 3 * YCELLS, :] = picks(2 * YCELLS, YCELLS, own_m, 0.0)
    pick[3 * YCELLS :, :] = picks(YCELLS, 3 * YCELLS, own_n, off_r.astype(F32))
    e_row = iota((16, n_cols), 0)
    e_col = jnp.where(e_row % 8 == 1, half_y, 0) + jnp.where(e_row >= 8, half_y - 1, 0)
    e_sel = (iota((16, n_cols), 1) == e_col).astype(F32).astype(B16)
    edge_pick[...] = (dot_t(e_sel, wide(own_m, n_gx)) == lane_agg).astype(F32).astype(B16)

    def edge_masks(rows_n):
        z = iota((rows_n, PLANES), 1)
        return z == 0, z == PLANES - 1

    def z_sum(value, low, high):
        return jnp.where(high, 0.0, pltpu.roll(value, PLANES - 1, 1)) + jnp.where(low, 0.0, pltpu.roll(value, 1, 1))

    def settle(x, mid, c, u, diagonal, mass_part, pot_part):
        step = relax_fine / (1.0 + 4.0 * diagonal)
        w_d[x - 1, mid, :] = diagonal
        w_a[x - 1, mid, :] = step
        excess_mass = mass_part - diagonal * u
        new[0, x, mid, :] = c + step * (excess_mass - diagonal * pot_part)
        new[1, x, mid, :] = u + step * (pot_part + 4.0 * excess_mass)

    def sweep(base, with_sides):
        mid, up, dn = pl.ds(base, 8), pl.ds(base + 1, 8), pl.ds(base - 1, 8)
        low, high = edge_masks(8)
        need = range(XROWS + 2) if with_sides else range(1, XROWS + 1)
        mob = {x: fld[2, x, mid, :] for x in need}
        cc = {x: fld[0, x, mid, :] for x in need}
        uu = {x: fld[1, x, mid, :] for x in need}
        face_x = {x: 0.125 * (mob[x] + mob[x + 1]) for x in need if x + 1 in mob}
        for x, face in face_x.items():
            w_x[x, mid, :] = face
        for x in range(1, XROWS + 1):
            m, c, u = mob[x], cc[x], uu[x]
            y_up = 0.125 * (m + fld[2, x, up, :])
            y_dn = 0.125 * (m + fld[2, x, dn, :])
            z_up = 0.125 * (m + jnp.where(high, 0.0, pltpu.roll(m, PLANES - 1, 1)))
            z_dn = jnp.where(low, 0.125 * m, pltpu.roll(z_up, 1, 1))
            z_w = jnp.where(high, 0.0, z_up)
            w_y[0, x - 1, mid, :] = y_dn
            w_y[1, x - 1, mid, :] = y_up
            w_z[x - 1, mid, :] = z_w
            diagonal = (y_up + y_dn) + (z_up + z_dn)
            flow = y_up * fld[1, x, up, :] + y_dn * fld[1, x, dn, :]
            flow = flow + (z_w * pltpu.roll(u, PLANES - 1, 1) + pltpu.roll(z_w * u, 1, 1))
            around = (fld[0, x, up, :] + fld[0, x, dn, :]) + z_sum(c, low, high)
            for face, other in ((x, x + 1), (x - 1, x - 1)):
                if face in face_x:
                    diagonal = diagonal + face_x[face]
                    flow = flow + face_x[face] * uu[other]
                    around = around + cc[other]
            mass_part = (src[0, x - 1, mid, :] - c) + flow
            pot_part = (src[1, x - 1, mid, :] - u + 4.0 * c) - 0.5 * around
            if x in face_x and x - 1 in face_x:
                settle(x, mid, c, u, diagonal, mass_part, pot_part)
            else:
                w_d[x - 1, mid, :] = diagonal
                new[0, x, mid, :] = mass_part
                new[1, x, mid, :] = pot_part

    def add_sides(base):
        mid = pl.ds(base, 8)
        for x, face, other in ((1, 0, 0), (XROWS, XROWS, XROWS + 1)):
            weight = 0.125 * (fld[2, x, mid, :] + fld[2, other, mid, :])
            w_x[face, mid, :] = weight
            diagonal = w_d[x - 1, mid, :] + weight
            mass_part = new[0, x, mid, :] + weight * fld[1, other, mid, :]
            pot_part = new[1, x, mid, :] - 0.5 * fld[0, other, mid, :]
            settle(x, mid, fld[0, x, mid, :], fld[1, x, mid, :], diagonal, mass_part, pot_part)

    def over_rows(count, base, stride, do):
        def body(j, carry):
            do(base + stride * j)
            return carry

        lax.fori_loop(0, count, body, 0)

    n_mid = (YCELLS - 8) // 8
    over_rows(n_mid, first + 1, 8, lambda base: sweep(base, False))

    for copy in ex:
        copy.wait_recv()

    @pl.when(gx == 0)
    def _():
        for f in range(3):
            fld[f, 0] = jnp.zeros((YCELLS + 2 * PAD, PLANES), F32)

    @pl.when(gx == n_gx - 1)
    def _():
        for f in range(3):
            fld[f, XROWS + 1] = jnp.zeros((YCELLS + 2 * PAD, PLANES), F32)

    @pl.when(gy == 0)
    def _():
        for f in range(3):
            for x in range(XROWS + 2):
                fld[f, x, 0:PAD, :] = jnp.zeros((PAD, PLANES), F32)

    @pl.when(gy == n_gy - 1)
    def _():
        for f in range(3):
            for x in range(XROWS + 2):
                fld[f, x, last : last + PAD, :] = jnp.zeros((PAD, PLANES), F32)

    over_rows(n_mid, first + 1, 8, add_sides)
    over_rows(2, 1, YCELLS, lambda base: sweep(base, True))

    @pl.when(gy == 0)
    def _():
        for f in range(2):
            for x in range(1, XROWS + 1):
                new[f, x, 0:PAD, :] = jnp.zeros((PAD, PLANES), F32)

    @pl.when(gy == n_gy - 1)
    def _():
        for f in range(2):
            for x in range(1, XROWS + 1):
                new[f, x, last : last + PAD, :] = jnp.zeros((PAD, PLANES), F32)

    def mass_excess(x, base, rows_n, cc, uu):
        mid, up, dn = pl.ds(base, rows_n), pl.ds(base + 1, rows_n), pl.ds(base - 1, rows_n)
        u, z_w = uu[x], w_z[x - 1, mid, :]
        flow = w_y[1, x - 1, mid, :] * new[1, x, up, :] + w_y[0, x - 1, mid, :] * new[1, x, dn, :]
        flow = flow + (z_w * pltpu.roll(u, PLANES - 1, 1) + pltpu.roll(z_w * u, 1, 1))
        if (x + 1) in uu:
            flow = flow + w_x[x, mid, :] * uu[x + 1]
        if (x - 1) in uu:
            flow = flow + w_x[x - 1, mid, :] * uu[x - 1]
        return (src[0, x - 1, mid, :] - cc[x]) + (flow - w_d[x - 1, mid, :] * u)

    def collect(j, carry):
        base = pl.multiple_of(PAD + 16 * j, 8)
        mid = pl.ds(base, 16)
        low, high = edge_masks(16)
        cc = {x: new[0, x, mid, :] for x in range(1, XROWS + 1)}
        uu = {x: new[1, x, mid, :] for x in range(1, XROWS + 1)}
        mass = {x: mass_excess(x, base, 16, cc, uu) for x in cc}
        up, dn = pl.ds(base + 1, 16), pl.ds(base - 1, 16)
        parts = [(w_x[0, mid, :] * uu[1], -0.5 * cc[1])]
        for a in range(1, XROWS, 2):
            conc = cc[a] + cc[a + 1]
            around = (new[0, a, up, :] + new[0, a + 1, up, :]) + (new[0, a, dn, :] + new[0, a + 1, dn, :])
            around = around + z_sum(conc, low, high)
            for other in (a - 1, a + 2):
                if other in cc:
                    around = around + cc[other]
            psrc = src[1, a - 1, mid, :] + src[1, a, mid, :]
            parts.append((mass[a] + mass[a + 1], psrc - (uu[a] + uu[a + 1]) + 3.5 * conc - 0.5 * around))
        parts.append((w_x[XROWS, mid, :] * uu[XROWS], -0.5 * cc[XROWS]))
        for block, pair in enumerate(parts):
            at = pl.ds(pl.multiple_of(block * YCELLS + 16 * j, 16), 16)
            for f in range(2):
                top, rest = halves(pair[f])
                r_hi[at, f * PLANES : (f + 1) * PLANES] = top
                r_mid[at, f * PLANES : (f + 1) * PLANES] = rest
        return carry

    lax.fori_loop(0, YCELLS // 16, collect, 0)

    fine = dot(place[...], r_hi[...]) + dot(place[...], r_mid[...])
    k = iota((2 * PLANES, PLANES), 0)
    pair_up = (iota((2 * PLANES, PLANES), 1) == (k // PLANES) * (PLANES // 2) + (k % PLANES) // 2).astype(F32).astype(B16)
    top, rest = halves(fine)
    totals[...] = (dot(top, pair_up) + dot(rest, pair_up)).reshape(ring, 8, PLANES)

    def to_ring(source, target, index):
        def one(offset, cross, slot):
            p = ring_at(offset, cross)
            remote(source(p), target.at[slot], g_send.at[index], g_recv.at[index], (q * ring + p, gy))

        def body(i, carry):
            for cross in range(2):
                one(away(i, chips), cross, 2 * i + cross)
            return carry

        lax.fori_loop(0, chips - 1, body, 0)
        one(0, 1, ring - 2)

    if ring_relay:
        for i in range(2):
            pl.semaphore_wait(relay.at[2 + i], 1)
    to_ring(lambda p: totals.at[p], rs_buf, 0)

    def all_of(ref, count, sem):
        pltpu.make_async_copy(ref.at[pl.ds(0, count)], ref.at[pl.ds(0, count)], sem).wait()

    tally = jnp.zeros((8, n_gx), F32)
    for j in range(8):
        hits = (owner_v[...] == r * 8 + j).astype(F32)
        tally = jnp.where(iota((8, n_gx), 0) == j, jnp.sum(hits, axis=0, keepdims=True), tally)
    count = dot(tally.astype(B16), jnp.ones((n_gx, PLANES), B16))
    count_v[...] = 1.0 / jnp.maximum(count, 1.0)

    hp = PLANES // 2
    z = iota((PLANES, PLANES), 1)
    in_c = z < hp
    no_up = (z % hp) == hp - 1
    no_dn = (z % hp) == 0
    gap_pot = jnp.where(in_c, -2.0 * coarse_flux, 1.0 + 2.0 * coarse_bend)
    unit = (iota((PLANES, PLANES), 0) == z).astype(F32)
    value = jnp.zeros((PLANES, PLANES), F32)
    for sweep_at in range(CSWEEP):
        gap = unit
        if sweep_at:
            around = jnp.where(no_up, 0.0, pltpu.roll(value, PLANES - 1, 1)) + jnp.where(no_dn, 0.0, pltpu.roll(value, 1, 1))
            bend = 2.0 * value - around
            cross = jnp.where(in_c, value + coarse_bend * bend, coarse_flux * bend)
            moved = pltpu.roll(cross, hp, 1)
            gap = unit - value + jnp.where(in_c, -moved, moved)
        value = value + (relax_coarse / coarse_det) * (gap + gap_pot * pltpu.roll(gap, hp, 1))
    k = iota((PLANES, 2 * PLANES), 0)
    n = iota((PLANES, 2 * PLANES), 1)
    widen = (k == (n // PLANES) * hp + (n % PLANES) // 2).astype(F32).astype(B16)
    for i, piece in enumerate(halves(value)):
        solve_v[i] = dot(piece, widen).astype(B16)

    def correct(high_mid):
        high, rest = high_mid[:, :PLANES], high_mid[:, PLANES:]
        return dot(high, solve_v[0]) + (dot(rest, solve_v[0]) + dot(high, solve_v[1]))

    all_of(rs_buf, ring - 1, g_recv.at[0])
    mine = totals[r]
    for i in range(ring - 1):
        mine = mine + rs_buf[i]
    part[...] = mine

    def swap(i, carry):
        p = (q + away(i, XGROUP)) % XGROUP
        remote(part, ar_buf.at[i], g_send.at[1], g_recv.at[1], (p * ring + r, gy))
        return carry

    for i in range(2):
        pl.semaphore_wait(relay.at[i], 1)
    lax.fori_loop(0, XGROUP - 1, swap, 0)
    sides = [
        remote(new.at[:, 1, inner], new.at[:, XROWS + 1, inner], n_send.at[0], n_recv.at[0], (left, gy)),
        remote(new.at[:, XROWS, inner], new.at[:, 0, inner], n_send.at[1], n_recv.at[1], (right, gy)),
    ]
    all_of(ar_buf, XGROUP - 1, g_recv.at[1])
    for i in range(XGROUP - 1):
        mine = mine + ar_buf[i]
    mean = mine * count_v[...]

    sol[ring - 1] = mean
    to_ring(lambda p: sol.at[ring - 1], sol, 2)

    all_of(sol, ring - 1, g_recv.at[2])
    solved = sol[...].reshape(n_gx, PLANES)
    both = jnp.concatenate(halves(solved), axis=1)

    edge = dot(edge_pick[...], both)
    edge = edge[:, :PLANES] + edge[:, PLANES:]
    y_out[...] = edge.reshape(2, 8, PLANES)
    ends = [
        remote(y_out.at[0], y_in.at[1], y_send.at[0], y_recv.at[0], (gx, below)),
        remote(y_out.at[1], y_in.at[0], y_send.at[1], y_recv.at[1], (gx, above)),
    ]
    corr[...] = correct(dot(pick[...], both).astype(B16))

    for copy in sides:
        copy.wait()

    @pl.when(gx == 0)
    def _():
        for f in range(2):
            new[f, 0, inner, :] = jnp.zeros((YCELLS, PLANES), F32)

    @pl.when(gx == n_gx - 1)
    def _():
        for f in range(2):
            new[f, XROWS + 1, inner, :] = jnp.zeros((YCELLS, PLANES), F32)

    for x in range(XROWS + 2):
        block = (x + 1) // 2
        at = pl.ds(block * YCELLS, YCELLS)
        for f in range(2):
            new[f, x, inner, :] = new[f, x, inner, :] + corr[at, f * PLANES : (f + 1) * PLANES]

    def finish(j, carry):
        base = pl.multiple_of(PAD + 8 * j, 8)
        mid = pl.ds(base, 8)
        to = pl.ds(pl.multiple_of(8 * j, 8), 8)
        low, high = edge_masks(8)
        cc = {x: new[0, x, mid, :] for x in range(XROWS + 2)}
        uu = {x: new[1, x, mid, :] for x in range(XROWS + 2)}
        for x in range(1, XROWS + 1):
            around = cc[x + 1] + cc[x - 1] + new[0, x, pl.ds(base + 1, 8), :] + new[0, x, pl.ds(base - 1, 8), :]
            around = around + z_sum(cc[x], low, high)
            excess_mass = mass_excess(x, base, 8, cc, uu)
            excess_pot = src[1, x - 1, mid, :] - uu[x] + 4.0 * cc[x] - 0.5 * around
            step, diagonal = w_a[x - 1, mid, :], w_d[x - 1, mid, :]
            conc_o[x - 1, to, :] = cc[x] + step * (excess_mass - diagonal * excess_pot)
            pot_o[x - 1, to, :] = uu[x] + step * (excess_pot + 4.0 * excess_mass)
        return carry

    lax.fori_loop(0, YCELLS // 8, finish, 0)

    for copy in ends:
        copy.wait()
    y_fine = correct(jnp.concatenate(halves(y_in[...].reshape(16, PLANES)), axis=1))
    inside = (jnp.where(gy == 0, 0.0, 1.0), jnp.where(gy == n_gy - 1, 0.0, 1.0))
    for side in range(2):
        row, out_row = (first, 0) if side == 0 else (last - 1, YCELLS - 1)
        for x in range(XROWS):
            at = side * 8 + x // 2
            add_conc = y_fine[at : at + 1, :PLANES] * inside[side]
            add_pot = y_fine[at : at + 1, PLANES:] * inside[side]
            step = w_a[x, row : row + 1, :]
            mass = w_y[side, x, row : row + 1, :] * add_pot
            pot = -0.5 * add_conc
            spot = slice(out_row, out_row + 1)
            conc_o[x, spot, :] = conc_o[x, spot, :] + step * (mass - w_d[x, row : row + 1, :] * pot)
            pot_o[x, spot, :] = pot_o[x, spot, :] + step * (pot + 4.0 * mass)

    for copy in ex:
        copy.wait_send()
    all_of(rs_buf, ring - 1, g_send.at[0])
    all_of(ar_buf, XGROUP - 1, g_send.at[1])
    all_of(rs_buf, ring - 1, g_send.at[2])


def hand_out(conc_v, pot_v, conc_o, pot_o, sem):
    copies = []
    for x in range(XROWS):
        copies.append(pltpu.make_async_copy(conc_v.at[x], conc_o.at[x], sem.at[2 * x]))
        copies.append(pltpu.make_async_copy(pot_v.at[x], pot_o.at[x], sem.at[2 * x + 1]))
    for copy in copies:
        copy.start()
    for copy in copies:
        copy.wait()


def solution(mesh):
    n_gx, n_gy = mesh.shape["gx"], mesh.shape["gy"]
    ring = n_gx // XGROUP
    any_spec = pl.BlockSpec(memory_space=pl.ANY)
    y_pad = YCELLS + 2 * PAD
    k_all = 2 * XROWS // 2 * YCELLS

    def on_device(conc, pot, mass, psrc, mask, classes, table, owner):
        out = jax.ShapeDtypeStruct(conc.shape, F32)
        held = pl.pallas_call(
            functools.partial(kernel, n_gx, n_gy),
            out_shape=(out, out),
            in_specs=[any_spec] * 8,
            out_specs=(pl.BlockSpec(memory_space=pltpu.VMEM),) * 2,
            scratch_shapes=[
                pltpu.VMEM((3, XROWS + 2, y_pad, PLANES), F32),
                pltpu.VMEM((2, XROWS, y_pad, PLANES), F32),
                pltpu.VMEM((XROWS, YCELLS, PLANES), jnp.int32),
                pltpu.VMEM((XROWS, YCELLS, PLANES), jnp.int32),
                pltpu.VMEM((owner.shape[1], owner.shape[0]), jnp.int32),
                pltpu.SMEM((NCLASS,), F32),
                pltpu.VMEM((XROWS + 1, y_pad, PLANES), F32),
                pltpu.VMEM((2, XROWS, y_pad, PLANES), F32),
                pltpu.VMEM((XROWS, y_pad, PLANES), F32),
                pltpu.VMEM((XROWS, y_pad, PLANES), F32),
                pltpu.VMEM((XROWS, y_pad, PLANES), F32),
                pltpu.VMEM((2, XROWS + 2, y_pad, PLANES), F32),
                pltpu.VMEM((k_all, 2 * PLANES), B16),
                pltpu.VMEM((k_all, 2 * PLANES), B16),
                pltpu.VMEM((n_gx, k_all), B16),
                pltpu.VMEM((k_all, n_gx), B16),
                pltpu.VMEM((16, n_gx), B16),
                pltpu.VMEM((8, PLANES), F32),
                pltpu.VMEM((ring, 8, PLANES), F32),
                pltpu.VMEM((ring - 1, 8, PLANES), F32),
                pltpu.VMEM((8, PLANES), F32),
                pltpu.VMEM((XGROUP - 1, 8, PLANES), F32),
                pltpu.VMEM((ring, 8, PLANES), F32),
                pltpu.VMEM((2, 8, PLANES), F32),
                pltpu.VMEM((2, 8, PLANES), F32),
                pltpu.VMEM((k_all, 2 * PLANES), F32),
                pltpu.VMEM((2, PLANES, 2 * PLANES), B16),
                pltpu.SemaphoreType.DMA((8,)),
                pltpu.SemaphoreType.DMA((10,)),
                pltpu.SemaphoreType.DMA((10,)),
                pltpu.SemaphoreType.DMA((2,)),
                pltpu.SemaphoreType.DMA((2,)),
                pltpu.SemaphoreType.DMA((3,)),
                pltpu.SemaphoreType.DMA((3,)),
                pltpu.SemaphoreType.DMA((2,)),
                pltpu.SemaphoreType.DMA((2,)),
                pltpu.SemaphoreType.REGULAR((4,)),
            ],
            compiler_params=pltpu.CompilerParams(collective_id=0, has_side_effects=True, vmem_limit_bytes=24 << 20),
        )(*(pltpu.with_memory_space_constraint(a, pltpu.HBM) for a in (conc, pot, mass, psrc, mask, classes, table, owner.T)))
        return pl.pallas_call(
            hand_out,
            out_shape=(out, out),
            in_specs=[pl.BlockSpec(memory_space=pltpu.VMEM)] * 2,
            out_specs=(any_spec, any_spec),
            scratch_shapes=[pltpu.SemaphoreType.DMA((2 * XROWS,))],
            compiler_params=pltpu.CompilerParams(vmem_limit_bytes=1 << 20),
        )(*held)

    field = P("gx", "gy", None)
    return jax.shard_map(
        on_device,
        mesh=mesh,
        in_specs=(field,) * 6 + (P(), P(None, "gy")),
        out_specs=(field, field),
        check_vma=False,
    )
```
